32 devices in a mesh: dp: 16 (over z, y, core), seq: 2 (over x).
Axes of the slice: x: 2, y: 2, z: 4, core: 2. Of those that a mesh axis runs over, the one named last changes fastest.
Arguments:
- inputs: bfloat16 [16, 2, 256, 2048], P('dp', 'seq'), may hold values from -6 to 6
- cotangent: bfloat16 [16, 2, 256, 2048], P('dp', 'seq'), may hold values from -6 to 6
- adapter_ids: int32 [16], P('dp'), may hold values from 0 to 7
- block_index: int32 [16, 2], P('dp'), may hold values from 0 to 1, each once within a row
- gain_first: bfloat16 [2048], P(('dp', 'seq')), may hold values from 0.25 to 1.75
- gain_second: bfloat16 [2048], P(('dp', 'seq')), may hold values from 0.25 to 1.75
- w_query: bfloat16 [2048, 2048], P(('dp', 'seq')), may hold values from -0.125 to 0.125
- w_key: bfloat16 [2048, 256], P(('dp', 'seq')), may hold values from -0.125 to 0.125
- w_value: bfloat16 [2048, 256], P(('dp', 'seq')), may hold values from -0.125 to 0.125
- w_output: bfloat16 [2048, 2048], P(('dp', 'seq')), may hold values from -1 to 1
- w_gate_up: bfloat16 [2, 2048, 5632], P(None, None, ('dp', 'seq')), may hold values from -0.125 to 0.125
- w_down: bfloat16 [5632, 2048], P(('dp', 'seq')), may hold values from -0.15625 to 0.15625
- reduce_attention: bfloat16 [3, 128, 2048], P(None, ('dp', 'seq')), may hold values from -0.125 to 0.125
- raise_query: bfloat16 [128, 2048], P(('dp', 'seq')), may hold values from -0.75 to 0.75
- raise_keyvalue: bfloat16 [2, 128, 256], P(None, ('dp', 'seq')), may hold values from -0.75 to 0.75
- reduce_output: bfloat16 [128, 2048], P(('dp', 'seq')), may hold values from -1 to 1
- raise_output: bfloat16 [128, 2048], P(('dp', 'seq')), may hold values from -0.75 to 0.75
- reduce_gate_up: bfloat16 [2, 128, 2048], P(None, ('dp', 'seq')), may hold values from -0.125 to 0.125
- raise_gate_up: bfloat16 [2, 128, 5632], P(None, ('dp', 'seq')), may hold values from -0.75 to 0.75
- reduce_down: bfloat16 [128, 5632], P(('dp', 'seq')), may hold values from -0.15625 to 0.15625
- raise_down: bfloat16 [128, 2048], P(('dp', 'seq')), may hold values from -0.75 to 0.75
Outputs:
- output: bfloat16 [16, 2, 256, 2048], P('dp', 'seq')
- input_grad: float32 [16, 2, 256, 2048], P('dp', 'seq')
- gradient_gain_first: float32 [2048], P(('dp', 'seq'))
- gradient_gain_second: float32 [2048], P(('dp', 'seq'))
- gradient_reduce_attention: float32 [3, 128, 2048], P(None, ('dp', 'seq'))
- gradient_raise_query: float32 [128, 2048], P(('dp', 'seq'))
- gradient_raise_keyvalue: float32 [2, 128, 256], P(None, ('dp', 'seq'))
- gradient_reduce_output: float32 [128, 2048], P(('dp', 'seq'))
- gradient_raise_output: float32 [128, 2048], P(('dp', 'seq'))
- gradient_reduce_gate_up: float32 [2, 128, 2048], P(None, ('dp', 'seq'))
- gradient_raise_gate_up: float32 [2, 128, 5632], P(None, ('dp', 'seq'))
- gradient_reduce_down: float32 [128, 5632], P(('dp', 'seq'))
- gradient_raise_down: float32 [128, 2048], P(('dp', 'seq'))
The draws below stay inside these ranges and needn't reach their ends.
Inputs may be any that keep to these rules, and one draw needn't show every extreme that they name: `block_index`: each row is an ordering of 0 to 1.
All inputs are finite; a program needn't handle non-finite values.
Results may differ from the reference program's by a relative error of at most 0.019.
Values may be sent and summed in bfloat16 or wider, within the bound.
No kernel may reach another device: no remote copies, remote signals or barrier semaphores. Data moves between devices by JAX's collectives and lax.ppermute only.
A program may use at most 256 MiB of HBM per device.

```python
import jax
import jax.numpy as jnp
from jax import lax

D = 2048
HEADS = 32
KV_HEADS = 4
HEAD_DIM = 64
FF = 5632
ADAPTERS = 8
RANK = 16
BLOCK = 256
QUERY_W = 2048
KV_W = 256
BLOCKS = 2
LENGTH = 512
SEQS = 16


def touch_ends(entries, key, smallest, top_value):
    spot = [jax.random.randint(jax.random.fold_in(key, axis), (), 0, length) for axis, length in enumerate(entries.shape)]
    longest = entries.shape.index(max(entries.shape))
    next_to = spot[:longest] + [(spot[longest] + 1) % entries.shape[longest]] + spot[longest + 1:]
    return entries.at[tuple(spot)].set(smallest).at[tuple(next_to)].set(top_value)


def steps_of(key, shape, pieces, least, high):
    factor_of, own = 1.0, jax.random.fold_in(key, 6)
    for axis_at, parts in pieces:
        heights = jnp.exp(jax.random.uniform(jax.random.fold_in(own, axis_at), (parts,), jnp.float32, least / len(pieces), high / len(pieces)))
        factor_of = factor_of * jnp.repeat(heights, shape[axis_at] // parts).reshape([-1 if axis == axis_at else 1 for axis in range(len(shape))])
    return factor_of


def scatter_about(key, shape, spread, bound, pieces=(), held_as=jnp.bfloat16):
    drawn = jax.random.normal(key, shape, jnp.float32) * spread
    if len(pieces) > 0:
        drawn = steps_of(key, shape, pieces, -0.22, 0.18) * drawn
    return jnp.clip(drawn, min=-bound, max=bound).astype(held_as)


def setup_inputs(seed: int = 0) -> dict:
    key_of = jax.random.split(jax.random.key(seed), 22)
    return {
        "inputs": scatter_about(key_of[0], (SEQS, BLOCKS, BLOCK, D), 1.0, 6.0, ((0, 16), (1, 2))),
        "cotangent": scatter_about(key_of[1], (SEQS, BLOCKS, BLOCK, D), 1.0, 6.0, ((0, 16), (1, 2))),
        "adapter_ids": touch_ends(jax.random.randint(key_of[2], (SEQS,), 0, ADAPTERS), jax.random.fold_in(key_of[2], 1), 0, ADAPTERS - 1).astype(jnp.int32),
        "block_index": jax.vmap(lambda own: jax.random.permutation(own, BLOCKS))(jax.random.split(key_of[3], SEQS)).reshape((SEQS, BLOCKS)).astype(jnp.int32),
        "gain_first": jnp.clip(1.0 + 0.15 * jax.random.normal(key_of[4], (D,), jnp.float32), 0.25, 1.75).astype(jnp.bfloat16),
        "gain_second": jnp.clip(1.0 + 0.15 * jax.random.normal(key_of[5], (D,), jnp.float32), 0.25, 1.75).astype(jnp.bfloat16),
        "w_query": scatter_about(key_of[6], (D, QUERY_W), D ** -0.5, 0.125, ((0, 32),)),
        "w_key": scatter_about(key_of[7], (D, KV_W), D ** -0.5, 0.125, ((0, 32),)),
        "w_value": scatter_about(key_of[8], (D, KV_W), D ** -0.5, 0.125, ((0, 32),)),
        "w_output": scatter_about(key_of[9], (QUERY_W, D), (QUERY_W // 64) ** -0.5, 1.0, ((0, 32),)),
        "w_gate_up": scatter_about(key_of[10], (2, D, FF), D ** -0.5, 0.125, ((2, 32),)),
        "w_down": scatter_about(key_of[11], (FF, D), (FF // 4) ** -0.5, 0.15625, ((0, 32),)),
        "reduce_attention": scatter_about(key_of[12], (3, ADAPTERS * RANK, D), D ** -0.5, 0.125, ((1, 32),)),
        "raise_query": scatter_about(key_of[13], (ADAPTERS * RANK, QUERY_W), (4 * RANK) ** -0.5, 0.75, ((0, 32),)),
        "raise_keyvalue": scatter_about(key_of[14], (2, ADAPTERS * RANK, KV_W), (4 * RANK) ** -0.5, 0.75, ((1, 32),)),
        "reduce_output": scatter_about(key_of[15], (ADAPTERS * RANK, QUERY_W), (QUERY_W // 64) ** -0.5, 1.0, ((0, 32),)),
        "raise_output": scatter_about(key_of[16], (ADAPTERS * RANK, D), (4 * RANK) ** -0.5, 0.75, ((0, 32),)),
        "reduce_gate_up": scatter_about(key_of[17], (2, ADAPTERS * RANK, D), D ** -0.5, 0.125, ((1, 32),)),
        "raise_gate_up": scatter_about(key_of[18], (2, ADAPTERS * RANK, FF), (4 * RANK) ** -0.5, 0.75, ((1, 32),)),
        "reduce_down": scatter_about(key_of[19], (ADAPTERS * RANK, FF), (FF // 4) ** -0.5, 0.15625, ((0, 32),)),
        "raise_down": scatter_about(key_of[20], (ADAPTERS * RANK, D), (4 * RANK) ** -0.5, 0.75, ((0, 32),)),
    }


EPS = 1e-05
THETA = 10000.0

@jax.custom_vjp
def low(v):
    return lax.optimization_barrier(v.astype(jnp.bfloat16)).astype(jnp.float32)

@jax.custom_vjp
def low_back(v):
    return v

def low_keep(v):
    return (low(v), None)

def low_pass(kept, grad):
    return (grad,)

def back_keep(v):
    return (v, None)

def back_low(kept, grad):
    return (low(grad),)
low.defvjp(low_keep, low_pass)
low_back.defvjp(back_keep, back_low)

def matmul(left, right):
    return jnp.dot(left, right, precision=lax.Precision.HIGHEST)

def rotary_tables(positions, head_size):
    split_at = head_size // 2
    speeds = THETA ** (-jnp.arange(split_at, dtype=jnp.float32) * (2.0 / head_size))
    angles = positions.astype(jnp.float32)[..., None] * speeds
    angles = jnp.concatenate([angles, angles], -1)
    return (jnp.cos(angles), jnp.sin(angles))

def rotate(values, cosine, sine_values):
    split_at = values.shape[-1] // 2
    turned = jnp.concatenate([-values[..., split_at:], values[..., :split_at]], -1)
    return values * cosine[..., None, :] + turned * sine_values[..., None, :]

def normalize(values, gain):
    scale = lax.rsqrt(lax.optimization_barrier(jnp.mean(values * values, -1, keepdims=True)) + EPS)
    return values * scale * gain

def choose_rows(choose, table):
    shaped = table.reshape(ADAPTERS, RANK, table.shape[-1])
    return jnp.einsum('a,arw->rw', choose, shaped, precision=lax.Precision.HIGHEST)

def choose_stacked(choose, table):
    shaped = table.reshape(table.shape[0], ADAPTERS, RANK, table.shape[-1])
    return jnp.einsum('a,karw->krw', choose, shaped, precision=lax.Precision.HIGHEST)

def layer(frozen, trained, tokens, positions, choose):
    w_query, w_key, w_value, w_output, w_gate_up, w_down = frozen
    gain_first, gain_second, reduce_attention, raise_query, raise_keyvalue, reduce_output, raise_output, reduce_gate_up, raise_gate_up, reduce_down, raise_down = trained
    length_seq = tokens.shape[0]
    groups = HEADS // KV_HEADS
    normed_one = low(normalize(tokens, gain_first))
    lows_att = low(low_back(jnp.einsum('nd,krd->knr', normed_one, choose_stacked(choose, reduce_attention), precision=lax.Precision.HIGHEST)))
    raise_kv = choose_stacked(choose, raise_keyvalue)
    query = low_back(matmul(normed_one, w_query) + matmul(lows_att[0], choose_rows(choose, raise_query)))
    key = low_back(matmul(normed_one, w_key) + matmul(lows_att[1], raise_kv[0]))
    value = low(low_back(matmul(normed_one, w_value) + matmul(lows_att[2], raise_kv[1])))
    cosine, sine_values = rotary_tables(positions, HEAD_DIM)
    query_rot = low(rotate(query.reshape(length_seq, HEADS, HEAD_DIM), cosine, sine_values))
    key_rot = low(rotate(key.reshape(length_seq, KV_HEADS, HEAD_DIM), cosine, sine_values))
    query_grouped = query_rot.reshape(length_seq, KV_HEADS, groups, HEAD_DIM)
    value_heads = value.reshape(length_seq, KV_HEADS, HEAD_DIM)
    scores = low_back(jnp.einsum('qkgd,tkd->kgqt', query_grouped, key_rot, precision=lax.Precision.HIGHEST) * HEAD_DIM ** (-0.5))
    visible = positions[:, None] >= positions[None, :]
    scores = jnp.where(visible, scores, -1e+30)
    probs = low(jax.nn.softmax(scores, axis=-1))
    mixed = jnp.einsum('kgqt,tkd->qkgd', probs, value_heads, precision=lax.Precision.HIGHEST).reshape(length_seq, HEADS * HEAD_DIM)
    attended = low(low_back(mixed))
    low_out = low(low_back(matmul(attended, choose_rows(choose, reduce_output).T)))
    branch_one = low_back(matmul(attended, w_output) + matmul(low_out, choose_rows(choose, raise_output)))
    middle = tokens + branch_one
    normed_two = low(normalize(middle, gain_second))
    lows_gu = low(low_back(jnp.einsum('nd,krd->knr', normed_two, choose_stacked(choose, reduce_gate_up), precision=lax.Precision.HIGHEST)))
    raise_gu = choose_stacked(choose, raise_gate_up)
    gate = low_back(matmul(normed_two, w_gate_up[0]) + matmul(lows_gu[0], raise_gu[0]))
    up_part = low_back(matmul(normed_two, w_gate_up[1]) + matmul(lows_gu[1], raise_gu[1]))
    hidden = low(jax.nn.silu(gate) * up_part)
    low_down = low(low_back(matmul(hidden, choose_rows(choose, reduce_down).T)))
    branch_two = low_back(matmul(hidden, w_down) + matmul(low_down, choose_rows(choose, raise_down)))
    return middle + branch_two

def reference(inputs, cotangent, adapter_ids, block_index, gain_first, gain_second, w_query, w_key, w_value, w_output, w_gate_up, w_down, reduce_attention, raise_query, raise_keyvalue, reduce_output, raise_output, reduce_gate_up, raise_gate_up, reduce_down, raise_down):
    frozen = tuple((weight_array.astype(jnp.float32) for weight_array in (w_query, w_key, w_value, w_output, w_gate_up, w_down)))
    trained = tuple((weight_array.astype(jnp.float32) for weight_array in (gain_first, gain_second, reduce_attention, raise_query, raise_keyvalue, reduce_output, raise_output, reduce_gate_up, raise_gate_up, reduce_down, raise_down)))
    tokens = inputs.astype(jnp.float32).reshape(SEQS, LENGTH, D)
    grad_out = cotangent.astype(jnp.float32).reshape(SEQS, LENGTH, D)
    positions = (block_index[:, :, None] * BLOCK + jnp.arange(BLOCK, dtype=jnp.int32)[None, None, :]).reshape(SEQS, LENGTH).astype(jnp.int32)
    choose = (adapter_ids[:, None] == jnp.arange(ADAPTERS, dtype=jnp.int32)[None, :]).astype(jnp.float32)
    checked = jax.checkpoint(layer)

    def forward(trained_now, tokens_now):

        def one_sequence(carry, packed):
            seq_tokens, seq_positions, seq_choose = packed
            return (carry, checked(frozen, trained_now, seq_tokens, seq_positions, seq_choose))
        unused, results = lax.scan(one_sequence, jnp.zeros((), jnp.float32), (tokens_now, positions, choose))
        return results
    results, pullback = jax.vjp(forward, trained, tokens)
    trained_grads, input_grad = pullback(grad_out)
    output = results.astype(jnp.bfloat16).reshape(SEQS, BLOCKS, BLOCK, D)
    input_grad = input_grad.reshape(SEQS, BLOCKS, BLOCK, D)
    return (output, input_grad, trained_grads[0], trained_grads[1], trained_grads[2], trained_grads[3], trained_grads[4], trained_grads[5], trained_grads[6], trained_grads[7], trained_grads[8], trained_grads[9], trained_grads[10])
```

```python
import functools

import jax
import jax.numpy as jnp
from jax import lax
from jax.experimental import pallas as pl
from jax.experimental.pallas import tpu as pltpu
from jax.sharding import PartitionSpec as P

HEADS = 32
KV_HEADS = 4
HEAD_DIM = 64
ADAPTERS = 8
RANK = 16
TABLE = ADAPTERS * RANK

EPS = 1e-05
THETA = 10000.0

ALL = ("dp", "seq")
X, C, Y = 1, 2, 4
BF = jnp.bfloat16
F32 = jnp.float32


def dot(a, b, dims):
    return lax.dot_general(a, b, (dims, ((), ())), preferred_element_type=F32)


def nn(a, b):
    return dot(a, b, ((1,), (0,)))


def nt(a, b):
    return dot(a, b, ((1,), (1,)))


def tn(a, b):
    return dot(a, b, ((0,), (0,)))


def exchange(value, mask, n):
    return lax.ppermute(value, ALL, [(i, i ^ mask) for i in range(n)])


def rotary_tables(positions):
    half = HEAD_DIM // 2
    speeds = THETA ** (-jnp.arange(half, dtype=F32) * (2.0 / HEAD_DIM))
    angles = positions.astype(F32)[..., None] * speeds
    angles = jnp.concatenate([angles, angles], -1)
    return (jnp.cos(angles), jnp.sin(angles))


def rotate(values, cosine, sine):
    half = values.shape[-1] // 2
    turned = jnp.concatenate([-values[..., half:], values[..., :half]], -1)
    return values * cosine[:, None, :] + turned * sine[:, None, :]


def unrotate(grads, cosine, sine):
    half = grads.shape[-1] // 2
    scaled = grads * sine[:, None, :]
    turned = jnp.concatenate([scaled[..., half:], -scaled[..., :half]], -1)
    return grads * cosine[:, None, :] + turned


def norm_forward(values, gain):
    scale = lax.rsqrt(jnp.mean(values * values, -1, keepdims=True) + EPS)
    return (scale, (values * scale * gain).astype(BF))


def norm_backward(values, scale, gain, grad):
    weighted = grad * gain
    gain_grad = jnp.sum(grad * values * scale, axis=0)
    back = scale * weighted - values * (scale * scale * scale) * jnp.mean(
        weighted * values, -1, keepdims=True
    )
    return (back, gain_grad)


def outer_bits(n):
    bits, bit = [], 8
    while bit < n:
        bits.append(bit)
        bit *= 2
    return bits


class Outer:
    def __init__(self, value, n):
        self.n = n
        self.held = {0: value}
        self.offsets = sorted(range(8, n, 8), key=lambda offset: (bin(offset).count("1"), -offset))

    def step(self):
        level = bin(self.offsets[0]).count("1")
        while self.offsets and bin(self.offsets[0]).count("1") == level:
            offset = self.offsets.pop(0)
            low = offset & -offset
            self.held[offset] = exchange(self.held[offset ^ low], low, self.n)
        return bool(self.offsets)

    def pass_through(self, order, *others):
        keys = sorted(self.held)
        passed = order.point(*[self.held[k] for k in keys], *others)
        self.held = dict(zip(keys, passed))
        return passed[len(keys) :]

    def parts(self):
        return [self.held[offset] for offset in sorted(self.held)]


def sum_outer(parts, n):
    held = {8 * i: part for i, part in enumerate(parts)}
    for bit in outer_bits(n):
        for offset in sorted(held):
            if offset & bit:
                held[offset ^ bit] = held[offset ^ bit] + exchange(held.pop(offset), bit, n)
    return held[0]


def place_kernel(count, outer, width, me_ref, *refs):
    pieces, out, held, sems, last = refs[:count], *refs[count:]
    me = me_ref[0]
    z, y, c, x = me // 8, (me // 4) % 2, (me // 2) % 2, me % 2
    copies = []
    for i in range(count):
        part, dc, dy, dx = i // 8, (i // 4) % 2, (i // 2) % 2, i % 2
        for dz in range(outer):
            block = (((z ^ dz) * 2 + (y ^ dy)) * 2 + (c ^ dc)) * 2 + (x ^ dx)
            copies.append(
                pltpu.make_async_copy(
                    pieces[i].at[dz],
                    held.at[block, :, pl.ds(part * width, width)],
                    sems.at[len(copies)],
                )
            )
    for copy in copies:
        copy.start()
    for copy in copies:
        copy.wait()
    copy = pltpu.make_async_copy(held, out, last)
    copy.start()
    copy.wait()


class Rows(Outer):
    def __init__(self, shard, n):
        super().__init__(shard, n)
        self.shape = shard.shape
        self.outer = n // 8

    def start_plane(self):
        half = self.shape[1] // 2
        pieces = self.parts()
        first = jnp.stack([p[:, :half] for p in pieces])
        second = jnp.stack([p[:, half:] for p in pieces])
        self.near = [first, exchange(first, X, self.n), exchange(first, Y, self.n)]
        self.near += [second, exchange(second, X, self.n), exchange(second, Y, self.n)]

    def end_plane(self):
        first, first_x, first_y, second, second_x, second_y = self.near
        first_xy = exchange(first_x, Y, self.n)
        second_xy = exchange(second_y, X, self.n)
        self.near = [first, first_x, first_y, first_xy, second, second_x, second_y, second_xy]

    def place(self, me):
        n, outer = self.n, self.outer
        rows, width = self.shape
        far = [exchange(v, C, n) for v in self.near]
        held = self.near[:4] + far[:4] + self.near[4:] + far[4:]
        whole = pl.pallas_call(
            functools.partial(place_kernel, len(held), outer, width // 2),
            out_shape=jax.ShapeDtypeStruct((n, rows, width), held[0].dtype),
            in_specs=[pl.BlockSpec(memory_space=pltpu.SMEM)]
            + [pl.BlockSpec(memory_space=pl.ANY)] * len(held),
            out_specs=pl.BlockSpec(memory_space=pl.ANY),
            scratch_shapes=[
                pltpu.VMEM((n, rows, width), held[0].dtype),
                pltpu.SemaphoreType.DMA((len(held) * outer,)),
                pltpu.SemaphoreType.DMA(()),
            ],
            compiler_params=pltpu.CompilerParams(vmem_limit_bytes=16 << 20),
            name="place",
        )(me.reshape(1), *held)
        return whole.reshape(n * rows, width)


class Plane:
    def __init__(self, value, n):
        self.n = n
        half = value.shape[0] // 2
        first, second = value[:half], value[half:]
        self.value = value
        self.near = [exchange(first, X, n), exchange(second, Y, n)]
        self.near += [exchange(second, X, n), exchange(first, Y, n)]
        self.other = exchange(value, C, n)

    def end(self):
        first_x, second_y, second_x, first_y = self.near
        first_xy = exchange(first_x, Y, self.n)
        second_xy = exchange(second_y, X, self.n)
        near = [first_x, second_x, first_y, second_y]
        self.far = [exchange(v, C, self.n) for v in near]
        self.near = near + [first_xy, second_xy]

    def all(self):
        far = self.far + [exchange(v, C, self.n) for v in self.near[4:]]
        return jnp.concatenate([self.value] + self.near + [self.other] + far, 0)


class Order:
    def __init__(self):
        self.token = jnp.zeros((), F32)

    def point(self, *values):
        *values, self.token = lax.optimization_barrier((*values, self.token))
        return values[0] if len(values) == 1 else values


def half_of(block, part):
    half = block.shape[0] // 2
    return block[part * half : (part + 1) * half].astype(F32)


def sum_plane(mine, other, n):
    recv = exchange(other, C, n)
    held = lambda block, part: half_of(mine[block], part) + half_of(recv[block], part)
    x_first = exchange(held(1, 0).astype(BF), X, n)
    y_second = exchange(held(2, 1).astype(BF), Y, n)
    xy_first = exchange(held(3, 0).astype(BF), X, n)
    xy_second = exchange(held(3, 1).astype(BF), Y, n)
    last_first = exchange((held(2, 0) + xy_first.astype(F32)).astype(BF), Y, n)
    last_second = exchange((held(1, 1) + xy_second.astype(F32)).astype(BF), X, n)
    return jnp.concatenate(
        [
            held(0, 0) + x_first.astype(F32) + last_first.astype(F32),
            held(0, 1) + y_second.astype(F32) + last_second.astype(F32),
        ],
        0,
    )


def load_feed(pieces, shard, slots, sems):
    copies = []
    for i, piece in enumerate(pieces):
        for kind, slot in enumerate(slots):
            copies.append(
                pltpu.make_async_copy(
                    piece.at[pl.ds(kind * shard, shard)],
                    slot.at[pl.ds(i * shard, shard)],
                    sems.at[len(copies)],
                )
            )
    return copies


def lift_of(adapter, place):
    row = lax.broadcasted_iota(jnp.int32, (TABLE, TABLE), 0) - place * RANK
    col = lax.broadcasted_iota(jnp.int32, (TABLE, TABLE), 1) - adapter * RANK
    return ((row == col) & (row >= 0) & (row < RANK)).astype(F32).astype(BF)


def hidden_kernel(count, shard, width, ids_ref, normed_ref, cot_ref, *refs):
    pieces = refs[:count]
    hidden_ref, gate_ref, up_ref, grads_ref, w_gate, w_up, w_down, sems = refs[count:]
    group = pl.program_id(0)
    copies = load_feed(pieces, shard, (w_gate, w_up, w_down), sems)

    @pl.when(group == 0)
    def _():
        for copy in copies:
            copy.start()
        grads_ref[...] = jnp.zeros_like(grads_ref)
        for copy in copies:
            copy.wait()

    adapter = ids_ref[group]
    lows = normed_ref[:, width:]
    low_gate = nn(lows, lift_of(adapter, 0)).astype(BF)
    low_up = nn(lows, lift_of(adapter, 1)).astype(BF)
    low_cot = nn(lows, lift_of(adapter, 2)).astype(BF)
    normed = normed_ref[:, :width]
    gate = nt(normed, w_gate[:, :width]) + nt(low_gate, w_gate[:, width:])
    up = nt(normed, w_up[:, :width]) + nt(low_up, w_up[:, width:])
    grad = nt(cot_ref[...], w_down[:, :width]) + nt(low_cot, w_down[:, width:])
    sigmoid = 1.0 / (1.0 + jnp.exp(-gate))
    silu = gate * sigmoid
    hidden = (silu * up).astype(BF)
    grad_gate = (grad * up * sigmoid * (1.0 + gate * (1.0 - sigmoid))).astype(BF)
    grad_up = (grad * silu).astype(BF)
    hidden_ref[...] = hidden
    gate_ref[...] = grad_gate
    up_ref[...] = grad_up
    grads_ref[0] += tn(low_gate, grad_gate)
    grads_ref[1] += tn(low_up, grad_up)
    grads_ref[2] += tn(low_cot, hidden)


def hidden_stage(ids, normed, cot, pieces, shard):
    tokens, wide = normed.shape
    width = wide - TABLE
    count = len(pieces)
    cols = count * shard
    block = tokens // 4
    out = jax.ShapeDtypeStruct((tokens, cols), BF)
    tile = pl.BlockSpec((block, cols), lambda i: (i, 0))
    return pl.pallas_call(
        functools.partial(hidden_kernel, count, shard, width),
        grid=(4,),
        out_shape=(out, out, out, jax.ShapeDtypeStruct((3, TABLE, cols), F32)),
        in_specs=[
            pl.BlockSpec(memory_space=pltpu.SMEM),
            pl.BlockSpec((block, wide), lambda i: (i, 0)),
            pl.BlockSpec((block, width), lambda i: (i, 0)),
        ]
        + [pl.BlockSpec(memory_space=pl.ANY)] * count,
        out_specs=(tile, tile, tile, pl.BlockSpec((3, TABLE, cols), lambda i: (0, 0, 0))),
        scratch_shapes=[pltpu.VMEM((cols, wide), BF)] * 3
        + [pltpu.SemaphoreType.DMA((3 * count,))],
        compiler_params=pltpu.CompilerParams(vmem_limit_bytes=40 << 20),
        cost_estimate=pl.CostEstimate(
            flops=6 * tokens * wide * cols,
            bytes_accessed=2 * (tokens * (wide + width + 3 * cols) + 3 * cols * wide),
            transcendentals=tokens * cols,
        ),
        name="hidden",
    )(ids, normed, cot, *pieces)


def grad_kernel(count, parts, shard, width, *refs):
    acts, refs = refs[: 2 * parts], refs[2 * parts :]
    pieces, (out_ref, w_gate, w_up, sems) = refs[:count], refs[count:]
    copies = load_feed(pieces, shard, (w_gate, w_up), sems)

    @pl.when(pl.program_id(0) == 0)
    def _():
        for copy in copies:
            copy.start()
        for copy in copies:
            copy.wait()

    cols = acts[0].shape[1]
    main, low_gate, low_up = 0.0, 0.0, 0.0
    for i in range(parts):
        own = pl.ds(i * cols, cols)
        gate, up = acts[i][...], acts[parts + i][...]
        main += nn(gate, w_gate[own, :width]) + nn(up, w_up[own, :width])
        low_gate += nn(gate, w_gate[own, width:])
        low_up += nn(up, w_up[own, width:])
    out_ref[:, :width] = main.astype(BF)
    out_ref[:, width : width + TABLE] = low_gate.astype(BF)
    out_ref[:, width + TABLE :] = low_up.astype(BF)


def grad_stage(gates, ups, pieces, shard, first, groups):
    tokens, cols = gates[0].shape
    wide = pieces[0].shape[1]
    width = wide - TABLE
    count, parts = len(pieces), len(gates)
    block = tokens // 4
    tile = pl.BlockSpec((block, cols), lambda i: (i + first, 0))
    return pl.pallas_call(
        functools.partial(grad_kernel, count, parts, shard, width),
        grid=(groups,),
        out_shape=jax.ShapeDtypeStruct((groups * block, wide + TABLE), BF),
        in_specs=[tile] * (2 * parts) + [pl.BlockSpec(memory_space=pl.ANY)] * count,
        out_specs=pl.BlockSpec((block, wide + TABLE), lambda i: (i, 0)),
        scratch_shapes=[pltpu.VMEM((count * shard, wide), BF)] * 2
        + [pltpu.SemaphoreType.DMA((2 * count,))],
        compiler_params=pltpu.CompilerParams(vmem_limit_bytes=40 << 20),
        cost_estimate=pl.CostEstimate(
            flops=4 * groups * block * wide * cols * parts,
            bytes_accessed=2 * (groups * block * (2 * parts * cols + wide) + 2 * count * shard * wide),
            transcendentals=0,
        ),
        name="grad",
    )(*gates, *ups, *pieces)


def down_kernel(count, parts, shard, *refs):
    acts, refs = refs[:parts], refs[parts:]
    pieces, (out_ref, w_down, sems) = refs[:count], refs[count:]
    copies = [
        pltpu.make_async_copy(
            piece.at[pl.ds(2 * shard, shard)], w_down.at[pl.ds(i * shard, shard)], sems.at[i]
        )
        for i, piece in enumerate(pieces)
    ]

    @pl.when(pl.program_id(0) == 0)
    def _():
        for copy in copies:
            copy.start()
        for copy in copies:
            copy.wait()

    cols = acts[0].shape[1]
    total = 0.0
    for i in range(parts):
        total += nn(acts[i][...], w_down[pl.ds(i * cols, cols), :])
    out_ref[...] = total.astype(BF)


def down_stage(hiddens, pieces, shard):
    tokens, cols = hiddens[0].shape
    wide = pieces[0].shape[1]
    count, parts = len(pieces), len(hiddens)
    block = tokens // 4
    return pl.pallas_call(
        functools.partial(down_kernel, count, parts, shard),
        grid=(4,),
        out_shape=jax.ShapeDtypeStruct((tokens, wide), BF),
        in_specs=[pl.BlockSpec((block, cols), lambda i: (i, 0))] * parts
        + [pl.BlockSpec(memory_space=pl.ANY)] * count,
        out_specs=pl.BlockSpec((block, wide), lambda i: (i, 0)),
        scratch_shapes=[
            pltpu.VMEM((count * shard, wide), BF),
            pltpu.SemaphoreType.DMA((count,)),
        ],
        compiler_params=pltpu.CompilerParams(vmem_limit_bytes=40 << 20),
        cost_estimate=pl.CostEstimate(
            flops=2 * tokens * wide * cols * parts,
            bytes_accessed=2 * (tokens * (parts * cols + wide) + count * shard * wide),
            transcendentals=0,
        ),
        name="down",
    )(*hiddens, *pieces)


def per_device(
    n,
    inputs,
    cotangent,
    adapter_ids,
    block_index,
    gain_first,
    gain_second,
    w_query,
    w_key,
    w_value,
    w_output,
    w_gate_up,
    w_down,
    reduce_attention,
    raise_query,
    raise_keyvalue,
    reduce_output,
    raise_output,
    reduce_gate_up,
    raise_gate_up,
    reduce_down,
    raise_down,
):
    width = inputs.shape[-1]
    rows = inputs.shape[-2]
    shard = w_down.shape[0]
    own_rows = raise_down.shape[0]
    gains = gain_first.shape[0]
    kv_width = KV_HEADS * HEAD_DIM
    groups = HEADS // KV_HEADS
    attn_scale = HEAD_DIM ** (-0.5)
    side = lax.axis_index("seq")
    me = lax.axis_index(ALL).astype(jnp.int32)
    tokens = inputs.reshape(rows, width).astype(F32)
    grad_out = cotangent.reshape(rows, width)

    order = Order()
    qkv_rows = Rows(jnp.concatenate([w_query, w_key, w_value], 1), n)
    qkv_rows.step()
    cot_plane = Plane(grad_out, n)

    table_width = 10 * width
    chunk = table_width // n
    table = jnp.concatenate(
        [reduce_attention[0], reduce_attention[1], reduce_attention[2], raise_query]
        + [reduce_output, raise_output, reduce_gate_up[0], reduce_gate_up[1], raise_down]
        + [raise_keyvalue[0], raise_keyvalue[1]],
        1,
    )
    table = jnp.pad(table, ((0, 0), (0, table_width - table.shape[1])))
    table = jnp.moveaxis(table.reshape(own_rows, n, chunk), 1, 0)
    hidden_table = jnp.stack([raise_gate_up[0], raise_gate_up[1], reduce_down])
    hidden_table = hidden_table.reshape(3, own_rows, n, shard).transpose(2, 1, 0, 3)
    hidden_table = hidden_table.reshape(n, own_rows, 3 * shard)
    small = jnp.concatenate([gain_first, gain_second, adapter_ids.astype(BF)])
    used = chunk + 3 * shard
    sent = -(-(used + small.shape[0]) // 128) * 128
    small = jnp.pad(small, (0, sent - used - small.shape[0]))
    small = jnp.broadcast_to(small, (n, own_rows, small.shape[0]))
    came = lax.all_to_all(jnp.concatenate([table, hidden_table, small], -1), ALL, 0, 0, tiled=True)
    gain_one = came[:, 0, used : used + gains].reshape(width).astype(F32)
    gain_two = came[:, 0, used + gains : used + 2 * gains].reshape(width).astype(F32)
    ids = came[:, 0, used + 2 * gains].astype(jnp.int32)
    columns = came[:, :, :chunk].reshape(ADAPTERS, RANK, chunk)
    hidden_cols = came[:, :, chunk:used].reshape(TABLE, 3, shard)
    own = lax.all_to_all(jnp.take(columns, ids, axis=0), ALL, 0, 0, tiled=True)
    own = jnp.moveaxis(own, 0, 1).reshape(RANK, table_width)
    (a_query, a_key, a_value, b_query, a_out, b_out, a_gate, a_up, b_down) = [
        own[:, i * width : (i + 1) * width] for i in range(9)
    ]
    b_key = own[:, 9 * width : 9 * width + kv_width]
    b_value = own[:, 9 * width + kv_width : 9 * width + 2 * kv_width]
    lift = (
        jnp.arange(TABLE, dtype=jnp.int32)[None, :]
        == adapter_ids[0] * RANK + jnp.arange(RANK, dtype=jnp.int32)[:, None]
    ).astype(BF)

    (w_output,) = qkv_rows.pass_through(order, w_output)
    more = True
    while more:
        more = qkv_rows.step()
    out_rows = Rows(w_output, n)
    out_rows.step()
    feed = jnp.stack([w_gate_up[0].T, w_gate_up[1].T, w_down])
    feed = jnp.concatenate([feed, hidden_cols.transpose(1, 2, 0)], 2)
    padded = -(-shard // 16) * 16
    feed = jnp.pad(feed, ((0, 0), (0, padded - shard), (0, 0))).reshape(3 * padded, -1)
    (feed, *cot_plane.near) = qkv_rows.pass_through(order, feed, *cot_plane.near)
    qkv_rows.start_plane()
    (feed,) = out_rows.pass_through(order, feed)
    more = True
    while more:
        more = out_rows.step()
    cot_plane.end()
    feed_rows = Outer(feed, n)
    feed_rows.step()

    positions_of = lambda block: block * rows + jnp.arange(rows, dtype=jnp.int32)
    own_block = lax.dynamic_index_in_dim(block_index[0], side, 0, keepdims=False)
    other_block = lax.dynamic_index_in_dim(block_index[0], 1 - side, 0, keepdims=False)
    query_pos = positions_of(own_block)
    key_pos = jnp.concatenate([query_pos, positions_of(other_block)])
    visible = query_pos[:, None] >= key_pos[None, :]
    cosine, sine = rotary_tables(query_pos)

    scale_one, normed_one = norm_forward(tokens, gain_one)
    low_att = nt(normed_one, jnp.concatenate([a_query, a_key, a_value], 0)).astype(BF)
    low_query, low_key, low_value = [low_att[:, i * RANK : (i + 1) * RANK] for i in range(3)]
    qkv_rows.near = list(order.point(*qkv_rows.near))
    qkv_rows.end_plane()
    qkv_rows.near = list(order.point(*qkv_rows.near))
    w_qkv = qkv_rows.place(me)
    out_rows.pass_through(order)
    out_rows.start_plane()
    qkv = nn(normed_one, w_qkv)
    query = qkv[:, :width] + nn(low_query, b_query)
    key = qkv[:, width : width + kv_width] + nn(low_key, b_key)
    value = (qkv[:, width + kv_width :] + nn(low_value, b_value)).astype(BF)
    query_rot = rotate(query.reshape(rows, HEADS, HEAD_DIM), cosine, sine).astype(BF)
    key_rot = rotate(key.reshape(rows, KV_HEADS, HEAD_DIM), cosine, sine).astype(BF)
    key_value = jnp.concatenate([key_rot.reshape(rows, kv_width), value], 1)
    key_value = jnp.concatenate([key_value, exchange(key_value, X, n)], 0)
    key_value, query_rot, *out_rows.near = order.point(key_value, query_rot, *out_rows.near)
    out_rows.end_plane()
    key_heads = key_value[:, :kv_width].reshape(2 * rows, KV_HEADS, HEAD_DIM)
    value_heads = key_value[:, kv_width:].reshape(2 * rows, KV_HEADS, HEAD_DIM)
    query_heads = query_rot.reshape(rows, KV_HEADS, groups, HEAD_DIM)
    scores = jnp.einsum("mkgd,tkd->kgmt", query_heads, key_heads, preferred_element_type=F32)
    scores = jnp.where(visible, scores * attn_scale, -1e30)
    peak = jnp.max(scores, -1, keepdims=True)
    weights = jnp.exp(scores - peak)
    probs = (weights / jnp.sum(weights, -1, keepdims=True)).astype(BF)
    mixed = jnp.einsum("kgmt,tkd->mkgd", probs, value_heads, preferred_element_type=F32)
    attended = mixed.reshape(rows, width).astype(BF)
    low_out = nt(attended, a_out).astype(BF)
    attended, *out_rows.near = order.point(attended, *out_rows.near)
    w_out = out_rows.place(me)
    middle = tokens + nn(attended, w_out) + nn(low_out, b_out)

    scale_two, normed_two = norm_forward(middle, gain_two)
    low_gate = nt(normed_two, a_gate).astype(BF)
    low_up = nt(normed_two, a_up).astype(BF)
    grad_low_down = nt(grad_out, b_down).astype(BF)
    spare = jnp.zeros((rows, TABLE - 3 * RANK), BF)
    normed_plane = Plane(
        jnp.concatenate([normed_two, low_gate, low_up, grad_low_down, spare], 1), n
    )
    plane_ids = ids[me ^ jnp.array([0, Y, C, C | Y], jnp.int32)]
    cot_all = cot_plane.all()
    *normed_plane.near, cot_all = order.point(*normed_plane.near, cot_all)
    normed_plane.end()
    more = True
    while more:
        feed_rows.pass_through(order)
        more = feed_rows.step()
    normed_all = normed_plane.all()
    feeds = feed_rows.parts()
    half = len(feeds) // 2
    stages = [
        hidden_stage(plane_ids, normed_all, cot_all, part, padded)
        for part in (feeds[:half], feeds[half:])
    ]
    hiddens, gates, ups = [[stage[i] for stage in stages] for i in range(3)]
    wide = width + TABLE
    block_shape = (4, rows, wide + TABLE)
    grad_far = grad_stage(gates, ups, feeds, padded, 2, 2).reshape(block_shape)
    grad_near = grad_stage(gates, ups, feeds, padded, 0, 2).reshape(block_shape)
    grad_normed = sum_plane(grad_near, grad_far, n)
    branch_two = down_stage(hiddens, feeds, padded).reshape(2, 4, rows, wide)
    branch_two = sum_plane(branch_two[0], branch_two[1], n)
    hidden_grads = jnp.concatenate([stage[3] for stage in stages], 2)
    hidden_grads = sum_outer(
        [hidden_grads[:, :, i * padded : i * padded + shard] for i in range(n // 8)], n
    )
    low_down = nn(branch_two[:, width:].astype(BF), lift.T).astype(BF)
    output = (middle + branch_two[:, :width] + nn(low_down, b_down)).astype(BF)

    grad_low_gate = nn(grad_normed[:, width:wide].astype(BF), lift.T).astype(BF)
    grad_low_up = nn(grad_normed[:, wide:].astype(BF), lift.T).astype(BF)
    grad_normed_two = (
        grad_normed[:, :width] + nn(grad_low_gate, a_gate) + nn(grad_low_up, a_up)
    )
    back_two, gain_grad_two = norm_backward(middle, scale_two, gain_two, grad_normed_two)
    grad_middle = grad_out.astype(F32) + back_two
    grad_one = grad_middle.astype(BF)
    grad_low_out = nt(grad_one, b_out).astype(BF)
    grad_attended = (
        nt(grad_one, w_out)
        + nn(grad_low_out, a_out)
    ).astype(BF)
    grad_heads = grad_attended.reshape(rows, KV_HEADS, groups, HEAD_DIM)
    grad_probs = jnp.einsum("mkgd,tkd->kgmt", grad_heads, value_heads, preferred_element_type=F32)
    probs_f = probs.astype(F32)
    inner = jnp.sum(probs_f * grad_probs, -1, keepdims=True)
    grad_scores = (probs_f * (grad_probs - inner)).astype(BF)
    grad_query = jnp.einsum("kgmt,tkd->mkgd", grad_scores, key_heads, preferred_element_type=F32)
    grad_key = jnp.einsum("kgmt,mkgd->tkd", grad_scores, query_heads, preferred_element_type=F32)
    grad_value = jnp.einsum("kgmt,mkgd->tkd", probs, grad_heads, preferred_element_type=F32)
    grad_query = grad_query.reshape(rows, HEADS, HEAD_DIM) * attn_scale
    grad_kv = jnp.concatenate(
        [
            (grad_key * attn_scale).reshape(2 * rows, kv_width),
            grad_value.reshape(2 * rows, kv_width),
        ],
        1,
    )
    grad_kv = grad_kv[:rows] + exchange(grad_kv[rows:].astype(BF), X, n).astype(F32)
    grad_query = unrotate(grad_query, cosine, sine).reshape(rows, width).astype(BF)
    grad_key = unrotate(grad_kv[:, :kv_width].reshape(rows, KV_HEADS, HEAD_DIM), cosine, sine)
    grad_key = grad_key.reshape(rows, kv_width).astype(BF)
    grad_value = grad_kv[:, kv_width:].astype(BF)
    grad_low_query = nt(grad_query, b_query).astype(BF)
    grad_low_key = nt(grad_key, b_key).astype(BF)
    grad_low_value = nt(grad_value, b_value).astype(BF)
    grad_qkv = jnp.concatenate([grad_query, grad_key, grad_value], 1)
    grad_low_att = jnp.concatenate([grad_low_query, grad_low_key, grad_low_value], 1)
    grad_normed_one = nt(grad_qkv, w_qkv) + nn(
        grad_low_att, jnp.concatenate([a_query, a_key, a_value], 0)
    )
    back_one, gain_grad_one = norm_backward(tokens, scale_one, gain_one, grad_normed_one)
    input_grad = (grad_middle + back_one).reshape(inputs.shape)

    reduce_att = tn(grad_low_att, normed_one)
    per_seq = jnp.concatenate(
        [
            reduce_att[:RANK],
            reduce_att[RANK : 2 * RANK],
            reduce_att[2 * RANK :],
            tn(low_query, grad_query),
            tn(grad_low_out, attended),
            tn(low_out, grad_one),
            tn(grad_low_gate, normed_two),
            tn(grad_low_up, normed_two),
            tn(low_down, grad_out),
            tn(low_key, grad_key),
            tn(low_value, grad_value),
            jnp.zeros((RANK, table_width - 9 * width - 2 * kv_width), F32),
        ],
        1,
    )
    per_seq = jnp.moveaxis(per_seq.reshape(RANK, n, chunk), 1, 0)
    per_seq = lax.all_to_all(per_seq, ALL, 0, 0, tiled=True)
    onehot = (ids[:, None] == jnp.arange(ADAPTERS, dtype=jnp.int32)[None, :]).astype(F32)
    summed = jnp.einsum("na,nrc->arc", onehot, per_seq, precision=lax.Precision.HIGHEST)
    hidden_grads = hidden_grads.transpose(1, 0, 2).reshape(n, own_rows, 3 * shard)
    gain_grads = jnp.concatenate(
        [gain_grad_one.reshape(n, gains), gain_grad_two.reshape(n, gains)], 1
    )
    gain_grads = jnp.broadcast_to(gain_grads[:, None], (n, own_rows, 2 * gains))
    final = jnp.concatenate([summed.reshape(n, own_rows, chunk), hidden_grads, gain_grads], -1)
    final = lax.all_to_all(final, ALL, 0, 0, tiled=True)
    gain_grads = jnp.sum(final[:, 0, used:], 0)
    tables = jnp.moveaxis(final[:, :, :chunk], 0, 1).reshape(own_rows, table_width)
    parts = [tables[:, i * width : (i + 1) * width] for i in range(9)]
    kv = tables[:, 9 * width : 9 * width + 2 * kv_width]
    hidden_grads = final[:, :, chunk:used].reshape(n, own_rows, 3, shard).transpose(2, 1, 0, 3)
    hidden_grads = hidden_grads.reshape(3, own_rows, n * shard)
    return (
        output.reshape(inputs.shape),
        input_grad,
        gain_grads[:gains],
        gain_grads[gains:],
        jnp.stack(parts[:3]),
        parts[3],
        jnp.stack([kv[:, :kv_width], kv[:, kv_width:]]),
        parts[4],
        parts[5],
        jnp.stack(parts[6:8]),
        hidden_grads[:2],
        hidden_grads[2],
        parts[8],
    )


def solution(mesh):
    n = mesh.shape["dp"] * mesh.shape["seq"]
    rows = P(("dp", "seq"), None)
    stacked = P(None, ("dp", "seq"), None)
    vector = P(("dp", "seq"))
    blocks = P("dp", "seq", None, None)
    return jax.shard_map(
        functools.partial(per_device, n),
        mesh=mesh,
        in_specs=(
            blocks,
            blocks,
            P("dp"),
            P("dp", None),
            vector,
            vector,
            rows,
            rows,
            rows,
            rows,
            P(None, None, ("dp", "seq")),
            rows,
            stacked,
            rows,
            stacked,
            rows,
            rows,
            stacked,
            stacked,
            rows,
            rows,
        ),
        out_specs=(
            blocks,
            blocks,
            vector,
            vector,
            stacked,
            rows,
            stacked,
            rows,
            rows,
            stacked,
            stacked,
            rows,
            rows,
        ),
        check_vma=False,
    )
```

```python
import functools

import jax
import jax.numpy as jnp
from jax import lax
from jax.experimental import pallas as pl
from jax.experimental.pallas import tpu as pltpu
from jax.sharding import Mesh
from jax.sharding import PartitionSpec as P

HEADS = 32
KV_HEADS = 4
HEAD_DIM = 64
ADAPTERS = 8
RANK = 16
TABLE = ADAPTERS * RANK

EPS = 1e-05
THETA = 10000.0

ALL = ("outer", "pair", "seq")
X, C, Y = 1, 2, 4
BF = jnp.bfloat16
F32 = jnp.float32
HBM = lambda value: pltpu.with_memory_space_constraint(value, pltpu.HBM)
LIGHT = pl.CostEstimate(flops=1 << 20, bytes_accessed=1 << 16, transcendentals=0)


def dot(a, b, dims):
    return lax.dot_general(a, b, (dims, ((), ())), preferred_element_type=F32)


def nn(a, b):
    return dot(a, b, ((1,), (0,)))


def nt(a, b):
    return dot(a, b, ((1,), (1,)))


def tn(a, b):
    return dot(a, b, ((0,), (0,)))


def exchange(value, mask, n):
    return lax.ppermute(value, ALL, [(i, i ^ mask) for i in range(n)])


def rotary_tables(positions):
    half = HEAD_DIM // 2
    speeds = THETA ** (-jnp.arange(half, dtype=F32) * (2.0 / HEAD_DIM))
    angles = positions.astype(F32)[:, None] * speeds
    cosine, sine = jnp.cos(angles), jnp.sin(angles)
    return jnp.tile(cosine, (1, 4)), jnp.tile(jnp.concatenate([-sine, sine], 1), (1, 2))


def outer_bits(n):
    bits, bit = [], 8
    while bit < n:
        bits.append(bit)
        bit *= 2
    return bits


class Outer:
    def __init__(self, value, n):
        self.n = n
        self.held = {0: value}
        self.offsets = sorted(range(8, n, 8), key=lambda offset: (bin(offset).count("1"), -offset))

    def step(self):
        if not self.offsets:
            return False
        level = bin(self.offsets[0]).count("1")
        while self.offsets and bin(self.offsets[0]).count("1") == level:
            offset = self.offsets.pop(0)
            low = offset & -offset
            self.held[offset] = exchange(self.held[offset ^ low], low, self.n)
        return bool(self.offsets)

    def step_all(self):
        while self.step():
            pass

    def pass_through(self, order, *others):
        keys = sorted(self.held)
        passed = order.point(*[self.held[k] for k in keys], *others)
        self.held = dict(zip(keys, passed))
        return passed[len(keys) :]

    def parts(self):
        return [self.held[offset] for offset in sorted(self.held)]


def place_copies(me, pieces, held, sems):
    z, y, c, x = me // 8, (me // 4) % 2, (me // 2) % 2, me % 2
    copies = []
    for i, piece in enumerate(pieces):
        dc, kind = i // 5, i % 5
        dy, dx = ((0, 0), (0, 1), (1, 0), (1, 1), (1, 1))[kind]
        first = piece.shape[0] if kind == 4 else 0
        for j in range(piece.shape[0]):
            dz = first + j
            block = (((z ^ dz) * 2 + (y ^ dy)) * 2 + (c ^ dc)) * 2 + (x ^ dx)
            copies.append(
                pltpu.make_async_copy(piece.at[j], held.at[block], sems.at[len(copies)])
            )
    return copies


def normed_of(values, gain):
    scale = lax.rsqrt(jnp.mean(values * values, -1, keepdims=True) + EPS)
    return (values * scale * gain).astype(BF)


class Outer:
    def __init__(self, value, n):
        self.n = n
        self.held = {0: value}
        self.offsets = sorted(range(8, n, 8), key=lambda offset: (bin(offset).count("1"), -offset))

    def step(self):
        if not self.offsets:
            return False
        level = bin(self.offsets[0]).count("1")
        while self.offsets and bin(self.offsets[0]).count("1") == level:
            offset = self.offsets.pop(0)
            low = offset & -offset
            self.held[offset] = exchange(self.held[offset ^ low], low, self.n)
        return bool(self.offsets)

    def step_all(self):
        while self.step():
            pass

    def pass_through(self, order, *others):
        keys = sorted(self.held)
        passed = order.point(*[self.held[k] for k in keys], *others)
        self.held = dict(zip(keys, passed))
        return passed[len(keys) :]

    def parts(self):
        return [self.held[offset] for offset in sorted(self.held)]


def sum_outer(parts, n):
    held = {8 * i: part for i, part in enumerate(parts)}
    for bit in outer_bits(n):
        for offset in sorted(held):
            if offset & bit:
                held[offset ^ bit] = held[offset ^ bit] + exchange(held.pop(offset), bit, n)
    return held[0]


def place_kernel(count, outer, width, me_ref, *refs):
    pieces, out, held, sems, last = refs[:count], *refs[count:]
    me = me_ref[0]
    z, y, c, x = me // 8, (me // 4) % 2, (me // 2) % 2, me % 2
    copies = []
    for i in range(count):
        part, dc, dy, dx = i // 8, (i // 4) % 2, (i // 2) % 2, i % 2
        for dz in range(outer):
            block = (((z ^ dz) * 2 + (y ^ dy)) * 2 + (c ^ dc)) * 2 + (x ^ dx)
            copies.append(
                pltpu.make_async_copy(
                    pieces[i].at[dz],
                    held.at[block, :, pl.ds(part * width, width)],
                    sems.at[len(copies)],
                )
            )
    for copy in copies:
        copy.start()
    for copy in copies:
        copy.wait()
    copy = pltpu.make_async_copy(held, out, last)
    copy.start()
    copy.wait()


class Rows:
    def __init__(self, parts, n):
        self.n = n
        self.whole = jnp.stack(parts)

    def start_plane(self):
        self.near = [exchange(self.whole, bit, self.n) for bit in (X, Y, C)]

    def end_plane(self):
        from_x, from_y, _ = self.near
        half = from_x.shape[0] // 2
        self.last = [
            exchange(from_x[:half], Y, self.n),
            exchange(from_y[half:], X, self.n),
        ]
        self.far = [exchange(v, C, self.n) for v in (from_x, from_y)]

    def pieces(self):
        last_far = [exchange(v, C, self.n) for v in self.last]
        from_x, from_y, other = self.near
        return [self.whole, from_x, from_y, *self.last, other, *self.far, *last_far]


class Plane:
    def __init__(self, value, n):
        self.n = n
        self.own = value
        self.near = [exchange(value, X, n), exchange(value, Y, n), exchange(value, C, n)]

    def end(self):
        from_x, from_y, _ = self.near
        half = from_x.shape[0] // 2
        self.last = [exchange(from_x[:half], Y, self.n), exchange(from_y[half:], X, self.n)]
        self.far = [exchange(v, C, self.n) for v in (from_x, from_y)]

    def finish(self):
        self.last_far = [exchange(v, C, self.n) for v in self.last]

    def group(self, *which):
        parts = {0: [self.own, self.near[2]], 3: self.last + self.last_far}
        for g in (1, 2):
            parts[g] = [self.near[g - 1], self.far[g - 1]]
        return [part for g in which for part in parts[g]]


class Order:
    def __init__(self):
        self.token = jnp.zeros((), F32)

    def point(self, *values):
        *values, self.token = lax.optimization_barrier((*values, self.token))
        return values[0] if len(values) == 1 else values


def half_of(block, part):
    half = block.shape[0] // 2
    return block[part * half : (part + 1) * half].astype(F32)


class PlaneSum:
    def __init__(self, n):
        self.n = n
        self.mine, self.recv = {}, {}

    def put(self, block, near, recv):
        self.mine[block], self.recv[block] = near, recv

    def held(self, block, part):
        return half_of(self.mine[block], part) + half_of(self.recv[block], part)

    def far_sends(self):
        return self.held(3, 0).astype(BF), self.held(3, 1).astype(BF)

    def near_sends(self):
        return self.held(1, 0).astype(BF), self.held(2, 1).astype(BF)

    def last_sends(self, first, second):
        return (
            (self.held(2, 0) + first.astype(F32)).astype(BF),
            (self.held(1, 1) + second.astype(F32)).astype(BF),
        )

    def hop(self, first, second):
        return exchange(first, X, self.n), exchange(second, Y, self.n)

    def last_hop(self, first, second):
        return exchange(first, Y, self.n), exchange(second, X, self.n)

    def total(self, near, last):
        return jnp.concatenate(
            [self.held(0, i) + near[i].astype(F32) + last[i].astype(F32) for i in range(2)], 0
        )


def full(value):
    shape = value.shape
    return pl.BlockSpec(shape, lambda i: (0,) * len(shape), pipeline_mode=pl.Buffered(1))


def copies_of(pieces, target, stride, sems):
    copies, row = [], 0
    for i, piece in enumerate(pieces):
        size = piece.shape[0]
        copies.append(pltpu.make_async_copy(piece, target.at[pl.ds(row, size)], sems.at[i]))
        row += stride or size
    return copies


def clear_spare(target, used, slot):
    if slot > used:
        for row in range(0, target.shape[0], slot):
            target[pl.ds(row + used, slot - used), :] = jnp.zeros(
                (slot - used, target.shape[1]), target.dtype
            )


def lift_of(adapter):
    row = lax.broadcasted_iota(jnp.int32, (TABLE, 3 * TABLE), 0)
    col = lax.broadcasted_iota(jnp.int32, (TABLE, 3 * TABLE), 1)
    goal = (row // RANK) * TABLE + adapter * RANK + row % RANK
    return ((col == goal) & (row < 3 * RANK)).astype(F32).astype(BF)


def feed_copies(feed, kind, padded, slot, target, first, columns, sems):
    start, size, to = columns
    return [
        pltpu.make_async_copy(
            feed.at[pl.ds((3 * i + kind) * padded, padded), pl.ds(start, size)],
            target.at[pl.ds(first + i * slot, padded), pl.ds(to, size)],
            sems.at[i],
        )
        for i in range(sems.shape[0])
    ]


def feed_kernel(sizes, ids_ref, feed_ref, *refs):
    parts, padded, slot, width, place = sizes
    normed_in, cot_in, refs = refs[:parts], refs[parts : 2 * parts], refs[2 * parts :]
    hidden_ref, grads_ref, near_ref, far_ref, refs = *refs[:4], refs[4:]
    w_both, w_down, normed_all, cot_all, both_all, grad_all, acts, *sems = refs
    group = pl.program_id(0)
    block, cols = hidden_ref.shape
    half = block // 2
    wide = width + TABLE
    loads = [
        copies_of(normed_in, normed_all.at[:, pl.ds(0, wide)], None, sems[0]),
        feed_copies(feed_ref, 0, padded, slot, w_both, 0, (0, wide, 0), sems[1]),
        feed_copies(feed_ref, 1, padded, slot, w_both, cols, (0, width, 0), sems[2])
        + feed_copies(feed_ref, 1, padded, slot, w_both, cols, (width, TABLE, wide), sems[3]),
        copies_of(cot_in, cot_all.at[:, pl.ds(0, width)], None, sems[4]),
        feed_copies(feed_ref, 2, padded, slot, w_down, 0, (0, wide, 0), sems[5]),
    ]

    def arrive(*which):
        @pl.when(group == 0)
        def _():
            for i in which:
                for copy in loads[i]:
                    copy.wait()

    @pl.when(group == 0)
    def _():
        for load in loads:
            for copy in load:
                copy.start()
        grads_ref[...] = jnp.zeros_like(grads_ref)
        zeros = jnp.zeros((cols, TABLE), BF)
        w_both[pl.ds(0, cols), wide:] = zeros
        w_both[pl.ds(cols, cols), width:wide] = zeros
        clear_spare(w_both, padded, slot)
        clear_spare(w_down, padded, slot)

    row = pl.multiple_of(group * block, block)
    own = pl.ds(row, block)
    arrive(0)
    for i in range(2):
        here = pl.ds(row + i * half, half)
        lows = nn(normed_all[here, width:wide], lift_of(ids_ref[place + 2 * group + i])).astype(BF)
        normed_all[here, width:] = lows[:, : 2 * TABLE]
        cot_all[here, width:] = lows[:, 2 * TABLE :]
    arrive(1, 2)
    both_all[...] = nt(normed_all[own, :], w_both[...])
    arrive(3, 4)
    grad_all[...] = nt(cot_all[own, :], w_down[...])
    step = 16

    def rows_of(i, carry):
        here = pl.ds(pl.multiple_of(i * step, step), step)
        gate, up, grad = both_all[here, :cols], both_all[here, cols:], grad_all[here, :]
        sigmoid = 0.5 * jnp.tanh(0.5 * gate) + 0.5
        silu = gate * sigmoid
        hidden_ref[here, :] = (silu * up).astype(BF)
        acts[here, :cols] = (grad * up * (sigmoid + silu * (1.0 - sigmoid))).astype(BF)
        acts[here, cols:] = (grad * silu).astype(BF)
        return carry

    lax.fori_loop(0, block // step, rows_of, 0)
    out = nn(acts[...], w_both[...]).astype(BF)
    low = nn(hidden_ref[...], w_down[:, width:]).astype(BF)
    for i, ref in enumerate((near_ref, far_ref)):
        ref[:, : wide + TABLE] = out[i * half : (i + 1) * half]
        ref[:, wide + TABLE :] = low[i * half : (i + 1) * half]
    grads_ref[0] += tn(normed_all[own, width:wide], acts[:, :cols])
    grads_ref[1] += tn(normed_all[own, wide:], acts[:, cols:])
    grads_ref[2] += tn(cot_all[own, width:], hidden_ref[...])


def feed_stage(ids, place, groups, feed, normed, cot, padded, slot):
    wide, width = normed[0].shape[1], cot[0].shape[1]
    tokens = sum(part.shape[0] for part in normed)
    block = tokens // groups
    pieces = feed.shape[0] // (3 * padded)
    cols = pieces * slot
    tile = pl.BlockSpec((block, cols), lambda i: (i, 0))
    anywhere = pl.BlockSpec(memory_space=pl.ANY)
    out = jax.ShapeDtypeStruct((tokens // 2, wide + 2 * TABLE), BF)
    out_tile = pl.BlockSpec((block // 2, wide + 2 * TABLE), lambda i: (i, 0))
    counts = (len(normed),) + (pieces,) * 3 + (len(cot), pieces)
    return pl.pallas_call(
        functools.partial(feed_kernel, (len(normed), padded, slot, width, place)),
        grid=(groups,),
        out_shape=(
            jax.ShapeDtypeStruct((tokens, cols), BF),
            jax.ShapeDtypeStruct((3, TABLE, cols), F32),
            out,
            out,
        ),
        in_specs=[pl.BlockSpec(memory_space=pltpu.SMEM)]
        + [anywhere] * (1 + len(normed) + len(cot)),
        out_specs=(
            tile,
            pl.BlockSpec((3, TABLE, cols), lambda i: (0, 0, 0)),
            out_tile,
            out_tile,
        ),
        scratch_shapes=[
            pltpu.VMEM((2 * cols, wide + TABLE), BF),
            pltpu.VMEM((cols, wide), BF),
            pltpu.VMEM((tokens, wide + TABLE), BF),
            pltpu.VMEM((tokens, wide), BF),
            pltpu.VMEM((block, 2 * cols), F32),
            pltpu.VMEM((block, cols), F32),
            pltpu.VMEM((block, 2 * cols), BF),
        ]
        + [pltpu.SemaphoreType.DMA((count,)) for count in counts],
        compiler_params=pltpu.CompilerParams(vmem_limit_bytes=44 << 20),
        cost_estimate=LIGHT,
        name="feed",
    )(ids, HBM(feed), *map(HBM, normed), *map(HBM, cot))


def down_kernel(padded, slot, *refs):
    *acts, feed_ref, near_ref, far_ref, w_down, sems = refs
    loads = feed_copies(feed_ref, 2, padded, slot, w_down, 0, (0, w_down.shape[1], 0), sems)
    for copy in loads:
        copy.start()
    clear_spare(w_down, padded, slot)
    for copy in loads:
        copy.wait()
    rows = near_ref.shape[0] // 4
    done = 0
    for act in acts:
        for i in range(act.shape[0] // (2 * rows)):
            out = nn(act[pl.ds(i * 2 * rows, 2 * rows), :], w_down[...]).astype(BF)
            near_ref[pl.ds(done, rows), :] = out[:rows]
            far_ref[pl.ds(done, rows), :] = out[rows:]
            done += rows


def down_stage(hiddens, feed, pieces, padded, slot, rows):
    width = feed.shape[1] - TABLE
    out = jax.ShapeDtypeStruct((4 * rows, width), BF)
    return pl.pallas_call(
        functools.partial(down_kernel, padded, slot),
        grid=(1,),
        out_shape=(out, out),
        in_specs=[full(v) for v in hiddens] + [pl.BlockSpec(memory_space=pl.ANY)],
        out_specs=(full(out), full(out)),
        scratch_shapes=[
            pltpu.VMEM((pieces * slot, width), BF),
            pltpu.SemaphoreType.DMA((pieces,)),
        ],
        compiler_params=pltpu.CompilerParams(vmem_limit_bytes=32 << 20),
        cost_estimate=LIGHT,
        name="down",
    )(*map(HBM, hiddens), HBM(feed))


LANES = 2 * HEAD_DIM


def swap_halves(values):
    lane = lax.broadcasted_iota(jnp.int32, values.shape, 1) % HEAD_DIM
    half = HEAD_DIM // 2
    left = pltpu.roll(values, LANES - half, 1)
    return jnp.where(lane < half, left, pltpu.roll(values, half, 1))


def rope(slab, cosine, sine):
    return slab * cosine + swap_halves(slab) * sine


def project_kernel(
    me_ref, x_ref, gain_ref, a_ref, b_ref, cos_ref, sin_ref, *refs
):
    *pieces, normed_ref, low_ref, kv_ref, w_ref, held, sems, last = refs
    copies = place_copies(me_ref[0], pieces, held, sems)
    for copy in copies:
        copy.start()
    normed = normed_of(x_ref[...].astype(F32), gain_ref[...])
    normed_ref[...] = normed
    low = nt(normed, a_ref[...]).astype(BF)
    low_ref[...] = low
    for copy in copies:
        copy.wait()
    copy = pltpu.make_async_copy(held, w_ref, last)
    copy.start()
    width = kv_ref.shape[1]
    start = held.shape[2] - width
    weights = held[:, :, start:].reshape(normed.shape[1], width)
    kv = nn(normed, weights) + nn(low, b_ref[...])
    for i in range(width // LANES):
        cols = slice(i * LANES, (i + 1) * LANES)
        slab = kv[:, cols]
        if i < width // LANES // 2:
            slab = rope(slab, cos_ref[...], sin_ref[...])
        kv_ref[:, cols] = slab.astype(BF)
    copy.wait()


def project_stage(me, x, gain, a_att, b_kv, cosine, sine, pieces, n):
    rows, width = x.shape
    outer, shard, columns = pieces[0].shape
    anywhere = pl.BlockSpec(memory_space=pl.ANY)
    outs = (
        jax.ShapeDtypeStruct((rows, width), BF),
        jax.ShapeDtypeStruct((rows, a_att.shape[0]), BF),
        jax.ShapeDtypeStruct((rows, b_kv.shape[1]), BF),
    )
    operands = (x, gain, a_att, b_kv, cosine, sine)
    normed, low, kv, weights = pl.pallas_call(
        project_kernel,
        grid=(1,),
        out_shape=(*outs, jax.ShapeDtypeStruct((n, shard, columns), BF)),
        in_specs=[pl.BlockSpec(memory_space=pltpu.SMEM)]
        + [full(v) for v in operands]
        + [anywhere] * len(pieces),
        out_specs=(*[full(v) for v in outs], anywhere),
        scratch_shapes=[
            pltpu.VMEM((n, shard, columns), BF),
            pltpu.SemaphoreType.DMA((n,)),
            pltpu.SemaphoreType.DMA(()),
        ],
        compiler_params=pltpu.CompilerParams(vmem_limit_bytes=28 << 20),
        cost_estimate=LIGHT,
        name="project",
    )(me.reshape(1), *map(HBM, operands), *map(HBM, pieces))
    return normed, low, kv, weights.reshape(n * shard, columns)


def query_kernel(normed_ref, low_ref, b_ref, w_ref, cos_ref, sin_ref, out_ref):
    query = nn(normed_ref[...], w_ref[...]) + nn(low_ref[:, :RANK], b_ref[...])
    for i in range(out_ref.shape[1] // LANES):
        cols = slice(i * LANES, (i + 1) * LANES)
        slab = rope(query[:, cols], cos_ref[...], sin_ref[...]) * HEAD_DIM ** (-0.5)
        out_ref[:, cols] = slab.astype(BF)


def query_stage(normed, low, b_query, weights, cosine, sine):
    rows, width = normed.shape
    block = width // 4
    whole = lambda v: pl.BlockSpec(v.shape, lambda i: (0, 0))
    return pl.pallas_call(
        query_kernel,
        grid=(4,),
        out_shape=jax.ShapeDtypeStruct((rows, width), BF),
        in_specs=[
            whole(normed),
            whole(low),
            pl.BlockSpec((RANK, block), lambda i: (0, i)),
            pl.BlockSpec((width, block), lambda i: (0, i)),
            whole(cosine),
            whole(sine),
        ],
        out_specs=pl.BlockSpec((rows, block), lambda i: (0, i)),
        compiler_params=pltpu.CompilerParams(vmem_limit_bytes=24 << 20),
        cost_estimate=LIGHT,
        name="query",
    )(normed, low, b_query, HBM(weights), cosine, sine)


def output_kernel(me_ref, att_ref, a_ref, b_ref, x_ref, gain_ref, a_two_ref, e_ref, *refs):
    *pieces, middle_ref, normed_ref, low_ref, ext_ref, w_ref, held, sems, last = refs
    copies = place_copies(me_ref[0], pieces, held, sems)
    for copy in copies:
        copy.start()
    attended = att_ref[...]
    low = nt(attended, a_ref[...]).astype(BF)
    low_ref[...] = low
    for copy in copies:
        copy.wait()
    copy = pltpu.make_async_copy(held, w_ref, last)
    copy.start()
    rows, width = attended.shape
    weights = held[...].reshape(width, width)
    middle = x_ref[...].astype(F32) + nn(attended, weights) + nn(low, b_ref[...])
    middle_ref[...] = middle
    normed = normed_of(middle, gain_ref[...])
    normed_ref[...] = normed
    lows = nt(normed, a_two_ref[...]).astype(BF)
    spare = jnp.zeros((rows, TABLE - 3 * RANK), BF)
    lows = jnp.concatenate([lows, e_ref[...], spare], 1)
    ext_ref[:, :width] = normed
    ext_ref[:, width:] = lows
    copy.wait()


def output_stage(me, attended, a_out, b_out, x, gain, a_two, grad_low, pieces, n):
    rows, width = attended.shape
    outer, shard, columns = pieces[0].shape
    anywhere = pl.BlockSpec(memory_space=pl.ANY)
    outs = (
        jax.ShapeDtypeStruct((rows, width), F32),
        jax.ShapeDtypeStruct((rows, width), BF),
        jax.ShapeDtypeStruct((rows, RANK), BF),
        jax.ShapeDtypeStruct((rows, width + TABLE), BF),
    )
    operands = (attended, a_out, b_out, x, gain, a_two, grad_low)
    *results, weights = pl.pallas_call(
        output_kernel,
        grid=(1,),
        out_shape=(*outs, jax.ShapeDtypeStruct((n, shard, columns), BF)),
        in_specs=[pl.BlockSpec(memory_space=pltpu.SMEM)]
        + [full(v) for v in operands]
        + [anywhere] * len(pieces),
        out_specs=(*[full(v) for v in outs], anywhere),
        scratch_shapes=[
            pltpu.VMEM((n, shard, columns), BF),
            pltpu.SemaphoreType.DMA((n,)),
            pltpu.SemaphoreType.DMA(()),
        ],
        compiler_params=pltpu.CompilerParams(vmem_limit_bytes=32 << 20),
        cost_estimate=LIGHT,
        name="output",
    )(me.reshape(1), *map(HBM, operands), *map(HBM, pieces))
    return (*results, weights.reshape(n * shard, columns))


def back_kernel(grad_ref, w_ref, low_ref, a_ref, out_ref):
    out = nt(grad_ref[...], w_ref[...]) + nn(low_ref[...], a_ref[...])
    out_ref[...] = out.astype(out_ref.dtype)


def back_stage(grad, weights, low, table, dtype):
    rows, inner = grad.shape
    width = weights.shape[0]
    block = width // 4
    whole = lambda v: pl.BlockSpec(v.shape, lambda i: (0, 0))
    return pl.pallas_call(
        back_kernel,
        grid=(4,),
        out_shape=jax.ShapeDtypeStruct((rows, width), dtype),
        in_specs=[
            whole(grad),
            pl.BlockSpec((block, inner), lambda i: (i, 0)),
            whole(low),
            pl.BlockSpec((table.shape[0], block), lambda i: (0, i)),
        ],
        out_specs=pl.BlockSpec((rows, block), lambda i: (0, i)),
        compiler_params=pltpu.CompilerParams(vmem_limit_bytes=24 << 20),
        cost_estimate=LIGHT,
        name="back",
    )(*map(HBM, (grad, weights, low, table)))


def norm_two_kernel(adapter_ref, *refs):
    mine, recv, near, last, refs = refs[0], refs[1], refs[2:4], refs[4:6], refs[6:]
    middle_ref, gain_ref, cot_ref, att_ref, low_ref, normed_ref, a_ref, b_ref, refs = *refs[:8], refs[8:]
    grad_ref, one_ref, low_out_ref, low_down_ref, gain_grad_ref, tables_ref = refs
    width = middle_ref.shape[1]
    half = middle_ref.shape[0] // 2
    came = [
        near[i][...].astype(F32) + last[i][...].astype(F32) for i in range(2)
    ]
    total = mine[...].astype(F32) + recv[...].astype(F32) + jnp.concatenate(came, 0)
    lift = lift_of(adapter_ref[0])
    lows = [
        nt(total[:, width + i * TABLE : width + (i + 1) * TABLE].astype(BF), lift[:RANK, :TABLE])
        for i in range(3)
    ]
    low_down = lows[2].astype(BF)
    low_down_ref[...] = low_down
    grad_low = jnp.concatenate(lows[:2], 1).astype(BF)
    grad = total[:, :width] + nn(grad_low, a_ref[...])
    middle = middle_ref[...]
    scale = lax.rsqrt(jnp.mean(middle * middle, -1, keepdims=True) + EPS)
    gain_grad_ref[...] = jnp.sum(grad * middle * scale, 0, keepdims=True)
    grad = grad * gain_ref[...]
    inner = jnp.mean(grad * middle, -1, keepdims=True)
    grad = cot_ref[...].astype(F32) + scale * grad - middle * (scale * scale * scale * inner)
    grad_ref[...] = grad
    one = grad.astype(BF)
    one_ref[...] = one
    low_out = nt(one, b_ref[...]).astype(BF)
    low_out_ref[...] = low_out
    tables_ref[:, :width] = tn(low_out, att_ref[...]).astype(BF)
    tables_ref[:, width : 2 * width] = tn(low_ref[...], one).astype(BF)
    both = tn(grad_low, normed_ref[...]).astype(BF)
    tables_ref[:, 2 * width : 3 * width] = both[:RANK]
    tables_ref[:, 3 * width : 4 * width] = both[RANK:]
    tables_ref[:, 4 * width :] = tn(low_down, cot_ref[...]).astype(BF)


def norm_two_stage(adapter, parts, middle, gain, cot, attended, low_out, normed, a_two, b_out):
    rows, width = middle.shape
    operands = (*parts, middle, gain, cot, attended, low_out, normed, a_two, b_out)
    outs = (
        jax.ShapeDtypeStruct((rows, width), F32),
        jax.ShapeDtypeStruct((rows, width), BF),
        jax.ShapeDtypeStruct((rows, RANK), BF),
        jax.ShapeDtypeStruct((rows, RANK), BF),
        jax.ShapeDtypeStruct((1, width), F32),
        jax.ShapeDtypeStruct((RANK, 5 * width), BF),
    )
    return pl.pallas_call(
        norm_two_kernel,
        grid=(1,),
        out_shape=outs,
        in_specs=[pl.BlockSpec(memory_space=pltpu.SMEM)] + [full(v) for v in operands],
        out_specs=tuple(full(v) for v in outs),
        compiler_params=pltpu.CompilerParams(vmem_limit_bytes=40 << 20),
        cost_estimate=LIGHT,
        name="norm_two",
    )(adapter, *map(HBM, operands))


def project_back_kernel(
    query_ref, kv_ref, came_ref, cos_ref, sin_ref, bq_ref, bkv_ref, low_ref, normed_ref, *outs
):
    grad_ref, grad_low_ref, tables_ref = outs
    width = query_ref.shape[1]
    kv_width = kv_ref.shape[1] // 2
    query = query_ref[...]
    grad_ref[:, :width] = query
    kv = kv_ref[...] + came_ref[...].astype(F32)
    for i in range(kv_ref.shape[1] // LANES):
        slab = kv[:, i * LANES : (i + 1) * LANES]
        if i < kv_width // LANES:
            slab = slab * cos_ref[...] - swap_halves(slab) * sin_ref[...]
        grad_ref[:, width + i * LANES : width + (i + 1) * LANES] = slab.astype(BF)
    kv = grad_ref[:, width:]
    grad_low = nt(kv, bkv_ref[...])
    first = lax.broadcasted_iota(jnp.int32, grad_low.shape, 1) < RANK
    table = jnp.concatenate([bq_ref[...], jnp.zeros((2 * RANK, width), BF)], 0)
    grad_low = jnp.where(first, nt(query, table), grad_low).astype(BF)
    grad_low_ref[...] = grad_low
    reduced = tn(grad_low, normed_ref[...]).astype(BF)
    for i in range(3):
        tables_ref[:, i * width : (i + 1) * width] = reduced[i * RANK : (i + 1) * RANK]
    low = low_ref[...]
    tables_ref[:, 3 * width : 4 * width] = tn(low, query)[:RANK].astype(BF)
    raised = tn(low, kv).astype(BF)
    tables_ref[:, 4 * width : 4 * width + kv_width] = raised[RANK : 2 * RANK, :kv_width]
    tables_ref[:, 4 * width + kv_width :] = raised[2 * RANK :, kv_width:]


def project_back_stage(grad_query, grad_kv, came, cosine, sine, b_query, b_kv, low, normed):
    rows, width = grad_query.shape
    kv = grad_kv.shape[1]
    operands = (grad_query, grad_kv, came, cosine, sine, b_query, b_kv, low, normed)
    outs = (
        jax.ShapeDtypeStruct((rows, width + kv), BF),
        jax.ShapeDtypeStruct(low.shape, BF),
        jax.ShapeDtypeStruct((RANK, 4 * width + kv), BF),
    )
    return pl.pallas_call(
        project_back_kernel,
        grid=(1,),
        out_shape=outs,
        in_specs=[full(v) for v in operands],
        out_specs=tuple(full(v) for v in outs),
        compiler_params=pltpu.CompilerParams(vmem_limit_bytes=32 << 20),
        cost_estimate=LIGHT,
        name="project_back",
    )(*map(HBM, operands))


def norm_one_kernel(grad_ref, w_ref, low_ref, a_ref, x_ref, gain_ref, mid_ref, out_ref, gain_grad_ref, held):
    step = pl.program_id(0)
    block = w_ref.shape[0]
    cols = pl.ds(pl.multiple_of(step * block, block), block)
    held[:, cols] = nt(grad_ref[...], w_ref[...]) + nn(low_ref[...], a_ref[...])

    @pl.when(step == pl.num_programs(0) - 1)
    def _():
        values = x_ref[...].astype(F32)
        scale = lax.rsqrt(jnp.mean(values * values, -1, keepdims=True) + EPS)
        gain_grad_ref[...] = jnp.sum(held[...] * values * scale, 0, keepdims=True)
        grad = held[...] * gain_ref[...]
        inner = jnp.mean(grad * values, -1, keepdims=True)
        out_ref[...] = mid_ref[...] + scale * grad - values * (scale * scale * scale * inner)


def norm_one_stage(grad, weights, low, table, x, gain, grad_middle):
    rows, inner = grad.shape
    width = weights.shape[0]
    block = width // 4
    whole = lambda v: pl.BlockSpec(v.shape, lambda i: (0, 0))
    return pl.pallas_call(
        norm_one_kernel,
        grid=(4,),
        out_shape=(
            jax.ShapeDtypeStruct((rows, width), F32),
            jax.ShapeDtypeStruct((1, width), F32),
        ),
        in_specs=[
            whole(grad),
            pl.BlockSpec((block, inner), lambda i: (i, 0)),
            whole(low),
            pl.BlockSpec((table.shape[0], block), lambda i: (0, i)),
            whole(x),
            whole(gain),
            whole(grad_middle),
        ],
        out_specs=(whole(grad_middle), whole(gain)),
        scratch_shapes=[pltpu.VMEM((rows, width), F32)],
        compiler_params=pltpu.CompilerParams(vmem_limit_bytes=32 << 20),
        cost_estimate=LIGHT,
        name="norm_one",
    )(*map(HBM, (grad, weights, low, table, x, gain, grad_middle)))


def head_pair(own_ref, other_ref, start, group):
    cols = pl.ds(pl.multiple_of(start + (group // 2) * LANES, LANES), LANES)
    slab = jnp.concatenate([own_ref[:, cols], other_ref[:, cols]], 0).astype(F32)
    lane = lax.broadcasted_iota(jnp.int32, slab.shape, 1)
    slab = jnp.where(group % 2 == 0, slab, pltpu.roll(slab, HEAD_DIM, 1))
    first = jnp.where(lane < HEAD_DIM, slab, 0.0)
    return first, pltpu.roll(first, HEAD_DIM, 1)


def attend_kernel(pos_ref, query_ref, own_ref, other_ref, out_ref, probs_ref):
    group = pl.program_id(0)
    rows = query_ref.shape[0]
    keys = [k.astype(BF) for k in head_pair(own_ref, other_ref, 0, group)]
    values = head_pair(own_ref, other_ref, KV_HEADS * HEAD_DIM, group)
    values = [v.T.astype(BF) for v in values]
    key_at = lax.broadcasted_iota(jnp.int32, (2 * rows, rows), 0)
    query_at = lax.broadcasted_iota(jnp.int32, (2 * rows, rows), 1)
    before = (pos_ref[1] < pos_ref[0]).astype(jnp.int32)
    visible = (key_at <= query_at) | ((key_at >= rows) & (before > 0))
    for j in range(query_ref.shape[1] // LANES):
        cols = pl.ds(j * LANES, LANES)
        query = query_ref[:, cols].astype(F32).T.astype(BF)
        mixed = 0.0
        for h in range(2):
            scores = jnp.where(visible, nn(keys[h], query), -1e30)
            weights = jnp.exp(scores - jnp.max(scores, 0, keepdims=True))
            probs = (weights * (1.0 / jnp.sum(weights, 0, keepdims=True))).astype(BF)
            probs_ref[0, 2 * j + h] = probs
            mixed += nn(values[h], probs)
        out_ref[:, cols] = mixed.T.astype(BF)


def attend_stage(blocks, query, own, other):
    rows, width = query.shape
    cols = width // KV_HEADS
    heads = HEADS // KV_HEADS
    tile = pl.BlockSpec((rows, cols), lambda i: (0, i))
    whole = pl.BlockSpec(own.shape, lambda i: (0, 0))
    return pl.pallas_call(
        attend_kernel,
        grid=(KV_HEADS,),
        out_shape=(
            jax.ShapeDtypeStruct((rows, width), BF),
            jax.ShapeDtypeStruct((KV_HEADS, heads, 2 * rows, rows), BF),
        ),
        in_specs=[pl.BlockSpec(memory_space=pltpu.SMEM), tile, whole, whole],
        out_specs=(tile, pl.BlockSpec((1, heads, 2 * rows, rows), lambda i: (i, 0, 0, 0))),
        compiler_params=pltpu.CompilerParams(vmem_limit_bytes=32 << 20),
        cost_estimate=LIGHT,
        name="attend",
    )(blocks, query, own, other)


def attend_back_kernel(
    grad_ref,
    out_ref,
    query_ref,
    own_ref,
    other_ref,
    probs_ref,
    cos_ref,
    sin_ref,
    gq_ref,
    gown_ref,
    gother_ref,
    gkv_ref,
):
    group = pl.program_id(0)
    keys = [k.T.astype(BF) for k in head_pair(own_ref, other_ref, 0, group)]
    values = head_pair(own_ref, other_ref, KV_HEADS * HEAD_DIM, group)
    values = [v.astype(BF) for v in values]
    cosine, sine = cos_ref[...], sin_ref[...]
    grad_keys, grad_values = [0.0, 0.0], [0.0, 0.0]
    for j in range(query_ref.shape[1] // LANES):
        cols = pl.ds(j * LANES, LANES)
        grad = grad_ref[:, cols]
        query = query_ref[:, cols]
        turned = grad.astype(F32).T
        product = turned * out_ref[:, cols].astype(F32).T
        turned = turned.astype(BF)
        grad_query = 0.0
        for h in range(2):
            inner = jnp.sum(product[h * HEAD_DIM : (h + 1) * HEAD_DIM], 0, keepdims=True)
            probs = probs_ref[0, 2 * j + h]
            grad_scores = (probs.astype(F32) * (nn(values[h], turned) - inner)).astype(BF)
            grad_values[h] += nn(probs, grad)
            grad_keys[h] += nn(grad_scores, query)
            grad_query += nn(keys[h], grad_scores)
        grad_query = grad_query.T * HEAD_DIM ** (-0.5)
        grad_query = grad_query * cosine - swap_halves(grad_query) * sine
        gq_ref[:, cols] = grad_query.astype(BF)

    @pl.when(group == 0)
    def _():
        gkv_ref[...] = jnp.zeros_like(gkv_ref)

    lane = lax.broadcasted_iota(jnp.int32, grad_keys[0].shape, 1)
    for start, (first, last) in ((0, grad_keys), (KV_HEADS * HEAD_DIM, grad_values)):
        total = jnp.where(lane < HEAD_DIM, first + pltpu.roll(last, HEAD_DIM, 1), 0.0)
        total = jnp.where(group % 2 == 0, total, pltpu.roll(total, HEAD_DIM, 1))
        cols = pl.ds(pl.multiple_of(start + (group // 2) * LANES, LANES), LANES)
        gkv_ref[:, cols] += total

    @pl.when(group == pl.num_programs(0) - 1)
    def _():
        rows = gown_ref.shape[0]
        gown_ref[...] = gkv_ref[pl.ds(0, rows), :]
        gother_ref[...] = gkv_ref[pl.ds(rows, rows), :].astype(BF)


def attend_back_stage(grad, out, query, own, other, probs, cosine, sine):
    rows, width = query.shape
    cols = width // KV_HEADS
    tile = pl.BlockSpec((rows, cols), lambda i: (0, i))
    whole = pl.BlockSpec(own.shape, lambda i: (0, 0))
    table = pl.BlockSpec((rows, LANES), lambda i: (0, 0))
    return pl.pallas_call(
        attend_back_kernel,
        grid=(KV_HEADS,),
        out_shape=(
            jax.ShapeDtypeStruct((rows, width), BF),
            jax.ShapeDtypeStruct(own.shape, F32),
            jax.ShapeDtypeStruct(own.shape, BF),
        ),
        scratch_shapes=[pltpu.VMEM((2 * rows, own.shape[1]), F32)],
        in_specs=[tile, tile, tile, whole, whole]
        + [pl.BlockSpec((1,) + probs.shape[1:], lambda i: (i, 0, 0, 0)), table, table],
        out_specs=(tile, whole, whole),
        compiler_params=pltpu.CompilerParams(vmem_limit_bytes=32 << 20),
        cost_estimate=LIGHT,
        name="attend_back",
    )(grad, out, query, own, other, probs, cosine, sine)


def send_columns(parts, n):
    whole = jnp.concatenate(parts, 1).astype(BF)
    whole = jnp.pad(whole, ((0, 0), (0, -whole.shape[1] % n)))
    return jnp.moveaxis(whole.reshape(RANK, n, -1), 1, 0)


def sum_columns(parts, ids, own_rows):
    n, _, chunk = parts.shape
    onehot = (ids[:, None] == jnp.arange(ADAPTERS, dtype=jnp.int32)[None, :]).astype(BF)
    summed = jnp.einsum("na,nrc->arc", onehot, parts, preferred_element_type=F32)
    return summed.reshape(n, own_rows, chunk)


def per_device(
    n,
    inputs,
    cotangent,
    adapter_ids,
    block_index,
    gain_first,
    gain_second,
    w_query,
    w_key,
    w_value,
    w_output,
    w_gate_up,
    w_down,
    reduce_attention,
    raise_query,
    raise_keyvalue,
    reduce_output,
    raise_output,
    reduce_gate_up,
    raise_gate_up,
    reduce_down,
    raise_down,
):
    width = inputs.shape[-1]
    rows = inputs.shape[-2]
    shard = w_down.shape[0]
    own_rows = raise_down.shape[0]
    gains = gain_first.shape[0]
    kv_width = KV_HEADS * HEAD_DIM
    side = lax.axis_index("seq")
    me = lax.axis_index(ALL).astype(jnp.int32)
    tokens = inputs.reshape(rows, width)
    grad_out = cotangent.reshape(rows, width)

    order = Order()
    qkv_width = width + 2 * kv_width
    att_rows = Outer(jnp.concatenate([w_query, w_key, w_value, w_output], 1), n)
    att_rows.step()
    cot_plane = Plane(grad_out, n)
    padded = -(-shard // 16) * 16
    slot = -(-(n // 8) * padded // 256) * 256 // (n // 8)
    feed = jnp.stack([w_gate_up[0].T, w_gate_up[1].T, w_down])

    table_width = 10 * width
    chunk = table_width // n
    table = jnp.concatenate(
        [reduce_attention[0], reduce_attention[1], reduce_attention[2], raise_query]
        + [reduce_output, raise_output, reduce_gate_up[0], reduce_gate_up[1], raise_down]
        + [raise_keyvalue[0], raise_keyvalue[1]],
        1,
    )
    table = jnp.pad(table, ((0, 0), (0, table_width - table.shape[1])))
    table = jnp.moveaxis(table.reshape(own_rows, n, chunk), 1, 0)
    hidden_table = jnp.stack([raise_gate_up[0], raise_gate_up[1], reduce_down])
    hidden_table = hidden_table.reshape(3, own_rows, n, shard).transpose(2, 1, 0, 3)
    hidden_table = hidden_table.reshape(n, own_rows, 3 * shard)
    small = jnp.concatenate([gain_first, gain_second, adapter_ids.astype(BF)])
    used = chunk + 3 * shard
    sent = -(-(used + small.shape[0]) // 128) * 128
    small = jnp.pad(small, (0, sent - used - small.shape[0]))
    small = jnp.broadcast_to(small, (n, own_rows, small.shape[0]))
    table = jnp.concatenate([table, hidden_table, small], -1)
    came = lax.all_to_all(table, ALL, 0, 0, tiled=True)
    cot_plane.near = att_rows.pass_through(order, *cot_plane.near)
    att_rows.step_all()
    gain_one = came[:, 0, used : used + gains].reshape(width).astype(F32)
    gain_two = came[:, 0, used + gains : used + 2 * gains].reshape(width).astype(F32)
    ids = came[:, 0, used + 2 * gains].astype(jnp.int32)
    columns = came[:, :, :chunk].reshape(ADAPTERS, RANK, chunk)
    hidden_cols = came[:, :, chunk:used].reshape(TABLE, 3, shard)
    own = lax.all_to_all(jnp.take(columns, ids, axis=0), ALL, 0, 0, tiled=True)
    feed = jnp.concatenate([feed, hidden_cols.transpose(1, 2, 0)], 2)
    feed = jnp.pad(feed, ((0, 0), (0, padded - shard), (0, 0))).reshape(3 * padded, -1)
    (feed,) = att_rows.pass_through(order, feed)
    feed = lax.all_gather(feed, "outer", axis=0, tiled=True)
    qkv_rows = Rows([part[:, :qkv_width] for part in att_rows.parts()], n)
    qkv_rows.start_plane()
    qkv_rows.near = order.point(*qkv_rows.near)
    qkv_rows.end_plane()
    own = jnp.moveaxis(own, 0, 1).reshape(RANK, table_width)
    (a_query, a_key, a_value, b_query, a_out, b_out, a_gate, a_up, b_down) = [
        own[:, i * width : (i + 1) * width] for i in range(9)
    ]
    b_key = own[:, 9 * width : 9 * width + kv_width]
    b_value = own[:, 9 * width + kv_width : 9 * width + 2 * kv_width]

    own_block = lax.dynamic_index_in_dim(block_index[0], side, 0, keepdims=False)
    other_block = lax.dynamic_index_in_dim(block_index[0], 1 - side, 0, keepdims=False)
    blocks = jnp.stack([own_block, other_block])
    cosine, sine = rotary_tables(own_block * rows + jnp.arange(rows, dtype=jnp.int32))
    a_att = jnp.concatenate([a_query, a_key, a_value], 0)
    a_two = jnp.concatenate([a_gate, a_up], 0)
    b_kv = jnp.concatenate(
        [
            jnp.zeros((RANK, 2 * kv_width), BF),
            jnp.pad(b_key, ((0, 0), (0, kv_width))),
            jnp.pad(b_value, ((0, 0), (kv_width, 0))),
        ],
        0,
    )
    grad_low_down = nt(grad_out, b_down).astype(BF)
    plane_ids = jnp.stack([ids[me], ids[me ^ C], ids[me ^ Y], ids[me ^ (Y | C)]])
    *qkv_rows.last, a_att, a_two, b_kv, cosine, sine, grad_low_down, plane_ids = order.point(
        *qkv_rows.last, a_att, a_two, b_kv, cosine, sine, grad_low_down, plane_ids
    )
    normed_one, low_att, key_value, w_qkv = project_stage(
        me, tokens, gain_one[None], a_att, b_kv, cosine, sine, qkv_rows.pieces(), n
    )
    low_query, low_key, low_value = [low_att[:, i * RANK : (i + 1) * RANK] for i in range(3)]
    (key_value,) = att_rows.pass_through(order, key_value)
    other_kv = exchange(key_value, X, n)
    out_rows = Rows([part[:, qkv_width:] for part in att_rows.parts()], n)
    query = query_stage(normed_one, low_att, b_query, w_qkv, cosine, sine)
    key_value, other_kv, query, out_rows.whole = order.point(
        key_value, other_kv, query, out_rows.whole
    )
    out_rows.start_plane()
    attended, probs = attend_stage(blocks, query, key_value, other_kv)
    probs = HBM(probs)
    attended, *out_rows.near = order.point(attended, *out_rows.near)
    out_rows.end_plane()
    attended, *out_rows.last = order.point(attended, *out_rows.last)
    cot_plane.end()
    middle, normed_two, low_out, normed_ext, w_out = output_stage(
        me,
        attended,
        a_out,
        b_out,
        tokens,
        gain_two[None],
        a_two,
        grad_low_down,
        out_rows.pieces(),
        n,
    )

    normed_ext, *cot_plane.last = order.point(normed_ext, *cot_plane.last)
    cot_plane.finish()
    normed_plane = Plane(normed_ext, n)
    normed_plane.near = order.point(*normed_plane.near)
    normed_plane.end()
    passed = order.point(
        *normed_plane.last, *normed_plane.far, *cot_plane.far, *cot_plane.last_far
    )
    normed_plane.last, normed_plane.far = passed[:2], passed[2:4]
    cot_plane.far, cot_plane.last_far = passed[4:6], passed[6:]
    normed_plane.finish()
    feed_of = lambda ids_here, place, groups: feed_stage(
        ids_here,
        place,
        len(groups),
        feed,
        normed_plane.group(*groups),
        cot_plane.group(*groups),
        padded,
        slot,
    )
    hidden_far, grads_far, near_out, far_out = feed_of(plane_ids, 2, (3,))
    normed_sum = PlaneSum(n)
    normed_sum.put(3, near_out, exchange(far_out, C, n))
    ids_mid, near_out = order.point(plane_ids, near_out)
    hidden_mid, grads_mid, near_out, far_out = feed_of(ids_mid, 0, (1, 2))
    far_sends = normed_sum.far_sends()
    near_out, far_out, *far_sends = order.point(near_out, far_out, *far_sends)
    far_came = normed_sum.hop(*far_sends)
    mid_recv = exchange(far_out, C, n)
    for j in range(2):
        part = slice(j * rows, (j + 1) * rows)
        normed_sum.put(j + 1, near_out[part], mid_recv[part])
    ids_own, *near_sends = order.point(plane_ids, *normed_sum.near_sends())
    near_came = normed_sum.hop(*near_sends)
    hidden_own, grads_own, near_out, far_out = feed_of(ids_own, 0, (0,))
    recv = exchange(far_out, C, n)
    near_out, grads_own, *came = order.point(near_out, grads_own, *far_came, *near_came)
    far_came, near_came = came[:2], came[2:]
    hidden_grads = grads_own + grads_mid + grads_far
    hidden_grads = jnp.concatenate([hidden_grads[i] for i in range(3)], 1).astype(BF)
    hidden_grads = hidden_grads.reshape(n, own_rows, -1)
    last_sends = order.point(*normed_sum.last_sends(*far_came))
    last_came = normed_sum.last_hop(*last_sends)
    hidden_own, hidden_grads = order.point(hidden_own, hidden_grads)
    hidden_grads = lax.all_to_all(hidden_grads, ALL, 0, 0, tiled=True)
    down_near, down_far = down_stage(
        [hidden_own, hidden_mid, hidden_far], feed, n // 8, padded, slot, rows
    )
    parts = order.point(recv, *near_came, *last_came, down_far)
    down_far = parts[5]
    parts = (near_out, *parts[:5])

    grad_middle, grad_one, grad_low_out, low_down, gain_grad_two, early = norm_two_stage(
        adapter_ids, parts, middle, gain_two[None], grad_out, attended, low_out, normed_two, a_two, b_out
    )
    down_recv = exchange(down_far, C, n)
    grad_attended = back_stage(grad_one, w_out, grad_low_out, a_out, BF)
    down_sum = PlaneSum(n)
    for i in range(4):
        part = slice(i * rows, (i + 1) * rows)
        down_sum.put(i, down_near[part], down_recv[part])
    grad_query, grad_kv, kv_away = attend_back_stage(
        grad_attended, attended, query, key_value, other_kv, probs, cosine, sine
    )
    grad_query, grad_kv, kv_away, hidden_grads = order.point(
        grad_query, grad_kv, kv_away, hidden_grads
    )
    kv_came = exchange(kv_away, X, n)
    grad_qkv, grad_low_att, late = project_back_stage(
        grad_query, grad_kv, kv_came, cosine, sine, b_query, b_kv, low_att, normed_one
    )

    late, down_near = order.point(send_columns([late, early], n), down_near)
    late = lax.all_to_all(late, ALL, 0, 0, tiled=True)
    for i in range(4):
        down_sum.mine[i] = down_near[i * rows : (i + 1) * rows]
    grad_qkv, *sends = order.point(
        grad_qkv, *down_sum.far_sends(), *down_sum.near_sends()
    )
    down_far = down_sum.hop(*sends[:2])
    down_near = down_sum.hop(*sends[2:])
    input_grad, gain_grad_one = norm_one_stage(
        grad_qkv, w_qkv, grad_low_att, a_att, tokens, gain_one[None], grad_middle
    )
    input_grad = input_grad.reshape(inputs.shape)
    gain_grads = jnp.concatenate(
        [gain_grad_one.reshape(n, gains), gain_grad_two.reshape(n, gains)], 1
    )
    gain_grads = jnp.broadcast_to(gain_grads[:, None], (n, own_rows, 2 * gains))
    input_grad, gain_grads, *down_far = order.point(input_grad, gain_grads, *down_far)
    down_last = down_sum.last_hop(*down_sum.last_sends(*down_far))
    late = jnp.concatenate([sum_columns(late, ids, own_rows), gain_grads], -1)
    late, hidden_grads, down_sum.mine[0] = order.point(late, hidden_grads, down_sum.mine[0])
    late = lax.all_to_all(late, ALL, 0, 0, tiled=True)
    branch_two = down_sum.total(down_near, down_last)
    output = (middle + branch_two + nn(low_down, b_down)).astype(BF)
    hidden_grads = hidden_grads.reshape(n // 8, 8, own_rows, 3, n // 8, slot)
    hidden_grads = jnp.sum(hidden_grads[..., :shard].astype(F32), 0)
    hidden_grads = hidden_grads.transpose(2, 1, 3, 0, 4).reshape(3, own_rows, -1)
    gain_grads = jnp.sum(late[:, 0, -2 * gains :], 0) + order.token
    late_rows = jnp.moveaxis(late[:, :, : -2 * gains], 0, 1).reshape(own_rows, -1)
    parts = [late_rows[:, i * width : (i + 1) * width] for i in range(4)]
    kv = late_rows[:, 4 * width : 4 * width + 2 * kv_width]
    start = 4 * width + 2 * kv_width
    parts += [late_rows[:, start + i * width : start + (i + 1) * width] for i in range(5)]
    return (
        output.reshape(inputs.shape),
        input_grad,
        gain_grads[:gains],
        gain_grads[gains:],
        jnp.stack(parts[:3]),
        parts[3],
        jnp.stack([kv[:, :kv_width], kv[:, kv_width:]]),
        parts[4],
        parts[5],
        jnp.stack(parts[6:8]),
        hidden_grads[:2],
        hidden_grads[2],
        parts[8],
    )


def solution(mesh):
    dp, seq = mesh.shape["dp"], mesh.shape["seq"]
    n = dp * seq
    dp_axes = ALL[:2]
    rows = P(ALL, None)
    stacked = P(None, ALL, None)
    vector = P(ALL)
    blocks = P(dp_axes, "seq", None, None)
    return jax.shard_map(
        functools.partial(per_device, n),
        mesh=Mesh(mesh.devices.reshape(dp // 4, 4, seq), ALL),
        in_specs=(
            (blocks, blocks, P(dp_axes), P(dp_axes, None), vector, vector)
            + (rows, rows, rows, rows, P(None, None, ALL), rows)
            + (stacked, rows, stacked, rows, rows, stacked, stacked, rows, rows)
        ),
        out_specs=(
            (blocks, blocks, vector, vector, stacked, rows, stacked, rows, rows)
            + (stacked, stacked, rows, rows)
        ),
        check_vma=False,
    )
```

```python
import functools

import jax
import jax.numpy as jnp
from jax import lax
from jax.experimental import pallas as pl
from jax.experimental.pallas import tpu as pltpu
from jax.sharding import Mesh
from jax.sharding import PartitionSpec as P

HEADS = 32
KV_HEADS = 4
HEAD_DIM = 64
ADAPTERS = 8
RANK = 16
TABLE = ADAPTERS * RANK

EPS = 1e-05
THETA = 10000.0

ALL = ("outer", "pair", "seq")
X, C, Y = 1, 2, 4
BF = jnp.bfloat16
F32 = jnp.float32
HBM = lambda value: pltpu.with_memory_space_constraint(value, pltpu.HBM)
LIGHT = pl.CostEstimate(flops=1 << 20, bytes_accessed=1 << 16, transcendentals=0)


def dot(a, b, dims):
    return lax.dot_general(a, b, (dims, ((), ())), preferred_element_type=F32)


def nn(a, b):
    return dot(a, b, ((1,), (0,)))


def nt(a, b):
    return dot(a, b, ((1,), (1,)))


def tn(a, b):
    return dot(a, b, ((0,), (0,)))


def exchange(value, mask, n):
    return lax.ppermute(value, ALL, [(i, i ^ mask) for i in range(n)])


def rotary_tables(positions):
    half = HEAD_DIM // 2
    speeds = THETA ** (-jnp.arange(half, dtype=F32) * (2.0 / HEAD_DIM))
    angles = positions.astype(F32)[:, None] * speeds
    cosine, sine = jnp.cos(angles), jnp.sin(angles)
    return jnp.tile(cosine, (1, 4)), jnp.tile(jnp.concatenate([-sine, sine], 1), (1, 2))


def outer_bits(n):
    bits, bit = [], 8
    while bit < n:
        bits.append(bit)
        bit *= 2
    return bits


class Outer:
    def __init__(self, value, n):
        self.n = n
        self.held = {0: value}
        self.offsets = sorted(range(8, n, 8), key=lambda offset: (bin(offset).count("1"), -offset))

    def step(self):
        if not self.offsets:
            return False
        level = bin(self.offsets[0]).count("1")
        while self.offsets and bin(self.offsets[0]).count("1") == level:
            offset = self.offsets.pop(0)
            low = offset & -offset
            self.held[offset] = exchange(self.held[offset ^ low], low, self.n)
        return bool(self.offsets)

    def step_all(self):
        while self.step():
            pass

    def pass_through(self, order, *others):
        keys = sorted(self.held)
        passed = order.point(*[self.held[k] for k in keys], *others)
        self.held = dict(zip(keys, passed))
        return passed[len(keys) :]

    def parts(self):
        return [self.held[offset] for offset in sorted(self.held)]


def place_copies(me, pieces, held, sems):
    z, y, c, x = me // 8, (me // 4) % 2, (me // 2) % 2, me % 2
    copies = []
    for i, piece in enumerate(pieces):
        dc, kind = i // 5, i % 5
        dy, dx = ((0, 0), (0, 1), (1, 0), (1, 1), (1, 1))[kind]
        first = piece.shape[0] if kind == 4 else 0
        for j in range(piece.shape[0]):
            dz = first + j
            block = (((z ^ dz) * 2 + (y ^ dy)) * 2 + (c ^ dc)) * 2 + (x ^ dx)
            rows = pl.ds(pl.multiple_of(block * piece.shape[1], piece.shape[1]), piece.shape[1])
            copies.append(
                pltpu.make_async_copy(piece.at[j], held.at[rows], sems.at[len(copies)])
            )
    return copies


def normed_of(values, gain):
    scale = lax.rsqrt(jnp.mean(values * values, -1, keepdims=True) + EPS)
    return (values * scale * gain).astype(BF)


class Outer:
    def __init__(self, value, n):
        self.n = n
        self.held = {0: value}
        self.offsets = sorted(range(8, n, 8), key=lambda offset: (bin(offset).count("1"), -offset))

    def step(self):
        if not self.offsets:
            return False
        level = bin(self.offsets[0]).count("1")
        while self.offsets and bin(self.offsets[0]).count("1") == level:
            offset = self.offsets.pop(0)
            low = offset & -offset
            self.held[offset] = exchange(self.held[offset ^ low], low, self.n)
        return bool(self.offsets)

    def step_all(self):
        while self.step():
            pass

    def pass_through(self, order, *others):
        keys = sorted(self.held)
        passed = order.point(*[self.held[k] for k in keys], *others)
        self.held = dict(zip(keys, passed))
        return passed[len(keys) :]

    def parts(self):
        return [self.held[offset] for offset in sorted(self.held)]


def sum_outer(parts, n):
    held = {8 * i: part for i, part in enumerate(parts)}
    for bit in outer_bits(n):
        for offset in sorted(held):
            if offset & bit:
                held[offset ^ bit] = held[offset ^ bit] + exchange(held.pop(offset), bit, n)
    return held[0]


def place_kernel(count, outer, width, me_ref, *refs):
    pieces, out, held, sems, last = refs[:count], *refs[count:]
    me = me_ref[0]
    z, y, c, x = me // 8, (me // 4) % 2, (me // 2) % 2, me % 2
    copies = []
    for i in range(count):
        part, dc, dy, dx = i // 8, (i // 4) % 2, (i // 2) % 2, i % 2
        for dz in range(outer):
            block = (((z ^ dz) * 2 + (y ^ dy)) * 2 + (c ^ dc)) * 2 + (x ^ dx)
            copies.append(
                pltpu.make_async_copy(
                    pieces[i].at[dz],
                    held.at[block, :, pl.ds(part * width, width)],
                    sems.at[len(copies)],
                )
            )
    for copy in copies:
        copy.start()
    for copy in copies:
        copy.wait()
    copy = pltpu.make_async_copy(held, out, last)
    copy.start()
    copy.wait()


class Rows:
    def __init__(self, parts, n):
        self.n = n
        self.whole = jnp.stack(parts)

    def start_plane(self):
        self.near = [exchange(self.whole, bit, self.n) for bit in (X, Y, C)]

    def end_plane(self):
        from_x, from_y, _ = self.near
        half = from_x.shape[0] // 2
        self.last = [
            exchange(from_x[:half], Y, self.n),
            exchange(from_y[half:], X, self.n),
        ]
        self.far = [exchange(v, C, self.n) for v in (from_x, from_y)]

    def pieces(self):
        last_far = [exchange(v, C, self.n) for v in self.last]
        from_x, from_y, other = self.near
        return [self.whole, from_x, from_y, *self.last, other, *self.far, *last_far]


class Plane:
    def __init__(self, value, n):
        self.n = n
        self.own = value
        self.near = [exchange(value, X, n), exchange(value, Y, n), exchange(value, C, n)]

    def end(self):
        from_x, from_y, _ = self.near
        half = from_x.shape[0] // 2
        self.last = [exchange(from_x[:half], Y, self.n), exchange(from_y[half:], X, self.n)]
        self.far = [exchange(v, C, self.n) for v in (from_x, from_y)]

    def finish(self):
        self.last_far = [exchange(v, C, self.n) for v in self.last]

    def group(self, *which):
        parts = {0: [self.own, self.near[2]], 3: self.last + self.last_far}
        for g in (1, 2):
            parts[g] = [self.near[g - 1], self.far[g - 1]]
        return [part for g in which for part in parts[g]]


class Order:
    def __init__(self):
        self.token = jnp.zeros((), F32)

    def point(self, *values):
        *values, self.token = lax.optimization_barrier((*values, self.token))
        return values[0] if len(values) == 1 else values


def half_of(block, part):
    half = block.shape[0] // 2
    return block[part * half : (part + 1) * half].astype(F32)


class PlaneSum:
    def __init__(self, n):
        self.n = n
        self.mine, self.recv = {}, {}

    def put(self, block, near, recv):
        self.mine[block], self.recv[block] = near, recv

    def held(self, block, part):
        return half_of(self.mine[block], part) + half_of(self.recv[block], part)

    def far_sends(self):
        return self.held(3, 0).astype(BF), self.held(3, 1).astype(BF)

    def near_sends(self):
        return self.held(1, 0).astype(BF), self.held(2, 1).astype(BF)

    def last_sends(self, first, second):
        return (
            (self.held(2, 0) + first.astype(F32)).astype(BF),
            (self.held(1, 1) + second.astype(F32)).astype(BF),
        )

    def hop(self, first, second):
        return exchange(first, X, self.n), exchange(second, Y, self.n)

    def last_hop(self, first, second):
        return exchange(first, Y, self.n), exchange(second, X, self.n)

    def total(self, near, last):
        return jnp.concatenate(
            [self.held(0, i) + near[i].astype(F32) + last[i].astype(F32) for i in range(2)], 0
        )


def full(value):
    shape = value.shape
    return pl.BlockSpec(shape, lambda i: (0,) * len(shape), pipeline_mode=pl.Buffered(1))


def copies_of(pieces, target, stride, sems):
    copies, row = [], 0
    for i, piece in enumerate(pieces):
        size = piece.shape[0]
        copies.append(pltpu.make_async_copy(piece, target.at[pl.ds(row, size)], sems.at[i]))
        row += stride or size
    return copies


def clear_spare(target, used, slot):
    if slot > used:
        for row in range(0, target.shape[0], slot):
            target[pl.ds(row + used, slot - used), :] = jnp.zeros(
                (slot - used, target.shape[1]), target.dtype
            )


def lift_of(adapter):
    row = lax.broadcasted_iota(jnp.int32, (TABLE, 3 * TABLE), 0)
    col = lax.broadcasted_iota(jnp.int32, (TABLE, 3 * TABLE), 1)
    goal = (row // RANK) * TABLE + adapter * RANK + row % RANK
    return ((col == goal) & (row < 3 * RANK)).astype(F32).astype(BF)


def feed_copies(feed, kind, padded, slot, target, first, columns, sems):
    start, size, to = columns
    return [
        pltpu.make_async_copy(
            feed.at[pl.ds((3 * i + kind) * padded, padded), pl.ds(start, size)],
            target.at[pl.ds(first + i * slot, padded), pl.ds(to, size)],
            sems.at[i],
        )
        for i in range(sems.shape[0])
    ]


def feed_kernel(sizes, ids_ref, feed_ref, *refs):
    parts, padded, slot, width, place = sizes
    normed_in, cot_in, refs = refs[:parts], refs[parts : 2 * parts], refs[2 * parts :]
    hidden_ref, grads_ref, near_ref, far_ref, refs = *refs[:4], refs[4:]
    w_both, w_down, normed_all, cot_all, both_all, grad_all, acts, *sems = refs
    group = pl.program_id(0)
    block, cols = hidden_ref.shape
    half = block // 2
    wide = width + TABLE
    loads = [
        copies_of(normed_in, normed_all.at[:, pl.ds(0, wide)], None, sems[0]),
        feed_copies(feed_ref, 0, padded, slot, w_both, 0, (0, wide, 0), sems[1]),
        feed_copies(feed_ref, 1, padded, slot, w_both, cols, (0, width, 0), sems[2])
        + feed_copies(feed_ref, 1, padded, slot, w_both, cols, (width, TABLE, wide), sems[3]),
        copies_of(cot_in, cot_all.at[:, pl.ds(0, width)], None, sems[4]),
        feed_copies(feed_ref, 2, padded, slot, w_down, 0, (0, wide, 0), sems[5]),
    ]

    def arrive(*which):
        @pl.when(group == 0)
        def _():
            for i in which:
                for copy in loads[i]:
                    copy.wait()

    @pl.when(group == 0)
    def _():
        for load in loads:
            for copy in load:
                copy.start()
        grads_ref[...] = jnp.zeros_like(grads_ref)
        zeros = jnp.zeros((cols, TABLE), BF)
        w_both[pl.ds(0, cols), wide:] = zeros
        w_both[pl.ds(cols, cols), width:wide] = zeros
        clear_spare(w_both, padded, slot)
        clear_spare(w_down, padded, slot)

    row = pl.multiple_of(group * block, block)
    own = pl.ds(row, block)
    arrive(0)
    for i in range(2):
        here = pl.ds(row + i * half, half)
        lows = nn(normed_all[here, width:wide], lift_of(ids_ref[place + 2 * group + i])).astype(BF)
        normed_all[here, width:] = lows[:, : 2 * TABLE]
        cot_all[here, width:] = lows[:, 2 * TABLE :]
    arrive(1, 2)
    both_all[...] = nt(normed_all[own, :], w_both[...])
    arrive(3, 4)
    grad_all[...] = nt(cot_all[own, :], w_down[...])
    step = 16

    def rows_of(i, carry):
        here = pl.ds(pl.multiple_of(i * step, step), step)
        gate, up, grad = both_all[here, :cols], both_all[here, cols:], grad_all[here, :]
        sigmoid = 0.5 * jnp.tanh(0.5 * gate) + 0.5
        silu = gate * sigmoid
        hidden_ref[here, :] = (silu * up).astype(BF)
        acts[here, :cols] = (grad * up * (sigmoid + silu * (1.0 - sigmoid))).astype(BF)
        acts[here, cols:] = (grad * silu).astype(BF)
        return carry

    lax.fori_loop(0, block // step, rows_of, 0)
    out = nn(acts[...], w_both[...]).astype(BF)
    low = nn(hidden_ref[...], w_down[:, width:]).astype(BF)
    for i, ref in enumerate((near_ref, far_ref)):
        ref[:, : wide + TABLE] = out[i * half : (i + 1) * half]
        ref[:, wide + TABLE :] = low[i * half : (i + 1) * half]
    grads_ref[0] += tn(normed_all[own, width:wide], acts[:, :cols])
    grads_ref[1] += tn(normed_all[own, wide:], acts[:, cols:])
    grads_ref[2] += tn(cot_all[own, width:], hidden_ref[...])


def feed_stage(ids, place, groups, feed, normed, cot, padded, slot):
    wide, width = normed[0].shape[1], cot[0].shape[1]
    tokens = sum(part.shape[0] for part in normed)
    block = tokens // groups
    pieces = feed.shape[0] // (3 * padded)
    cols = pieces * slot
    tile = pl.BlockSpec((block, cols), lambda i: (i, 0))
    anywhere = pl.BlockSpec(memory_space=pl.ANY)
    out = jax.ShapeDtypeStruct((tokens // 2, wide + 2 * TABLE), BF)
    out_tile = pl.BlockSpec((block // 2, wide + 2 * TABLE), lambda i: (i, 0))
    counts = (len(normed),) + (pieces,) * 3 + (len(cot), pieces)
    return pl.pallas_call(
        functools.partial(feed_kernel, (len(normed), padded, slot, width, place)),
        grid=(groups,),
        out_shape=(
            jax.ShapeDtypeStruct((tokens, cols), BF),
            jax.ShapeDtypeStruct((3, TABLE, cols), F32),
            out,
            out,
        ),
        in_specs=[pl.BlockSpec(memory_space=pltpu.SMEM)]
        + [anywhere] * (1 + len(normed) + len(cot)),
        out_specs=(
            tile,
            pl.BlockSpec((3, TABLE, cols), lambda i: (0, 0, 0)),
            out_tile,
            out_tile,
        ),
        scratch_shapes=[
            pltpu.VMEM((2 * cols, wide + TABLE), BF),
            pltpu.VMEM((cols, wide), BF),
            pltpu.VMEM((tokens, wide + TABLE), BF),
            pltpu.VMEM((tokens, wide), BF),
            pltpu.VMEM((block, 2 * cols), F32),
            pltpu.VMEM((block, cols), F32),
            pltpu.VMEM((block, 2 * cols), BF),
        ]
        + [pltpu.SemaphoreType.DMA((count,)) for count in counts],
        compiler_params=pltpu.CompilerParams(vmem_limit_bytes=44 << 20),
        cost_estimate=LIGHT,
        name="feed",
    )(ids, HBM(feed), *map(HBM, normed), *map(HBM, cot))


def down_kernel(padded, slot, *refs):
    *acts, feed_ref, near_ref, far_ref, w_down, sems = refs
    loads = feed_copies(feed_ref, 2, padded, slot, w_down, 0, (0, w_down.shape[1], 0), sems)
    for copy in loads:
        copy.start()
    clear_spare(w_down, padded, slot)
    for copy in loads:
        copy.wait()
    rows = near_ref.shape[0] // 4
    done = 0
    for act in acts:
        for i in range(act.shape[0] // (2 * rows)):
            out = nn(act[pl.ds(i * 2 * rows, 2 * rows), :], w_down[...]).astype(BF)
            near_ref[pl.ds(done, rows), :] = out[:rows]
            far_ref[pl.ds(done, rows), :] = out[rows:]
            done += rows


def down_stage(hiddens, feed, pieces, padded, slot, rows):
    width = feed.shape[1] - TABLE
    out = jax.ShapeDtypeStruct((4 * rows, width), BF)
    return pl.pallas_call(
        functools.partial(down_kernel, padded, slot),
        grid=(1,),
        out_shape=(out, out),
        in_specs=[full(v) for v in hiddens] + [pl.BlockSpec(memory_space=pl.ANY)],
        out_specs=(full(out), full(out)),
        scratch_shapes=[
            pltpu.VMEM((pieces * slot, width), BF),
            pltpu.SemaphoreType.DMA((pieces,)),
        ],
        compiler_params=pltpu.CompilerParams(vmem_limit_bytes=32 << 20),
        cost_estimate=LIGHT,
        name="down",
    )(*map(HBM, hiddens), HBM(feed))


LANES = 2 * HEAD_DIM


def swap_halves(values):
    lane = lax.broadcasted_iota(jnp.int32, values.shape, 1) % HEAD_DIM
    half = HEAD_DIM // 2
    left = pltpu.roll(values, LANES - half, 1)
    return jnp.where(lane < half, left, pltpu.roll(values, half, 1))


def rope(slab, cosine, sine):
    return slab * cosine + swap_halves(slab) * sine


def project_kernel(
    me_ref, x_ref, gain_ref, a_ref, b_ref, cos_ref, sin_ref, *refs
):
    *pieces, normed_ref, low_ref, kv_ref, w_ref, held, sems, last = refs
    copies = place_copies(me_ref[0], pieces, held, sems)
    for copy in copies:
        copy.start()
    normed = normed_of(x_ref[...].astype(F32), gain_ref[...])
    normed_ref[...] = normed
    low = nt(normed, a_ref[...]).astype(BF)
    low_ref[...] = low
    for copy in copies:
        copy.wait()
    copy = pltpu.make_async_copy(held, w_ref, last)
    copy.start()
    width = kv_ref.shape[1]
    kv = nn(normed, held[:, held.shape[1] - width :]) + nn(low, b_ref[...])
    for i in range(width // LANES):
        cols = slice(i * LANES, (i + 1) * LANES)
        slab = kv[:, cols]
        if i < width // LANES // 2:
            slab = rope(slab, cos_ref[...], sin_ref[...])
        kv_ref[:, cols] = slab.astype(BF)
    copy.wait()


def project_stage(me, x, gain, a_att, b_kv, cosine, sine, pieces, n):
    rows, width = x.shape
    outer, shard, columns = pieces[0].shape
    anywhere = pl.BlockSpec(memory_space=pl.ANY)
    outs = (
        jax.ShapeDtypeStruct((rows, width), BF),
        jax.ShapeDtypeStruct((rows, a_att.shape[0]), BF),
        jax.ShapeDtypeStruct((rows, b_kv.shape[1]), BF),
    )
    operands = (x, gain, a_att, b_kv, cosine, sine)
    normed, low, kv, weights = pl.pallas_call(
        project_kernel,
        grid=(1,),
        out_shape=(*outs, pltpu.HBM((n * shard, columns), BF)),
        in_specs=[pl.BlockSpec(memory_space=pltpu.SMEM)]
        + [full(v) for v in operands]
        + [anywhere] * len(pieces),
        out_specs=(*[full(v) for v in outs], anywhere),
        scratch_shapes=[
            pltpu.VMEM((n * shard, columns), BF),
            pltpu.SemaphoreType.DMA((n,)),
            pltpu.SemaphoreType.DMA(()),
        ],
        compiler_params=pltpu.CompilerParams(vmem_limit_bytes=28 << 20),
        cost_estimate=LIGHT,
        name="project",
    )(me.reshape(1), *map(HBM, operands), *map(HBM, pieces))
    return normed, low, kv, weights


def query_kernel(normed_ref, low_ref, b_ref, w_ref, cos_ref, sin_ref, out_ref):
    query = nn(normed_ref[...], w_ref[...]) + nn(low_ref[:, :RANK], b_ref[...])
    for i in range(out_ref.shape[1] // LANES):
        cols = slice(i * LANES, (i + 1) * LANES)
        slab = rope(query[:, cols], cos_ref[...], sin_ref[...]) * HEAD_DIM ** (-0.5)
        out_ref[:, cols] = slab.astype(BF)


def query_stage(normed, low, b_query, weights, cosine, sine):
    rows, width = normed.shape
    block = width // 4
    whole = lambda v: pl.BlockSpec(v.shape, lambda i: (0, 0))
    return pl.pallas_call(
        query_kernel,
        grid=(4,),
        out_shape=jax.ShapeDtypeStruct((rows, width), BF),
        in_specs=[
            whole(normed),
            whole(low),
            pl.BlockSpec((RANK, block), lambda i: (0, i)),
            pl.BlockSpec((width, block), lambda i: (0, i)),
            whole(cosine),
            whole(sine),
        ],
        out_specs=pl.BlockSpec((rows, block), lambda i: (0, i)),
        compiler_params=pltpu.CompilerParams(vmem_limit_bytes=24 << 20),
        cost_estimate=LIGHT,
        name="query",
    )(normed, low, b_query, HBM(weights), cosine, sine)


def output_kernel(me_ref, att_ref, a_ref, b_ref, x_ref, gain_ref, a_two_ref, e_ref, *refs):
    *pieces, middle_ref, normed_ref, low_ref, ext_ref, w_ref, held, sems, last = refs
    copies = place_copies(me_ref[0], pieces, held, sems)
    for copy in copies:
        copy.start()
    attended = att_ref[...]
    low = nt(attended, a_ref[...]).astype(BF)
    low_ref[...] = low
    for copy in copies:
        copy.wait()
    copy = pltpu.make_async_copy(held, w_ref, last)
    copy.start()
    rows, width = attended.shape
    middle = x_ref[...].astype(F32) + nn(attended, held[...]) + nn(low, b_ref[...])
    middle_ref[...] = middle
    normed = normed_of(middle, gain_ref[...])
    normed_ref[...] = normed
    lows = nt(normed, a_two_ref[...]).astype(BF)
    spare = jnp.zeros((rows, TABLE - 3 * RANK), BF)
    lows = jnp.concatenate([lows, e_ref[...], spare], 1)
    ext_ref[:, :width] = normed
    ext_ref[:, width:] = lows
    copy.wait()


def output_stage(me, attended, a_out, b_out, x, gain, a_two, grad_low, pieces, n):
    rows, width = attended.shape
    outer, shard, columns = pieces[0].shape
    anywhere = pl.BlockSpec(memory_space=pl.ANY)
    outs = (
        jax.ShapeDtypeStruct((rows, width), F32),
        jax.ShapeDtypeStruct((rows, width), BF),
        jax.ShapeDtypeStruct((rows, RANK), BF),
        jax.ShapeDtypeStruct((rows, width + TABLE), BF),
    )
    operands = (attended, a_out, b_out, x, gain, a_two, grad_low)
    *results, weights = pl.pallas_call(
        output_kernel,
        grid=(1,),
        out_shape=(*outs, pltpu.HBM((n * shard, columns), BF)),
        in_specs=[pl.BlockSpec(memory_space=pltpu.SMEM)]
        + [full(v) for v in operands]
        + [anywhere] * len(pieces),
        out_specs=(*[full(v) for v in outs], anywhere),
        scratch_shapes=[
            pltpu.VMEM((n * shard, columns), BF),
            pltpu.SemaphoreType.DMA((n,)),
            pltpu.SemaphoreType.DMA(()),
        ],
        compiler_params=pltpu.CompilerParams(vmem_limit_bytes=32 << 20),
        cost_estimate=LIGHT,
        name="output",
    )(me.reshape(1), *map(HBM, operands), *map(HBM, pieces))
    return (*results, weights)


def back_kernel(grad_ref, w_ref, low_ref, a_ref, out_ref):
    out = nt(grad_ref[...], w_ref[...]) + nn(low_ref[...], a_ref[...])
    out_ref[...] = out.astype(out_ref.dtype)


def back_stage(grad, weights, low, table, dtype):
    rows, inner = grad.shape
    width = weights.shape[0]
    block = width // 4
    whole = lambda v: pl.BlockSpec(v.shape, lambda i: (0, 0))
    return pl.pallas_call(
        back_kernel,
        grid=(4,),
        out_shape=jax.ShapeDtypeStruct((rows, width), dtype),
        in_specs=[
            whole(grad),
            pl.BlockSpec((block, inner), lambda i: (i, 0)),
            whole(low),
            pl.BlockSpec((table.shape[0], block), lambda i: (0, i)),
        ],
        out_specs=pl.BlockSpec((rows, block), lambda i: (0, i)),
        compiler_params=pltpu.CompilerParams(vmem_limit_bytes=24 << 20),
        cost_estimate=LIGHT,
        name="back",
    )(*map(HBM, (grad, weights, low, table)))


def norm_two_kernel(adapter_ref, *refs):
    mine, recv, near, last, refs = refs[0], refs[1], refs[2:4], refs[4:6], refs[6:]
    middle_ref, gain_ref, cot_ref, att_ref, low_ref, normed_ref, a_ref, b_ref, refs = *refs[:8], refs[8:]
    grad_ref, one_ref, low_out_ref, low_down_ref, gain_grad_ref, tables_ref = refs
    width = middle_ref.shape[1]
    half = middle_ref.shape[0] // 2
    came = [
        near[i][...].astype(F32) + last[i][...].astype(F32) for i in range(2)
    ]
    total = mine[...].astype(F32) + recv[...].astype(F32) + jnp.concatenate(came, 0)
    lift = lift_of(adapter_ref[0])
    lows = [
        nt(total[:, width + i * TABLE : width + (i + 1) * TABLE].astype(BF), lift[:RANK, :TABLE])
        for i in range(3)
    ]
    low_down = lows[2].astype(BF)
    low_down_ref[...] = low_down
    grad_low = jnp.concatenate(lows[:2], 1).astype(BF)
    grad = total[:, :width] + nn(grad_low, a_ref[...])
    middle = middle_ref[...]
    scale = lax.rsqrt(jnp.mean(middle * middle, -1, keepdims=True) + EPS)
    gain_grad_ref[...] = jnp.sum(grad * middle * scale, 0, keepdims=True)
    grad = grad * gain_ref[...]
    inner = jnp.mean(grad * middle, -1, keepdims=True)
    grad = cot_ref[...].astype(F32) + scale * grad - middle * (scale * scale * scale * inner)
    grad_ref[...] = grad
    one = grad.astype(BF)
    one_ref[...] = one
    low_out = nt(one, b_ref[...]).astype(BF)
    low_out_ref[...] = low_out
    tables_ref[:, :width] = tn(low_out, att_ref[...]).astype(BF)
    tables_ref[:, width : 2 * width] = tn(low_ref[...], one).astype(BF)
    both = tn(grad_low, normed_ref[...]).astype(BF)
    tables_ref[:, 2 * width : 3 * width] = both[:RANK]
    tables_ref[:, 3 * width : 4 * width] = both[RANK:]
    tables_ref[:, 4 * width :] = tn(low_down, cot_ref[...]).astype(BF)


def norm_two_stage(adapter, parts, middle, gain, cot, attended, low_out, normed, a_two, b_out):
    rows, width = middle.shape
    operands = (*parts, middle, gain, cot, attended, low_out, normed, a_two, b_out)
    outs = (
        jax.ShapeDtypeStruct((rows, width), F32),
        jax.ShapeDtypeStruct((rows, width), BF),
        jax.ShapeDtypeStruct((rows, RANK), BF),
        jax.ShapeDtypeStruct((rows, RANK), BF),
        jax.ShapeDtypeStruct((1, width), F32),
        jax.ShapeDtypeStruct((RANK, 5 * width), BF),
    )
    return pl.pallas_call(
        norm_two_kernel,
        grid=(1,),
        out_shape=outs,
        in_specs=[pl.BlockSpec(memory_space=pltpu.SMEM)] + [full(v) for v in operands],
        out_specs=tuple(full(v) for v in outs),
        compiler_params=pltpu.CompilerParams(vmem_limit_bytes=40 << 20),
        cost_estimate=LIGHT,
        name="norm_two",
    )(adapter, *map(HBM, operands))


def project_back_kernel(
    query_ref, kv_ref, came_ref, cos_ref, sin_ref, bq_ref, bkv_ref, low_ref, normed_ref, *outs
):
    grad_ref, grad_low_ref, tables_ref = outs
    width = query_ref.shape[1]
    kv_width = kv_ref.shape[1] // 2
    query = query_ref[...]
    grad_ref[:, :width] = query
    kv = kv_ref[...] + came_ref[...].astype(F32)
    for i in range(kv_ref.shape[1] // LANES):
        slab = kv[:, i * LANES : (i + 1) * LANES]
        if i < kv_width // LANES:
            slab = slab * cos_ref[...] - swap_halves(slab) * sin_ref[...]
        grad_ref[:, width + i * LANES : width + (i + 1) * LANES] = slab.astype(BF)
    kv = grad_ref[:, width:]
    grad_low = nt(kv, bkv_ref[...])
    first = lax.broadcasted_iota(jnp.int32, grad_low.shape, 1) < RANK
    table = jnp.concatenate([bq_ref[...], jnp.zeros((2 * RANK, width), BF)], 0)
    grad_low = jnp.where(first, nt(query, table), grad_low).astype(BF)
    grad_low_ref[...] = grad_low
    reduced = tn(grad_low, normed_ref[...]).astype(BF)
    for i in range(3):
        tables_ref[:, i * width : (i + 1) * width] = reduced[i * RANK : (i + 1) * RANK]
    low = low_ref[...]
    tables_ref[:, 3 * width : 4 * width] = tn(low, query)[:RANK].astype(BF)
    raised = tn(low, kv).astype(BF)
    tables_ref[:, 4 * width : 4 * width + kv_width] = raised[RANK : 2 * RANK, :kv_width]
    tables_ref[:, 4 * width + kv_width :] = raised[2 * RANK :, kv_width:]


def project_back_stage(grad_query, grad_kv, came, cosine, sine, b_query, b_kv, low, normed):
    rows, width = grad_query.shape
    kv = grad_kv.shape[1]
    operands = (grad_query, grad_kv, came, cosine, sine, b_query, b_kv, low, normed)
    outs = (
        jax.ShapeDtypeStruct((rows, width + kv), BF),
        jax.ShapeDtypeStruct(low.shape, BF),
        jax.ShapeDtypeStruct((RANK, 4 * width + kv), BF),
    )
    return pl.pallas_call(
        project_back_kernel,
        grid=(1,),
        out_shape=outs,
        in_specs=[full(v) for v in operands],
        out_specs=tuple(full(v) for v in outs),
        compiler_params=pltpu.CompilerParams(vmem_limit_bytes=32 << 20),
        cost_estimate=LIGHT,
        name="project_back",
    )(*map(HBM, operands))


def norm_one_kernel(grad_ref, w_ref, low_ref, a_ref, x_ref, gain_ref, mid_ref, out_ref, gain_grad_ref, held):
    step = pl.program_id(0)
    block = w_ref.shape[0]
    cols = pl.ds(pl.multiple_of(step * block, block), block)
    held[:, cols] = nt(grad_ref[...], w_ref[...]) + nn(low_ref[...], a_ref[...])

    @pl.when(step == pl.num_programs(0) - 1)
    def _():
        values = x_ref[...].astype(F32)
        scale = lax.rsqrt(jnp.mean(values * values, -1, keepdims=True) + EPS)
        gain_grad_ref[...] = jnp.sum(held[...] * values * scale, 0, keepdims=True)
        grad = held[...] * gain_ref[...]
        inner = jnp.mean(grad * values, -1, keepdims=True)
        out_ref[...] = mid_ref[...] + scale * grad - values * (scale * scale * scale * inner)


def norm_one_stage(grad, weights, low, table, x, gain, grad_middle):
    rows, inner = grad.shape
    width = weights.shape[0]
    block = width // 4
    whole = lambda v: pl.BlockSpec(v.shape, lambda i: (0, 0))
    return pl.pallas_call(
        norm_one_kernel,
        grid=(4,),
        out_shape=(
            jax.ShapeDtypeStruct((rows, width), F32),
            jax.ShapeDtypeStruct((1, width), F32),
        ),
        in_specs=[
            whole(grad),
            pl.BlockSpec((block, inner), lambda i: (i, 0)),
            whole(low),
            pl.BlockSpec((table.shape[0], block), lambda i: (0, i)),
            whole(x),
            whole(gain),
            whole(grad_middle),
        ],
        out_specs=(whole(grad_middle), whole(gain)),
        scratch_shapes=[pltpu.VMEM((rows, width), F32)],
        compiler_params=pltpu.CompilerParams(vmem_limit_bytes=32 << 20),
        cost_estimate=LIGHT,
        name="norm_one",
    )(*map(HBM, (grad, weights, low, table, x, gain, grad_middle)))


def head_pair(own_ref, other_ref, start, group):
    cols = pl.ds(pl.multiple_of(start + (group // 2) * LANES, LANES), LANES)
    slab = jnp.concatenate([own_ref[:, cols], other_ref[:, cols]], 0).astype(F32)
    lane = lax.broadcasted_iota(jnp.int32, slab.shape, 1)
    slab = jnp.where(group % 2 == 0, slab, pltpu.roll(slab, HEAD_DIM, 1))
    first = jnp.where(lane < HEAD_DIM, slab, 0.0)
    return first, pltpu.roll(first, HEAD_DIM, 1)


def attend_kernel(pos_ref, query_ref, own_ref, other_ref, out_ref, probs_ref):
    group = pl.program_id(0)
    rows = query_ref.shape[0]
    keys = [k.astype(BF) for k in head_pair(own_ref, other_ref, 0, group)]
    values = head_pair(own_ref, other_ref, KV_HEADS * HEAD_DIM, group)
    values = [v.T.astype(BF) for v in values]
    key_at = lax.broadcasted_iota(jnp.int32, (2 * rows, rows), 0)
    query_at = lax.broadcasted_iota(jnp.int32, (2 * rows, rows), 1)
    before = (pos_ref[1] < pos_ref[0]).astype(jnp.int32)
    visible = (key_at <= query_at) | ((key_at >= rows) & (before > 0))
    for j in range(query_ref.shape[1] // LANES):
        cols = pl.ds(j * LANES, LANES)
        query = query_ref[:, cols].astype(F32).T.astype(BF)
        mixed = 0.0
        for h in range(2):
            scores = jnp.where(visible, nn(keys[h], query), -1e30)
            weights = jnp.exp(scores - jnp.max(scores, 0, keepdims=True))
            probs = (weights * (1.0 / jnp.sum(weights, 0, keepdims=True))).astype(BF)
            probs_ref[0, 2 * j + h] = probs
            mixed += nn(values[h], probs)
        out_ref[:, cols] = mixed.T.astype(BF)


def attend_stage(blocks, query, own, other):
    rows, width = query.shape
    cols = width // KV_HEADS
    heads = HEADS // KV_HEADS
    tile = pl.BlockSpec((rows, cols), lambda i: (0, i))
    whole = pl.BlockSpec(own.shape, lambda i: (0, 0))
    return pl.pallas_call(
        attend_kernel,
        grid=(KV_HEADS,),
        out_shape=(
            jax.ShapeDtypeStruct((rows, width), BF),
            pltpu.HBM((KV_HEADS, heads, 2 * rows, rows), BF),
        ),
        in_specs=[pl.BlockSpec(memory_space=pltpu.SMEM), tile, whole, whole],
        out_specs=(tile, pl.BlockSpec((1, heads, 2 * rows, rows), lambda i: (i, 0, 0, 0))),
        compiler_params=pltpu.CompilerParams(vmem_limit_bytes=32 << 20),
        cost_estimate=LIGHT,
        name="attend",
    )(blocks, query, own, other)


def attend_back_kernel(
    grad_ref,
    out_ref,
    query_ref,
    own_ref,
    other_ref,
    probs_ref,
    cos_ref,
    sin_ref,
    gq_ref,
    gown_ref,
    gother_ref,
    gkv_ref,
):
    group = pl.program_id(0)
    keys = [k.T.astype(BF) for k in head_pair(own_ref, other_ref, 0, group)]
    values = head_pair(own_ref, other_ref, KV_HEADS * HEAD_DIM, group)
    values = [v.astype(BF) for v in values]
    cosine, sine = cos_ref[...], sin_ref[...]
    grad_keys, grad_values = [0.0, 0.0], [0.0, 0.0]
    for j in range(query_ref.shape[1] // LANES):
        cols = pl.ds(j * LANES, LANES)
        grad = grad_ref[:, cols]
        query = query_ref[:, cols]
        turned = grad.astype(F32).T
        product = turned * out_ref[:, cols].astype(F32).T
        turned = turned.astype(BF)
        grad_query = 0.0
        for h in range(2):
            inner = jnp.sum(product[h * HEAD_DIM : (h + 1) * HEAD_DIM], 0, keepdims=True)
            probs = probs_ref[0, 2 * j + h]
            grad_scores = (probs.astype(F32) * (nn(values[h], turned) - inner)).astype(BF)
            grad_values[h] += nn(probs, grad)
            grad_keys[h] += nn(grad_scores, query)
            grad_query += nn(keys[h], grad_scores)
        grad_query = grad_query.T * HEAD_DIM ** (-0.5)
        grad_query = grad_query * cosine - swap_halves(grad_query) * sine
        gq_ref[:, cols] = grad_query.astype(BF)

    @pl.when(group == 0)
    def _():
        gkv_ref[...] = jnp.zeros_like(gkv_ref)

    lane = lax.broadcasted_iota(jnp.int32, grad_keys[0].shape, 1)
    for start, (first, last) in ((0, grad_keys), (KV_HEADS * HEAD_DIM, grad_values)):
        total = jnp.where(lane < HEAD_DIM, first + pltpu.roll(last, HEAD_DIM, 1), 0.0)
        total = jnp.where(group % 2 == 0, total, pltpu.roll(total, HEAD_DIM, 1))
        cols = pl.ds(pl.multiple_of(start + (group // 2) * LANES, LANES), LANES)
        gkv_ref[:, cols] += total

    @pl.when(group == pl.num_programs(0) - 1)
    def _():
        rows = gown_ref.shape[0]
        gown_ref[...] = gkv_ref[pl.ds(0, rows), :]
        gother_ref[...] = gkv_ref[pl.ds(rows, rows), :].astype(BF)


def attend_back_stage(grad, out, query, own, other, probs, cosine, sine):
    rows, width = query.shape
    cols = width // KV_HEADS
    tile = pl.BlockSpec((rows, cols), lambda i: (0, i))
    whole = pl.BlockSpec(own.shape, lambda i: (0, 0))
    table = pl.BlockSpec((rows, LANES), lambda i: (0, 0))
    return pl.pallas_call(
        attend_back_kernel,
        grid=(KV_HEADS,),
        out_shape=(
            jax.ShapeDtypeStruct((rows, width), BF),
            jax.ShapeDtypeStruct(own.shape, F32),
            jax.ShapeDtypeStruct(own.shape, BF),
        ),
        scratch_shapes=[pltpu.VMEM((2 * rows, own.shape[1]), F32)],
        in_specs=[tile, tile, tile, whole, whole]
        + [pl.BlockSpec((1,) + probs.shape[1:], lambda i: (i, 0, 0, 0)), table, table],
        out_specs=(tile, whole, whole),
        compiler_params=pltpu.CompilerParams(vmem_limit_bytes=32 << 20),
        cost_estimate=LIGHT,
        name="attend_back",
    )(grad, out, query, own, other, probs, cosine, sine)


def send_columns(parts, n):
    whole = jnp.concatenate(parts, 1).astype(BF)
    whole = jnp.pad(whole, ((0, 0), (0, -whole.shape[1] % n)))
    return jnp.moveaxis(whole.reshape(RANK, n, -1), 1, 0)


def sum_columns(parts, ids, own_rows):
    n, _, chunk = parts.shape
    onehot = (ids[:, None] == jnp.arange(ADAPTERS, dtype=jnp.int32)[None, :]).astype(BF)
    summed = jnp.einsum("na,nrc->arc", onehot, parts, preferred_element_type=F32)
    return summed.reshape(n, own_rows, chunk)


def per_device(
    n,
    inputs,
    cotangent,
    adapter_ids,
    block_index,
    gain_first,
    gain_second,
    w_query,
    w_key,
    w_value,
    w_output,
    w_gate_up,
    w_down,
    reduce_attention,
    raise_query,
    raise_keyvalue,
    reduce_output,
    raise_output,
    reduce_gate_up,
    raise_gate_up,
    reduce_down,
    raise_down,
):
    width = inputs.shape[-1]
    rows = inputs.shape[-2]
    shard = w_down.shape[0]
    own_rows = raise_down.shape[0]
    gains = gain_first.shape[0]
    kv_width = KV_HEADS * HEAD_DIM
    side = lax.axis_index("seq")
    me = lax.axis_index(ALL).astype(jnp.int32)
    tokens = inputs.reshape(rows, width)
    grad_out = cotangent.reshape(rows, width)

    order = Order()
    qkv_width = width + 2 * kv_width
    att_rows = Outer(jnp.concatenate([w_query, w_key, w_value, w_output], 1), n)
    att_rows.step()
    cot_plane = Plane(grad_out, n)
    padded = -(-shard // 16) * 16
    slot = -(-(n // 8) * padded // 256) * 256 // (n // 8)
    feed = jnp.stack([w_gate_up[0].T, w_gate_up[1].T, w_down])

    table_width = 10 * width
    chunk = table_width // n
    table = jnp.concatenate(
        [reduce_attention[0], reduce_attention[1], reduce_attention[2], raise_query]
        + [reduce_output, raise_output, reduce_gate_up[0], reduce_gate_up[1], raise_down]
        + [raise_keyvalue[0], raise_keyvalue[1]],
        1,
    )
    table = jnp.pad(table, ((0, 0), (0, table_width - table.shape[1])))
    table = jnp.moveaxis(table.reshape(own_rows, n, chunk), 1, 0)
    hidden_table = jnp.stack([raise_gate_up[0], raise_gate_up[1], reduce_down])
    hidden_table = hidden_table.reshape(3, own_rows, n, shard).transpose(2, 1, 0, 3)
    hidden_table = hidden_table.reshape(n, own_rows, 3 * shard)
    small = jnp.concatenate([gain_first, gain_second, adapter_ids.astype(BF)])
    used = chunk + 3 * shard
    sent = -(-(used + small.shape[0]) // 128) * 128
    small = jnp.pad(small, (0, sent - used - small.shape[0]))
    small = jnp.broadcast_to(small, (n, own_rows, small.shape[0]))
    table = jnp.concatenate([table, hidden_table, small], -1)
    came = lax.all_to_all(table, ALL, 0, 0, tiled=True)
    cot_plane.near = att_rows.pass_through(order, *cot_plane.near)
    att_rows.step_all()
    gain_one = came[:, 0, used : used + gains].reshape(width).astype(F32)
    gain_two = came[:, 0, used + gains : used + 2 * gains].reshape(width).astype(F32)
    ids = came[:, 0, used + 2 * gains].astype(jnp.int32)
    columns = came[:, :, :chunk].reshape(ADAPTERS, RANK, chunk)
    hidden_cols = came[:, :, chunk:used].reshape(TABLE, 3, shard)
    own = lax.all_to_all(jnp.take(columns, ids, axis=0), ALL, 0, 0, tiled=True)
    feed = jnp.concatenate([feed, hidden_cols.transpose(1, 2, 0)], 2)
    feed = jnp.pad(feed, ((0, 0), (0, padded - shard), (0, 0))).reshape(3 * padded, -1)
    (feed,) = att_rows.pass_through(order, feed)
    feed = lax.all_gather(feed, "outer", axis=0, tiled=True)
    qkv_rows = Rows([part[:, :qkv_width] for part in att_rows.parts()], n)
    qkv_rows.start_plane()
    qkv_rows.near = order.point(*qkv_rows.near)
    qkv_rows.end_plane()
    own = jnp.moveaxis(own, 0, 1).reshape(RANK, table_width)
    (a_query, a_key, a_value, b_query, a_out, b_out, a_gate, a_up, b_down) = [
        own[:, i * width : (i + 1) * width] for i in range(9)
    ]
    b_key = own[:, 9 * width : 9 * width + kv_width]
    b_value = own[:, 9 * width + kv_width : 9 * width + 2 * kv_width]

    own_block = lax.dynamic_index_in_dim(block_index[0], side, 0, keepdims=False)
    other_block = lax.dynamic_index_in_dim(block_index[0], 1 - side, 0, keepdims=False)
    blocks = jnp.stack([own_block, other_block])
    cosine, sine = rotary_tables(own_block * rows + jnp.arange(rows, dtype=jnp.int32))
    a_att = jnp.concatenate([a_query, a_key, a_value], 0)
    a_two = jnp.concatenate([a_gate, a_up], 0)
    b_kv = jnp.concatenate(
        [
            jnp.zeros((RANK, 2 * kv_width), BF),
            jnp.pad(b_key, ((0, 0), (0, kv_width))),
            jnp.pad(b_value, ((0, 0), (kv_width, 0))),
        ],
        0,
    )
    grad_low_down = nt(grad_out, b_down).astype(BF)
    plane_ids = jnp.stack([ids[me], ids[me ^ C], ids[me ^ Y], ids[me ^ (Y | C)]])
    out_rows = Rows([part[:, qkv_width:] for part in att_rows.parts()], n)
    passed = order.point(
        *qkv_rows.last, a_att, a_two, b_kv, cosine, sine, grad_low_down, plane_ids, out_rows.whole
    )
    qkv_rows.last = passed[:2]
    a_att, a_two, b_kv, cosine, sine, grad_low_down, plane_ids, out_rows.whole = passed[2:]
    out_rows.start_plane()
    normed_one, low_att, key_value, w_qkv = project_stage(
        me, tokens, gain_one[None], a_att, b_kv, cosine, sine, qkv_rows.pieces(), n
    )
    low_query, low_key, low_value = [low_att[:, i * RANK : (i + 1) * RANK] for i in range(3)]
    key_value = order.point(key_value)
    other_kv = exchange(key_value, X, n)
    query = query_stage(normed_one, low_att, b_query, w_qkv, cosine, sine)
    key_value, other_kv, query = order.point(key_value, other_kv, query)
    attended, probs = attend_stage(blocks, query, key_value, other_kv)
    attended, *out_rows.near = order.point(attended, *out_rows.near)
    out_rows.end_plane()
    attended, *out_rows.last = order.point(attended, *out_rows.last)
    cot_plane.end()
    middle, normed_two, low_out, normed_ext, w_out = output_stage(
        me,
        attended,
        a_out,
        b_out,
        tokens,
        gain_two[None],
        a_two,
        grad_low_down,
        out_rows.pieces(),
        n,
    )

    normed_ext, *cot_plane.last = order.point(normed_ext, *cot_plane.last)
    cot_plane.finish()
    normed_plane = Plane(normed_ext, n)
    normed_plane.near = order.point(*normed_plane.near)
    normed_plane.end()
    passed = order.point(
        *normed_plane.last, *normed_plane.far, *cot_plane.far, *cot_plane.last_far
    )
    normed_plane.last, normed_plane.far = passed[:2], passed[2:4]
    cot_plane.far, cot_plane.last_far = passed[4:6], passed[6:]
    normed_plane.finish()
    feed_of = lambda ids_here, place, groups: feed_stage(
        ids_here,
        place,
        len(groups),
        feed,
        normed_plane.group(*groups),
        cot_plane.group(*groups),
        padded,
        slot,
    )
    hidden_far, grads_far, near_out, far_out = feed_of(plane_ids, 2, (3,))
    normed_sum = PlaneSum(n)
    normed_sum.put(3, near_out, exchange(far_out, C, n))
    ids_mid, near_out = order.point(plane_ids, near_out)
    hidden_mid, grads_mid, near_out, far_out = feed_of(ids_mid, 0, (1, 2))
    far_sends = normed_sum.far_sends()
    near_out, far_out, *far_sends = order.point(near_out, far_out, *far_sends)
    far_came = normed_sum.hop(*far_sends)
    mid_recv = exchange(far_out, C, n)
    for j in range(2):
        part = slice(j * rows, (j + 1) * rows)
        normed_sum.put(j + 1, near_out[part], mid_recv[part])
    ids_own, *near_sends = order.point(plane_ids, *normed_sum.near_sends())
    near_came = normed_sum.hop(*near_sends)
    hidden_own, grads_own, near_out, far_out = feed_of(ids_own, 0, (0,))
    recv = exchange(far_out, C, n)
    near_out, grads_own, *came = order.point(near_out, grads_own, *far_came, *near_came)
    far_came, near_came = came[:2], came[2:]
    hidden_grads = grads_own + grads_mid + grads_far
    hidden_grads = jnp.concatenate([hidden_grads[i] for i in range(3)], 1).astype(BF)
    hidden_grads = hidden_grads.reshape(n, own_rows, -1)
    last_sends = order.point(*normed_sum.last_sends(*far_came))
    last_came = normed_sum.last_hop(*last_sends)
    hidden_own, hidden_grads = order.point(hidden_own, hidden_grads)
    hidden_grads = lax.all_to_all(hidden_grads, ALL, 0, 0, tiled=True)
    down_near, down_far = down_stage(
        [hidden_own, hidden_mid, hidden_far], feed, n // 8, padded, slot, rows
    )
    parts = order.point(recv, *near_came, *last_came, down_far)
    down_far = parts[5]
    parts = (near_out, *parts[:5])

    grad_middle, grad_one, grad_low_out, low_down, gain_grad_two, early = norm_two_stage(
        adapter_ids, parts, middle, gain_two[None], grad_out, attended, low_out, normed_two, a_two, b_out
    )
    down_recv = exchange(down_far, C, n)
    grad_attended = back_stage(grad_one, w_out, grad_low_out, a_out, BF)
    down_sum = PlaneSum(n)
    for i in range(4):
        part = slice(i * rows, (i + 1) * rows)
        down_sum.put(i, down_near[part], down_recv[part])
    grad_query, grad_kv, kv_away = attend_back_stage(
        grad_attended, attended, query, key_value, other_kv, probs, cosine, sine
    )
    grad_query, grad_kv, kv_away, hidden_grads = order.point(
        grad_query, grad_kv, kv_away, hidden_grads
    )
    kv_came, *sends = order.point(
        exchange(kv_away, X, n), *down_sum.far_sends(), *down_sum.near_sends()
    )
    down_far = down_sum.hop(*sends[:2])
    grad_qkv, grad_low_att, late = project_back_stage(
        grad_query, grad_kv, kv_came, cosine, sine, b_query, b_kv, low_att, normed_one
    )

    late, grad_qkv = order.point(send_columns([late, early], n), grad_qkv)
    late = lax.all_to_all(late, ALL, 0, 0, tiled=True)
    down_near = down_sum.hop(*sends[2:])
    input_grad, gain_grad_one = norm_one_stage(
        grad_qkv, w_qkv, grad_low_att, a_att, tokens, gain_one[None], grad_middle
    )
    input_grad = input_grad.reshape(inputs.shape)
    gain_grads = jnp.concatenate(
        [gain_grad_one.reshape(n, gains), gain_grad_two.reshape(n, gains)], 1
    )
    gain_grads = jnp.broadcast_to(gain_grads[:, None], (n, own_rows, 2 * gains))
    input_grad, gain_grads, *down_far = order.point(input_grad, gain_grads, *down_far)
    down_last = down_sum.last_hop(*down_sum.last_sends(*down_far))
    late = jnp.concatenate([sum_columns(late, ids, own_rows), gain_grads], -1)
    late, hidden_grads, down_sum.mine[0] = order.point(late, hidden_grads, down_sum.mine[0])
    late = lax.all_to_all(late, ALL, 0, 0, tiled=True)
    branch_two = down_sum.total(down_near, down_last)
    output = (middle + branch_two + nn(low_down, b_down)).astype(BF)
    hidden_grads = hidden_grads.reshape(n // 8, 8, own_rows, 3, n // 8, slot)
    hidden_grads = jnp.sum(hidden_grads[..., :shard].astype(F32), 0)
    hidden_grads = hidden_grads.transpose(2, 1, 3, 0, 4).reshape(3, own_rows, -1)
    gain_grads = jnp.sum(late[:, 0, -2 * gains :], 0) + order.token
    late_rows = jnp.moveaxis(late[:, :, : -2 * gains], 0, 1).reshape(own_rows, -1)
    parts = [late_rows[:, i * width : (i + 1) * width] for i in range(4)]
    kv = late_rows[:, 4 * width : 4 * width + 2 * kv_width]
    start = 4 * width + 2 * kv_width
    parts += [late_rows[:, start + i * width : start + (i + 1) * width] for i in range(5)]
    return (
        output.reshape(inputs.shape),
        input_grad,
        gain_grads[:gains],
        gain_grads[gains:],
        jnp.stack(parts[:3]),
        parts[3],
        jnp.stack([kv[:, :kv_width], kv[:, kv_width:]]),
        parts[4],
        parts[5],
        jnp.stack(parts[6:8]),
        hidden_grads[:2],
        hidden_grads[2],
        parts[8],
    )


def solution(mesh):
    dp, seq = mesh.shape["dp"], mesh.shape["seq"]
    n = dp * seq
    dp_axes = ALL[:2]
    rows = P(ALL, None)
    stacked = P(None, ALL, None)
    vector = P(ALL)
    blocks = P(dp_axes, "seq", None, None)
    return jax.shard_map(
        functools.partial(per_device, n),
        mesh=Mesh(mesh.devices.reshape(dp // 4, 4, seq), ALL),
        in_specs=(
            (blocks, blocks, P(dp_axes), P(dp_axes, None), vector, vector)
            + (rows, rows, rows, rows, P(None, None, ALL), rows)
            + (stacked, rows, stacked, rows, rows, stacked, stacked, rows, rows)
        ),
        out_specs=(
            (blocks, blocks, vector, vector, stacked, rows, stacked, rows, rows)
            + (stacked, stacked, rows, rows)
        ),
        check_vma=False,
    )
```

```python
import functools

import jax
import jax.numpy as jnp
from jax import lax
from jax.experimental import pallas as pl
from jax.experimental.pallas import tpu as pltpu
from jax.sharding import Mesh
from jax.sharding import PartitionSpec as P

HEADS = 32
KV_HEADS = 4
HEAD_DIM = 64
ADAPTERS = 8
RANK = 16
TABLE = ADAPTERS * RANK

EPS = 1e-05
THETA = 10000.0

ALL = ("outer", "pair", "seq")
X, C, Y = 1, 2, 4
BF = jnp.bfloat16
F32 = jnp.float32
HBM = lambda value: pltpu.with_memory_space_constraint(value, pltpu.HBM)
LIGHT = pl.CostEstimate(flops=1 << 20, bytes_accessed=1 << 16, transcendentals=0)


def dot(a, b, dims):
    return lax.dot_general(a, b, (dims, ((), ())), preferred_element_type=F32)


def nn(a, b):
    return dot(a, b, ((1,), (0,)))


def nt(a, b):
    return dot(a, b, ((1,), (1,)))


def tn(a, b):
    return dot(a, b, ((0,), (0,)))


def exchange(value, mask, n):
    return lax.ppermute(value, ALL, [(i, i ^ mask) for i in range(n)])


def rotary_tables(positions):
    half = HEAD_DIM // 2
    speeds = THETA ** (-jnp.arange(half, dtype=F32) * (2.0 / HEAD_DIM))
    angles = positions.astype(F32)[:, None] * speeds
    cosine, sine = jnp.cos(angles), jnp.sin(angles)
    return jnp.tile(cosine, (1, 4)), jnp.tile(jnp.concatenate([-sine, sine], 1), (1, 2))


def outer_bits(n):
    bits, bit = [], 8
    while bit < n:
        bits.append(bit)
        bit *= 2
    return bits


class Outer:
    def __init__(self, value, n):
        self.n = n
        self.held = {0: value}
        self.offsets = sorted(range(8, n, 8), key=lambda offset: (bin(offset).count("1"), -offset))

    def step(self):
        if not self.offsets:
            return False
        level = bin(self.offsets[0]).count("1")
        while self.offsets and bin(self.offsets[0]).count("1") == level:
            offset = self.offsets.pop(0)
            low = offset & -offset
            self.held[offset] = exchange(self.held[offset ^ low], low, self.n)
        return bool(self.offsets)

    def step_all(self):
        while self.step():
            pass

    def pass_through(self, order, *others):
        keys = sorted(self.held)
        passed = order.point(*[self.held[k] for k in keys], *others)
        self.held = dict(zip(keys, passed))
        return passed[len(keys) :]

    def parts(self):
        return [self.held[offset] for offset in sorted(self.held)]


def place_copies(me, pieces, held, sems):
    z, y, c, x = me // 8, (me // 4) % 2, (me // 2) % 2, me % 2
    copies = []
    for i, piece in enumerate(pieces):
        dc, kind = i // 5, i % 5
        dy, dx = ((0, 0), (0, 1), (1, 0), (1, 1), (1, 1))[kind]
        first = piece.shape[0] if kind == 4 else 0
        for j in range(piece.shape[0]):
            dz = first + j
            block = (((z ^ dz) * 2 + (y ^ dy)) * 2 + (c ^ dc)) * 2 + (x ^ dx)
            rows = pl.ds(pl.multiple_of(block * piece.shape[1], piece.shape[1]), piece.shape[1])
            copies.append(
                pltpu.make_async_copy(piece.at[j], held.at[rows], sems.at[len(copies)])
            )
    return copies


def normed_of(values, gain):
    scale = lax.rsqrt(jnp.mean(values * values, -1, keepdims=True) + EPS)
    return (values * scale * gain).astype(BF)


class Outer:
    def __init__(self, value, n):
        self.n = n
        self.held = {0: value}
        self.offsets = sorted(range(8, n, 8), key=lambda offset: (bin(offset).count("1"), -offset))

    def step(self):
        if not self.offsets:
            return False
        level = bin(self.offsets[0]).count("1")
        while self.offsets and bin(self.offsets[0]).count("1") == level:
            offset = self.offsets.pop(0)
            low = offset & -offset
            self.held[offset] = exchange(self.held[offset ^ low], low, self.n)
        return bool(self.offsets)

    def step_all(self):
        while self.step():
            pass

    def pass_through(self, order, *others):
        keys = sorted(self.held)
        passed = order.point(*[self.held[k] for k in keys], *others)
        self.held = dict(zip(keys, passed))
        return passed[len(keys) :]

    def parts(self):
        return [self.held[offset] for offset in sorted(self.held)]


def sum_outer(parts, n):
    held = {8 * i: part for i, part in enumerate(parts)}
    for bit in outer_bits(n):
        for offset in sorted(held):
            if offset & bit:
                held[offset ^ bit] = held[offset ^ bit] + exchange(held.pop(offset), bit, n)
    return held[0]


def place_kernel(count, outer, width, me_ref, *refs):
    pieces, out, held, sems, last = refs[:count], *refs[count:]
    me = me_ref[0]
    z, y, c, x = me // 8, (me // 4) % 2, (me // 2) % 2, me % 2
    copies = []
    for i in range(count):
        part, dc, dy, dx = i // 8, (i // 4) % 2, (i // 2) % 2, i % 2
        for dz in range(outer):
            block = (((z ^ dz) * 2 + (y ^ dy)) * 2 + (c ^ dc)) * 2 + (x ^ dx)
            copies.append(
                pltpu.make_async_copy(
                    pieces[i].at[dz],
                    held.at[block, :, pl.ds(part * width, width)],
                    sems.at[len(copies)],
                )
            )
    for copy in copies:
        copy.start()
    for copy in copies:
        copy.wait()
    copy = pltpu.make_async_copy(held, out, last)
    copy.start()
    copy.wait()


class Rows:
    def __init__(self, parts, n):
        self.n = n
        self.whole = jnp.stack(parts)

    def start_plane(self):
        self.near = [exchange(self.whole, bit, self.n) for bit in (X, Y, C)]

    def end_plane(self):
        from_x, from_y, _ = self.near
        half = from_x.shape[0] // 2
        self.last = [
            exchange(from_x[:half], Y, self.n),
            exchange(from_y[half:], X, self.n),
        ]
        self.far = [exchange(v, C, self.n) for v in (from_x, from_y)]

    def pieces(self):
        last_far = [exchange(v, C, self.n) for v in self.last]
        from_x, from_y, other = self.near
        return [self.whole, from_x, from_y, *self.last, other, *self.far, *last_far]


class Plane:
    def __init__(self, value, n):
        self.n = n
        self.own = value
        self.near = [exchange(value, X, n), exchange(value, Y, n), exchange(value, C, n)]

    def end(self):
        from_x, from_y, _ = self.near
        half = from_x.shape[0] // 2
        self.last = [exchange(from_x[:half], Y, self.n), exchange(from_y[half:], X, self.n)]
        self.far = [exchange(v, C, self.n) for v in (from_x, from_y)]

    def finish(self):
        self.last_far = [exchange(v, C, self.n) for v in self.last]

    def group(self, *which):
        parts = []
        for g in which:
            if g == 3:
                parts += [*self.last, *self.last_far]
            else:
                parts += [self.near[g - 1], self.far[g - 1]] if g else [self.own, self.near[2]]
        return parts


class Order:
    def __init__(self):
        self.token = jnp.zeros((), F32)

    def point(self, *values):
        *values, self.token = lax.optimization_barrier((*values, self.token))
        return values[0] if len(values) == 1 else values


def half_of(block, part):
    half = block.shape[0] // 2
    return block[part * half : (part + 1) * half].astype(F32)


class PlaneSum:
    def __init__(self, n):
        self.n = n
        self.mine, self.recv = {}, {}

    def put(self, block, near, recv):
        self.mine[block], self.recv[block] = near, recv

    def held(self, block, part):
        return half_of(self.mine[block], part) + half_of(self.recv[block], part)

    def far_sends(self):
        return self.held(3, 0).astype(BF), self.held(3, 1).astype(BF)

    def near_sends(self):
        return self.held(1, 0).astype(BF), self.held(2, 1).astype(BF)

    def last_sends(self, first, second):
        return (
            (self.held(2, 0) + first.astype(F32)).astype(BF),
            (self.held(1, 1) + second.astype(F32)).astype(BF),
        )

    def hop(self, first, second):
        return exchange(first, X, self.n), exchange(second, Y, self.n)

    def last_hop(self, first, second):
        return exchange(first, Y, self.n), exchange(second, X, self.n)

    def total(self, near, last):
        return jnp.concatenate(
            [self.held(0, i) + near[i].astype(F32) + last[i].astype(F32) for i in range(2)], 0
        )


def full(value):
    shape = value.shape
    return pl.BlockSpec(shape, lambda i: (0,) * len(shape), pipeline_mode=pl.Buffered(1))


def copies_of(pieces, target, stride, sems):
    copies, row = [], 0
    for i, piece in enumerate(pieces):
        size = piece.shape[0]
        copies.append(pltpu.make_async_copy(piece, target.at[pl.ds(row, size)], sems.at[i]))
        row += stride or size
    return copies


def clear_spare(target, used, slot):
    if slot > used:
        for row in range(0, target.shape[0], slot):
            target[pl.ds(row + used, slot - used), :] = jnp.zeros(
                (slot - used, target.shape[1]), target.dtype
            )


def lift_of(adapter):
    row = lax.broadcasted_iota(jnp.int32, (TABLE, 3 * TABLE), 0)
    col = lax.broadcasted_iota(jnp.int32, (TABLE, 3 * TABLE), 1)
    goal = (row // RANK) * TABLE + adapter * RANK + row % RANK
    return ((col == goal) & (row < 3 * RANK)).astype(F32).astype(BF)


def feed_copies(feed, kind, padded, slot, target, first, columns, sems):
    start, size, to = columns
    return [
        pltpu.make_async_copy(
            feed.at[pl.ds((3 * i + kind) * padded, padded), pl.ds(start, size)],
            target.at[pl.ds(first + i * slot, padded), pl.ds(to, size)],
            sems.at[i],
        )
        for i in range(sems.shape[0])
    ]


def feed_kernel(sizes, ids_ref, feed_ref, *refs):
    parts, padded, slot, width, place = sizes
    normed_in, cot_in, refs = refs[:parts], refs[parts : 2 * parts], refs[2 * parts :]
    hidden_ref, grads_ref, near_ref, far_ref, refs = *refs[:4], refs[4:]
    w_both, w_down, normed_all, cot_all, both_all, grad_all, acts, *sems = refs
    group = pl.program_id(0)
    block, cols = hidden_ref.shape
    half = block // 2
    wide = width + TABLE
    loads = [
        copies_of(normed_in, normed_all.at[:, pl.ds(0, wide)], None, sems[0]),
        feed_copies(feed_ref, 0, padded, slot, w_both, 0, (0, wide, 0), sems[1]),
        feed_copies(feed_ref, 1, padded, slot, w_both, cols, (0, width, 0), sems[2])
        + feed_copies(feed_ref, 1, padded, slot, w_both, cols, (width, TABLE, wide), sems[3]),
        copies_of(cot_in, cot_all.at[:, pl.ds(0, width)], None, sems[4]),
        feed_copies(feed_ref, 2, padded, slot, w_down, 0, (0, wide, 0), sems[5]),
    ]

    def arrive(*which):
        @pl.when(group == 0)
        def _():
            for i in which:
                for copy in loads[i]:
                    copy.wait()

    @pl.when(group == 0)
    def _():
        for load in loads:
            for copy in load:
                copy.start()
        grads_ref[...] = jnp.zeros_like(grads_ref)
        zeros = jnp.zeros((cols, TABLE), BF)
        w_both[pl.ds(0, cols), wide:] = zeros
        w_both[pl.ds(cols, cols), width:wide] = zeros
        clear_spare(w_both, padded, slot)
        clear_spare(w_down, padded, slot)

    row = pl.multiple_of(group * block, block)
    own = pl.ds(row, block)
    arrive(0)
    for i in range(2):
        here = pl.ds(row + i * half, half)
        lows = nn(normed_all[here, width:wide], lift_of(ids_ref[place + 2 * group + i])).astype(BF)
        normed_all[here, width:] = lows[:, : 2 * TABLE]
        cot_all[here, width:] = lows[:, 2 * TABLE :]
    arrive(1, 2)
    both_all[...] = nt(normed_all[own, :], w_both[...])
    arrive(3, 4)
    grad_all[...] = nt(cot_all[own, :], w_down[...])
    step = 16

    def rows_of(i, carry):
        here = pl.ds(pl.multiple_of(i * step, step), step)
        gate, up, grad = both_all[here, :cols], both_all[here, cols:], grad_all[here, :]
        sigmoid = 0.5 * jnp.tanh(0.5 * gate) + 0.5
        silu = gate * sigmoid
        hidden_ref[here, :] = (silu * up).astype(BF)
        acts[here, :cols] = (grad * up * (sigmoid + silu * (1.0 - sigmoid))).astype(BF)
        acts[here, cols:] = (grad * silu).astype(BF)
        return carry

    lax.fori_loop(0, block // step, rows_of, 0)
    out = nn(acts[...], w_both[...]).astype(BF)
    low = nn(hidden_ref[...], w_down[:, width:]).astype(BF)
    for i, ref in enumerate((near_ref, far_ref)):
        ref[:, : wide + TABLE] = out[i * half : (i + 1) * half]
        ref[:, wide + TABLE :] = low[i * half : (i + 1) * half]
    grads_ref[0] += tn(normed_all[own, width:wide], acts[:, :cols])
    grads_ref[1] += tn(normed_all[own, wide:], acts[:, cols:])
    grads_ref[2] += tn(cot_all[own, width:], hidden_ref[...])


def feed_stage(ids, place, groups, feed, normed, cot, padded, slot):
    wide, width = normed[0].shape[1], cot[0].shape[1]
    tokens = sum(part.shape[0] for part in normed)
    block = tokens // groups
    pieces = feed.shape[0] // (3 * padded)
    cols = pieces * slot
    tile = pl.BlockSpec((block, cols), lambda i: (i, 0))
    anywhere = pl.BlockSpec(memory_space=pl.ANY)
    out = jax.ShapeDtypeStruct((tokens // 2, wide + 2 * TABLE), BF)
    out_tile = pl.BlockSpec((block // 2, wide + 2 * TABLE), lambda i: (i, 0))
    counts = (len(normed),) + (pieces,) * 3 + (len(cot), pieces)
    return pl.pallas_call(
        functools.partial(feed_kernel, (len(normed), padded, slot, width, place)),
        grid=(groups,),
        out_shape=(
            jax.ShapeDtypeStruct((tokens, cols), BF),
            jax.ShapeDtypeStruct((3, TABLE, cols), F32),
            out,
            out,
        ),
        in_specs=[pl.BlockSpec(memory_space=pltpu.SMEM)]
        + [anywhere] * (1 + len(normed) + len(cot)),
        out_specs=(
            tile,
            pl.BlockSpec((3, TABLE, cols), lambda i: (0, 0, 0)),
            out_tile,
            out_tile,
        ),
        scratch_shapes=[
            pltpu.VMEM((2 * cols, wide + TABLE), BF),
            pltpu.VMEM((cols, wide), BF),
            pltpu.VMEM((tokens, wide + TABLE), BF),
            pltpu.VMEM((tokens, wide), BF),
            pltpu.VMEM((block, 2 * cols), F32),
            pltpu.VMEM((block, cols), F32),
            pltpu.VMEM((block, 2 * cols), BF),
        ]
        + [pltpu.SemaphoreType.DMA((count,)) for count in counts],
        compiler_params=pltpu.CompilerParams(vmem_limit_bytes=44 << 20),
        cost_estimate=LIGHT,
        name="feed",
    )(ids, HBM(feed), *map(HBM, normed), *map(HBM, cot))


def down_kernel(padded, slot, *refs):
    *acts, feed_ref, near_ref, far_ref, w_down, sems = refs
    loads = feed_copies(feed_ref, 2, padded, slot, w_down, 0, (0, w_down.shape[1], 0), sems)
    for copy in loads:
        copy.start()
    clear_spare(w_down, padded, slot)
    for copy in loads:
        copy.wait()
    rows = near_ref.shape[0] // 4
    done = 0
    for act in acts:
        for i in range(act.shape[0] // (2 * rows)):
            out = nn(act[pl.ds(i * 2 * rows, 2 * rows), :], w_down[...]).astype(BF)
            near_ref[pl.ds(done, rows), :] = out[:rows]
            far_ref[pl.ds(done, rows), :] = out[rows:]
            done += rows


def down_stage(hiddens, feed, pieces, padded, slot, rows):
    width = feed.shape[1] - TABLE
    out = jax.ShapeDtypeStruct((4 * rows, width), BF)
    return pl.pallas_call(
        functools.partial(down_kernel, padded, slot),
        grid=(1,),
        out_shape=(out, out),
        in_specs=[full(v) for v in hiddens] + [pl.BlockSpec(memory_space=pl.ANY)],
        out_specs=(full(out), full(out)),
        scratch_shapes=[
            pltpu.VMEM((pieces * slot, width), BF),
            pltpu.SemaphoreType.DMA((pieces,)),
        ],
        compiler_params=pltpu.CompilerParams(vmem_limit_bytes=32 << 20),
        cost_estimate=LIGHT,
        name="down",
    )(*map(HBM, hiddens), HBM(feed))


LANES = 2 * HEAD_DIM


def swap_halves(values):
    lane = lax.broadcasted_iota(jnp.int32, values.shape, 1) % HEAD_DIM
    half = HEAD_DIM // 2
    left = pltpu.roll(values, LANES - half, 1)
    return jnp.where(lane < half, left, pltpu.roll(values, half, 1))


def rope(slab, cosine, sine):
    return slab * cosine + swap_halves(slab) * sine


def project_kernel(
    me_ref, x_ref, gain_ref, a_ref, b_ref, cos_ref, sin_ref, *refs
):
    *pieces, normed_ref, low_ref, kv_ref, w_ref, held, sems, last = refs
    copies = place_copies(me_ref[0], pieces, held, sems)
    for copy in copies:
        copy.start()
    normed = normed_of(x_ref[...].astype(F32), gain_ref[...])
    normed_ref[...] = normed
    low = nt(normed, a_ref[...]).astype(BF)
    low_ref[...] = low
    for copy in copies:
        copy.wait()
    copy = pltpu.make_async_copy(held, w_ref, last)
    copy.start()
    width = kv_ref.shape[1]
    kv = nn(normed, held[:, held.shape[1] - width :]) + nn(low, b_ref[...])
    for i in range(width // LANES):
        cols = slice(i * LANES, (i + 1) * LANES)
        slab = kv[:, cols]
        if i < width // LANES // 2:
            slab = rope(slab, cos_ref[...], sin_ref[...])
        kv_ref[:, cols] = slab.astype(BF)
    copy.wait()


def project_stage(me, x, gain, a_att, b_kv, cosine, sine, pieces, n):
    rows, width = x.shape
    outer, shard, columns = pieces[0].shape
    anywhere = pl.BlockSpec(memory_space=pl.ANY)
    outs = (
        jax.ShapeDtypeStruct((rows, width), BF),
        jax.ShapeDtypeStruct((rows, a_att.shape[0]), BF),
        jax.ShapeDtypeStruct((rows, b_kv.shape[1]), BF),
    )
    operands = (x, gain, a_att, b_kv, cosine, sine)
    normed, low, kv, weights = pl.pallas_call(
        project_kernel,
        grid=(1,),
        out_shape=(*outs, pltpu.HBM((n * shard, columns), BF)),
        in_specs=[pl.BlockSpec(memory_space=pltpu.SMEM)]
        + [full(v) for v in operands]
        + [anywhere] * len(pieces),
        out_specs=(*[full(v) for v in outs], anywhere),
        scratch_shapes=[
            pltpu.VMEM((n * shard, columns), BF),
            pltpu.SemaphoreType.DMA((n,)),
            pltpu.SemaphoreType.DMA(()),
        ],
        compiler_params=pltpu.CompilerParams(vmem_limit_bytes=28 << 20),
        cost_estimate=LIGHT,
        name="project",
    )(me.reshape(1), *map(HBM, operands), *map(HBM, pieces))
    return normed, low, kv, weights


def query_kernel(normed_ref, low_ref, b_ref, w_ref, cos_ref, sin_ref, out_ref):
    query = nn(normed_ref[...], w_ref[...]) + nn(low_ref[:, :RANK], b_ref[...])
    for i in range(out_ref.shape[1] // LANES):
        cols = slice(i * LANES, (i + 1) * LANES)
        slab = rope(query[:, cols], cos_ref[...], sin_ref[...]) * HEAD_DIM ** (-0.5)
        out_ref[:, cols] = slab.astype(BF)


def query_stage(normed, low, b_query, weights, cosine, sine):
    rows, width = normed.shape
    block = width // 4
    whole = lambda v: pl.BlockSpec(v.shape, lambda i: (0, 0))
    return pl.pallas_call(
        query_kernel,
        grid=(4,),
        out_shape=jax.ShapeDtypeStruct((rows, width), BF),
        in_specs=[
            whole(normed),
            whole(low),
            pl.BlockSpec((RANK, block), lambda i: (0, i)),
            pl.BlockSpec((width, block), lambda i: (0, i)),
            whole(cosine),
            whole(sine),
        ],
        out_specs=pl.BlockSpec((rows, block), lambda i: (0, i)),
        compiler_params=pltpu.CompilerParams(vmem_limit_bytes=24 << 20),
        cost_estimate=LIGHT,
        name="query",
    )(normed, low, b_query, HBM(weights), cosine, sine)


def output_kernel(me_ref, att_ref, a_ref, b_ref, x_ref, gain_ref, a_two_ref, e_ref, *refs):
    *pieces, middle_ref, normed_ref, low_ref, ext_ref, w_ref, held, sems, last = refs
    copies = place_copies(me_ref[0], pieces, held, sems)
    for copy in copies:
        copy.start()
    attended = att_ref[...]
    low = nt(attended, a_ref[...]).astype(BF)
    low_ref[...] = low
    for copy in copies:
        copy.wait()
    copy = pltpu.make_async_copy(held, w_ref, last)
    copy.start()
    rows, width = attended.shape
    middle = x_ref[...].astype(F32) + nn(attended, held[...]) + nn(low, b_ref[...])
    middle_ref[...] = middle
    normed = normed_of(middle, gain_ref[...])
    normed_ref[...] = normed
    lows = nt(normed, a_two_ref[...]).astype(BF)
    spare = jnp.zeros((rows, TABLE - 3 * RANK), BF)
    lows = jnp.concatenate([lows, e_ref[...], spare], 1)
    ext_ref[:, :width] = normed
    ext_ref[:, width:] = lows
    copy.wait()


def output_stage(me, attended, a_out, b_out, x, gain, a_two, grad_low, pieces, n):
    rows, width = attended.shape
    outer, shard, columns = pieces[0].shape
    anywhere = pl.BlockSpec(memory_space=pl.ANY)
    outs = (
        jax.ShapeDtypeStruct((rows, width), F32),
        jax.ShapeDtypeStruct((rows, width), BF),
        jax.ShapeDtypeStruct((rows, RANK), BF),
        jax.ShapeDtypeStruct((rows, width + TABLE), BF),
    )
    operands = (attended, a_out, b_out, x, gain, a_two, grad_low)
    *results, weights = pl.pallas_call(
        output_kernel,
        grid=(1,),
        out_shape=(*outs, pltpu.HBM((n * shard, columns), BF)),
        in_specs=[pl.BlockSpec(memory_space=pltpu.SMEM)]
        + [full(v) for v in operands]
        + [anywhere] * len(pieces),
        out_specs=(*[full(v) for v in outs], anywhere),
        scratch_shapes=[
            pltpu.VMEM((n * shard, columns), BF),
            pltpu.SemaphoreType.DMA((n,)),
            pltpu.SemaphoreType.DMA(()),
        ],
        compiler_params=pltpu.CompilerParams(vmem_limit_bytes=32 << 20),
        cost_estimate=LIGHT,
        name="output",
    )(me.reshape(1), *map(HBM, operands), *map(HBM, pieces))
    return (*results, weights)


def back_kernel(grad_ref, w_ref, low_ref, a_ref, out_ref):
    out = nt(grad_ref[...], w_ref[...]) + nn(low_ref[...], a_ref[...])
    out_ref[...] = out.astype(out_ref.dtype)


def back_stage(grad, weights, low, table, dtype):
    rows, inner = grad.shape
    width = weights.shape[0]
    block = width // 4
    whole = lambda v: pl.BlockSpec(v.shape, lambda i: (0, 0))
    return pl.pallas_call(
        back_kernel,
        grid=(4,),
        out_shape=jax.ShapeDtypeStruct((rows, width), dtype),
        in_specs=[
            whole(grad),
            pl.BlockSpec((block, inner), lambda i: (i, 0)),
            whole(low),
            pl.BlockSpec((table.shape[0], block), lambda i: (0, i)),
        ],
        out_specs=pl.BlockSpec((rows, block), lambda i: (0, i)),
        compiler_params=pltpu.CompilerParams(vmem_limit_bytes=24 << 20),
        cost_estimate=LIGHT,
        name="back",
    )(*map(HBM, (grad, weights, low, table)))


def norm_two_kernel(adapter_ref, *refs):
    mine, recv, near, last, refs = refs[0], refs[1], refs[2:4], refs[4:6], refs[6:]
    middle_ref, gain_ref, cot_ref, att_ref, low_ref, normed_ref, a_ref, b_ref, refs = *refs[:8], refs[8:]
    grad_ref, one_ref, low_out_ref, low_down_ref, gain_grad_ref, tables_ref = refs
    width = middle_ref.shape[1]
    half = middle_ref.shape[0] // 2
    came = [
        near[i][...].astype(F32) + last[i][...].astype(F32) for i in range(2)
    ]
    total = mine[...].astype(F32) + recv[...].astype(F32) + jnp.concatenate(came, 0)
    lift = lift_of(adapter_ref[0])
    lows = [
        nt(total[:, width + i * TABLE : width + (i + 1) * TABLE].astype(BF), lift[:RANK, :TABLE])
        for i in range(3)
    ]
    low_down = lows[2].astype(BF)
    low_down_ref[...] = low_down
    grad_low = jnp.concatenate(lows[:2], 1).astype(BF)
    grad = total[:, :width] + nn(grad_low, a_ref[...])
    middle = middle_ref[...]
    scale = lax.rsqrt(jnp.mean(middle * middle, -1, keepdims=True) + EPS)
    gain_grad_ref[...] = jnp.sum(grad * middle * scale, 0, keepdims=True)
    grad = grad * gain_ref[...]
    inner = jnp.mean(grad * middle, -1, keepdims=True)
    grad = cot_ref[...].astype(F32) + scale * grad - middle * (scale * scale * scale * inner)
    grad_ref[...] = grad
    one = grad.astype(BF)
    one_ref[...] = one
    low_out = nt(one, b_ref[...]).astype(BF)
    low_out_ref[...] = low_out
    tables_ref[:, :width] = tn(low_out, att_ref[...]).astype(BF)
    tables_ref[:, width : 2 * width] = tn(low_ref[...], one).astype(BF)
    both = tn(grad_low, normed_ref[...]).astype(BF)
    tables_ref[:, 2 * width : 3 * width] = both[:RANK]
    tables_ref[:, 3 * width : 4 * width] = both[RANK:]
    tables_ref[:, 4 * width :] = tn(low_down, cot_ref[...]).astype(BF)


def norm_two_stage(adapter, parts, middle, gain, cot, attended, low_out, normed, a_two, b_out):
    rows, width = middle.shape
    operands = (*parts, middle, gain, cot, attended, low_out, normed, a_two, b_out)
    outs = (
        jax.ShapeDtypeStruct((rows, width), F32),
        jax.ShapeDtypeStruct((rows, width), BF),
        jax.ShapeDtypeStruct((rows, RANK), BF),
        jax.ShapeDtypeStruct((rows, RANK), BF),
        jax.ShapeDtypeStruct((1, width), F32),
        jax.ShapeDtypeStruct((RANK, 5 * width), BF),
    )
    return pl.pallas_call(
        norm_two_kernel,
        grid=(1,),
        out_shape=outs,
        in_specs=[pl.BlockSpec(memory_space=pltpu.SMEM)] + [full(v) for v in operands],
        out_specs=tuple(full(v) for v in outs),
        compiler_params=pltpu.CompilerParams(vmem_limit_bytes=40 << 20),
        cost_estimate=LIGHT,
        name="norm_two",
    )(adapter, *map(HBM, operands))


def project_back_kernel(
    query_ref, kv_ref, came_ref, cos_ref, sin_ref, bq_ref, bkv_ref, low_ref, normed_ref, *outs
):
    grad_ref, grad_low_ref, tables_ref = outs
    width = query_ref.shape[1]
    kv_width = kv_ref.shape[1] // 2
    query = query_ref[...]
    grad_ref[:, :width] = query
    kv = kv_ref[...] + came_ref[...].astype(F32)
    for i in range(kv_ref.shape[1] // LANES):
        slab = kv[:, i * LANES : (i + 1) * LANES]
        if i < kv_width // LANES:
            slab = slab * cos_ref[...] - swap_halves(slab) * sin_ref[...]
        grad_ref[:, width + i * LANES : width + (i + 1) * LANES] = slab.astype(BF)
    kv = grad_ref[:, width:]
    grad_low = nt(kv, bkv_ref[...])
    first = lax.broadcasted_iota(jnp.int32, grad_low.shape, 1) < RANK
    table = jnp.concatenate([bq_ref[...], jnp.zeros((2 * RANK, width), BF)], 0)
    grad_low = jnp.where(first, nt(query, table), grad_low).astype(BF)
    grad_low_ref[...] = grad_low
    reduced = tn(grad_low, normed_ref[...]).astype(BF)
    for i in range(3):
        tables_ref[:, i * width : (i + 1) * width] = reduced[i * RANK : (i + 1) * RANK]
    low = low_ref[...]
    tables_ref[:, 3 * width : 4 * width] = tn(low, query)[:RANK].astype(BF)
    raised = tn(low, kv).astype(BF)
    tables_ref[:, 4 * width : 4 * width + kv_width] = raised[RANK : 2 * RANK, :kv_width]
    tables_ref[:, 4 * width + kv_width :] = raised[2 * RANK :, kv_width:]


def project_back_stage(grad_query, grad_kv, came, cosine, sine, b_query, b_kv, low, normed):
    rows, width = grad_query.shape
    kv = grad_kv.shape[1]
    operands = (grad_query, grad_kv, came, cosine, sine, b_query, b_kv, low, normed)
    outs = (
        jax.ShapeDtypeStruct((rows, width + kv), BF),
        jax.ShapeDtypeStruct(low.shape, BF),
        jax.ShapeDtypeStruct((RANK, 4 * width + kv), BF),
    )
    return pl.pallas_call(
        project_back_kernel,
        grid=(1,),
        out_shape=outs,
        in_specs=[full(v) for v in operands],
        out_specs=tuple(full(v) for v in outs),
        compiler_params=pltpu.CompilerParams(vmem_limit_bytes=32 << 20),
        cost_estimate=LIGHT,
        name="project_back",
    )(*map(HBM, operands))


def norm_one_kernel(grad_ref, w_ref, low_ref, a_ref, x_ref, gain_ref, mid_ref, out_ref, gain_grad_ref, held):
    step = pl.program_id(0)
    block = w_ref.shape[0]
    cols = pl.ds(pl.multiple_of(step * block, block), block)
    held[:, cols] = nt(grad_ref[...], w_ref[...]) + nn(low_ref[...], a_ref[...])

    @pl.when(step == pl.num_programs(0) - 1)
    def _():
        values = x_ref[...].astype(F32)
        scale = lax.rsqrt(jnp.mean(values * values, -1, keepdims=True) + EPS)
        gain_grad_ref[...] = jnp.sum(held[...] * values * scale, 0, keepdims=True)
        grad = held[...] * gain_ref[...]
        inner = jnp.mean(grad * values, -1, keepdims=True)
        out_ref[...] = mid_ref[...] + scale * grad - values * (scale * scale * scale * inner)


def norm_one_stage(grad, weights, low, table, x, gain, grad_middle):
    rows, inner = grad.shape
    width = weights.shape[0]
    block = width // 4
    whole = lambda v: pl.BlockSpec(v.shape, lambda i: (0, 0))
    return pl.pallas_call(
        norm_one_kernel,
        grid=(4,),
        out_shape=(
            jax.ShapeDtypeStruct((rows, width), F32),
            jax.ShapeDtypeStruct((1, width), F32),
        ),
        in_specs=[
            whole(grad),
            pl.BlockSpec((block, inner), lambda i: (i, 0)),
            whole(low),
            pl.BlockSpec((table.shape[0], block), lambda i: (0, i)),
            whole(x),
            whole(gain),
            whole(grad_middle),
        ],
        out_specs=(whole(grad_middle), whole(gain)),
        scratch_shapes=[pltpu.VMEM((rows, width), F32)],
        compiler_params=pltpu.CompilerParams(vmem_limit_bytes=32 << 20),
        cost_estimate=LIGHT,
        name="norm_one",
    )(*map(HBM, (grad, weights, low, table, x, gain, grad_middle)))


def head_pair(own_ref, other_ref, start, group):
    cols = pl.ds(pl.multiple_of(start + (group // 2) * LANES, LANES), LANES)
    slab = jnp.concatenate([own_ref[:, cols], other_ref[:, cols]], 0).astype(F32)
    lane = lax.broadcasted_iota(jnp.int32, slab.shape, 1)
    slab = jnp.where(group % 2 == 0, slab, pltpu.roll(slab, HEAD_DIM, 1))
    first = jnp.where(lane < HEAD_DIM, slab, 0.0)
    return first, pltpu.roll(first, HEAD_DIM, 1)


def attend_kernel(pos_ref, query_ref, own_ref, other_ref, out_ref, probs_ref):
    group = pl.program_id(0)
    rows = query_ref.shape[0]
    keys = [k.astype(BF) for k in head_pair(own_ref, other_ref, 0, group)]
    values = head_pair(own_ref, other_ref, KV_HEADS * HEAD_DIM, group)
    values = [v.T.astype(BF) for v in values]
    key_at = lax.broadcasted_iota(jnp.int32, (2 * rows, rows), 0)
    query_at = lax.broadcasted_iota(jnp.int32, (2 * rows, rows), 1)
    before = (pos_ref[1] < pos_ref[0]).astype(jnp.int32)
    visible = (key_at <= query_at) | ((key_at >= rows) & (before > 0))
    for j in range(query_ref.shape[1] // LANES):
        cols = pl.ds(j * LANES, LANES)
        query = query_ref[:, cols].astype(F32).T.astype(BF)
        mixed = 0.0
        for h in range(2):
            scores = jnp.where(visible, nn(keys[h], query), -1e30)
            weights = jnp.exp(scores - jnp.max(scores, 0, keepdims=True))
            probs = (weights * (1.0 / jnp.sum(weights, 0, keepdims=True))).astype(BF)
            probs_ref[0, 2 * j + h] = probs
            mixed += nn(values[h], probs)
        out_ref[:, cols] = mixed.T.astype(BF)


def attend_stage(blocks, query, own, other):
    rows, width = query.shape
    cols = width // KV_HEADS
    heads = HEADS // KV_HEADS
    tile = pl.BlockSpec((rows, cols), lambda i: (0, i))
    whole = pl.BlockSpec(own.shape, lambda i: (0, 0))
    return pl.pallas_call(
        attend_kernel,
        grid=(KV_HEADS,),
        out_shape=(
            jax.ShapeDtypeStruct((rows, width), BF),
            pltpu.HBM((KV_HEADS, heads, 2 * rows, rows), BF),
        ),
        in_specs=[pl.BlockSpec(memory_space=pltpu.SMEM), tile, whole, whole],
        out_specs=(tile, pl.BlockSpec((1, heads, 2 * rows, rows), lambda i: (i, 0, 0, 0))),
        compiler_params=pltpu.CompilerParams(vmem_limit_bytes=32 << 20),
        cost_estimate=LIGHT,
        name="attend",
    )(blocks, query, own, other)


def attend_back_kernel(
    grad_ref,
    out_ref,
    query_ref,
    own_ref,
    other_ref,
    probs_ref,
    cos_ref,
    sin_ref,
    gq_ref,
    gown_ref,
    gother_ref,
    gkv_ref,
):
    group = pl.program_id(0)
    keys = [k.T.astype(BF) for k in head_pair(own_ref, other_ref, 0, group)]
    values = head_pair(own_ref, other_ref, KV_HEADS * HEAD_DIM, group)
    values = [v.astype(BF) for v in values]
    cosine, sine = cos_ref[...], sin_ref[...]
    grad_keys, grad_values = [0.0, 0.0], [0.0, 0.0]
    for j in range(query_ref.shape[1] // LANES):
        cols = pl.ds(j * LANES, LANES)
        grad = grad_ref[:, cols]
        query = query_ref[:, cols]
        turned = grad.astype(F32).T
        product = turned * out_ref[:, cols].astype(F32).T
        turned = turned.astype(BF)
        grad_query = 0.0
        for h in range(2):
            inner = jnp.sum(product[h * HEAD_DIM : (h + 1) * HEAD_DIM], 0, keepdims=True)
            probs = probs_ref[0, 2 * j + h]
            grad_scores = (probs.astype(F32) * (nn(values[h], turned) - inner)).astype(BF)
            grad_values[h] += nn(probs, grad)
            grad_keys[h] += nn(grad_scores, query)
            grad_query += nn(keys[h], grad_scores)
        grad_query = grad_query.T * HEAD_DIM ** (-0.5)
        grad_query = grad_query * cosine - swap_halves(grad_query) * sine
        gq_ref[:, cols] = grad_query.astype(BF)

    @pl.when(group == 0)
    def _():
        gkv_ref[...] = jnp.zeros_like(gkv_ref)

    lane = lax.broadcasted_iota(jnp.int32, grad_keys[0].shape, 1)
    for start, (first, last) in ((0, grad_keys), (KV_HEADS * HEAD_DIM, grad_values)):
        total = jnp.where(lane < HEAD_DIM, first + pltpu.roll(last, HEAD_DIM, 1), 0.0)
        total = jnp.where(group % 2 == 0, total, pltpu.roll(total, HEAD_DIM, 1))
        cols = pl.ds(pl.multiple_of(start + (group // 2) * LANES, LANES), LANES)
        gkv_ref[:, cols] += total

    @pl.when(group == pl.num_programs(0) - 1)
    def _():
        rows = gown_ref.shape[0]
        gown_ref[...] = gkv_ref[pl.ds(0, rows), :]
        gother_ref[...] = gkv_ref[pl.ds(rows, rows), :].astype(BF)


def attend_back_stage(grad, out, query, own, other, probs, cosine, sine):
    rows, width = query.shape
    cols = width // KV_HEADS
    tile = pl.BlockSpec((rows, cols), lambda i: (0, i))
    whole = pl.BlockSpec(own.shape, lambda i: (0, 0))
    table = pl.BlockSpec((rows, LANES), lambda i: (0, 0))
    return pl.pallas_call(
        attend_back_kernel,
        grid=(KV_HEADS,),
        out_shape=(
            jax.ShapeDtypeStruct((rows, width), BF),
            jax.ShapeDtypeStruct(own.shape, F32),
            jax.ShapeDtypeStruct(own.shape, BF),
        ),
        scratch_shapes=[pltpu.VMEM((2 * rows, own.shape[1]), F32)],
        in_specs=[tile, tile, tile, whole, whole]
        + [pl.BlockSpec((1,) + probs.shape[1:], lambda i: (i, 0, 0, 0)), table, table],
        out_specs=(tile, whole, whole),
        compiler_params=pltpu.CompilerParams(vmem_limit_bytes=32 << 20),
        cost_estimate=LIGHT,
        name="attend_back",
    )(grad, out, query, own, other, probs, cosine, sine)


def send_columns(parts, n):
    whole = jnp.concatenate(parts, 1).astype(BF)
    whole = jnp.pad(whole, ((0, 0), (0, -whole.shape[1] % n)))
    return jnp.moveaxis(whole.reshape(RANK, n, -1), 1, 0)


def sum_columns(parts, ids, own_rows):
    n, _, chunk = parts.shape
    onehot = (ids[:, None] == jnp.arange(ADAPTERS, dtype=jnp.int32)[None, :]).astype(BF)
    summed = jnp.einsum("na,nrc->arc", onehot, parts, preferred_element_type=F32)
    return summed.reshape(n, own_rows, chunk)


def per_device(
    n,
    inputs,
    cotangent,
    adapter_ids,
    block_index,
    gain_first,
    gain_second,
    w_query,
    w_key,
    w_value,
    w_output,
    w_gate_up,
    w_down,
    reduce_attention,
    raise_query,
    raise_keyvalue,
    reduce_output,
    raise_output,
    reduce_gate_up,
    raise_gate_up,
    reduce_down,
    raise_down,
):
    width = inputs.shape[-1]
    rows = inputs.shape[-2]
    shard = w_down.shape[0]
    own_rows = raise_down.shape[0]
    gains = gain_first.shape[0]
    kv_width = KV_HEADS * HEAD_DIM
    side = lax.axis_index("seq")
    me = lax.axis_index(ALL).astype(jnp.int32)
    tokens = inputs.reshape(rows, width)
    grad_out = cotangent.reshape(rows, width)

    order = Order()
    qkv_width = width + 2 * kv_width
    att_rows = Outer(jnp.concatenate([w_query, w_key, w_value, w_output], 1), n)
    att_rows.step()
    cot_plane = Plane(grad_out, n)
    padded = -(-shard // 16) * 16
    slot = -(-(n // 8) * padded // 256) * 256 // (n // 8)
    feed = jnp.stack([w_gate_up[0].T, w_gate_up[1].T, w_down])

    table_width = 10 * width
    chunk = table_width // n
    table = jnp.concatenate(
        [reduce_attention[0], reduce_attention[1], reduce_attention[2], raise_query]
        + [reduce_output, raise_output, reduce_gate_up[0], reduce_gate_up[1], raise_down]
        + [raise_keyvalue[0], raise_keyvalue[1]],
        1,
    )
    table = jnp.pad(table, ((0, 0), (0, table_width - table.shape[1])))
    table = jnp.moveaxis(table.reshape(own_rows, n, chunk), 1, 0)
    hidden_table = jnp.stack([raise_gate_up[0], raise_gate_up[1], reduce_down])
    hidden_table = hidden_table.reshape(3, own_rows, n, shard).transpose(2, 1, 0, 3)
    hidden_table = hidden_table.reshape(n, own_rows, 3 * shard)
    small = jnp.concatenate([gain_first, gain_second, adapter_ids.astype(BF)])
    used = chunk + 3 * shard
    sent = -(-(used + small.shape[0]) // 128) * 128
    small = jnp.pad(small, (0, sent - used - small.shape[0]))
    small = jnp.broadcast_to(small, (n, own_rows, small.shape[0]))
    table = jnp.concatenate([table, hidden_table, small], -1)
    came = lax.all_to_all(table, ALL, 0, 0, tiled=True)
    cot_plane.near = att_rows.pass_through(order, *cot_plane.near)
    att_rows.step_all()
    gain_one = came[:, 0, used : used + gains].reshape(width).astype(F32)
    gain_two = came[:, 0, used + gains : used + 2 * gains].reshape(width).astype(F32)
    ids = came[:, 0, used + 2 * gains].astype(jnp.int32)
    columns = came[:, :, :chunk].reshape(ADAPTERS, RANK, chunk)
    hidden_cols = came[:, :, chunk:used].reshape(TABLE, 3, shard)
    own = lax.all_to_all(jnp.take(columns, ids, axis=0), ALL, 0, 0, tiled=True)
    feed = jnp.concatenate([feed, hidden_cols.transpose(1, 2, 0)], 2)
    feed = jnp.pad(feed, ((0, 0), (0, padded - shard), (0, 0))).reshape(3 * padded, -1)
    (feed,) = att_rows.pass_through(order, feed)
    feed = lax.all_gather(feed, "outer", axis=0, tiled=True)
    qkv_rows = Rows([part[:, :qkv_width] for part in att_rows.parts()], n)
    qkv_rows.start_plane()
    qkv_rows.near = order.point(*qkv_rows.near)
    qkv_rows.end_plane()
    own = jnp.moveaxis(own, 0, 1).reshape(RANK, table_width)
    (a_query, a_key, a_value, b_query, a_out, b_out, a_gate, a_up, b_down) = [
        own[:, i * width : (i + 1) * width] for i in range(9)
    ]
    b_key = own[:, 9 * width : 9 * width + kv_width]
    b_value = own[:, 9 * width + kv_width : 9 * width + 2 * kv_width]

    own_block = lax.dynamic_index_in_dim(block_index[0], side, 0, keepdims=False)
    other_block = lax.dynamic_index_in_dim(block_index[0], 1 - side, 0, keepdims=False)
    blocks = jnp.stack([own_block, other_block])
    cosine, sine = rotary_tables(own_block * rows + jnp.arange(rows, dtype=jnp.int32))
    a_att = jnp.concatenate([a_query, a_key, a_value], 0)
    a_two = jnp.concatenate([a_gate, a_up], 0)
    b_kv = jnp.concatenate(
        [
            jnp.zeros((RANK, 2 * kv_width), BF),
            jnp.pad(b_key, ((0, 0), (0, kv_width))),
            jnp.pad(b_value, ((0, 0), (kv_width, 0))),
        ],
        0,
    )
    grad_low_down = nt(grad_out, b_down).astype(BF)
    plane_ids = jnp.stack([ids[me], ids[me ^ C], ids[me ^ Y], ids[me ^ (Y | C)]])
    out_rows = Rows([part[:, qkv_width:] for part in att_rows.parts()], n)
    passed = order.point(
        *qkv_rows.last, a_att, a_two, b_kv, cosine, sine, grad_low_down, plane_ids, out_rows.whole
    )
    qkv_rows.last = passed[:2]
    a_att, a_two, b_kv, cosine, sine, grad_low_down, plane_ids, out_rows.whole = passed[2:]
    out_rows.start_plane()
    normed_one, low_att, key_value, w_qkv = project_stage(
        me, tokens, gain_one[None], a_att, b_kv, cosine, sine, qkv_rows.pieces(), n
    )
    low_query, low_key, low_value = [low_att[:, i * RANK : (i + 1) * RANK] for i in range(3)]
    key_value = order.point(key_value)
    other_kv = exchange(key_value, X, n)
    query = query_stage(normed_one, low_att, b_query, w_qkv, cosine, sine)
    key_value, other_kv, query = order.point(key_value, other_kv, query)
    attended, probs = attend_stage(blocks, query, key_value, other_kv)
    attended, *out_rows.near = order.point(attended, *out_rows.near)
    out_rows.end_plane()
    attended, *out_rows.last = order.point(attended, *out_rows.last)
    cot_plane.end()
    middle, normed_two, low_out, normed_ext, w_out = output_stage(
        me,
        attended,
        a_out,
        b_out,
        tokens,
        gain_two[None],
        a_two,
        grad_low_down,
        out_rows.pieces(),
        n,
    )

    normed_ext, *cot_plane.last = order.point(normed_ext, *cot_plane.last)
    cot_plane.finish()
    normed_plane = Plane(normed_ext, n)
    normed_plane.near = order.point(*normed_plane.near)
    normed_plane.end()
    passed = order.point(*normed_plane.far, *cot_plane.far, *cot_plane.last_far)
    normed_plane.far, cot_plane.far, cot_plane.last_far = passed[:2], passed[2:4], passed[4:]
    feed_of = lambda ids_here, place, groups: feed_stage(
        ids_here,
        place,
        len(groups),
        feed,
        normed_plane.group(*groups),
        cot_plane.group(*groups),
        padded,
        slot,
    )
    normed_sum = PlaneSum(n)
    hidden_mid, grads_mid, near_out, far_out = feed_of(plane_ids, 0, (1, 2))
    mid_recv = exchange(far_out, C, n)
    near_out, *normed_plane.last = order.point(near_out, *normed_plane.last)
    for j in range(2):
        part = slice(j * rows, (j + 1) * rows)
        normed_sum.put(j + 1, near_out[part], mid_recv[part])
    normed_plane.finish()
    hidden_far, grads_far, near_out, far_out = feed_of(plane_ids, 2, (3,))
    normed_sum.put(3, near_out, exchange(far_out, C, n))
    ids_own, *sends = order.point(plane_ids, *normed_sum.far_sends(), *normed_sum.near_sends())
    far_came, near_came = normed_sum.hop(*sends[:2]), normed_sum.hop(*sends[2:])
    hidden_own, grads_own, near_out, far_out = feed_of(ids_own, 0, (0,))
    recv = exchange(far_out, C, n)
    near_out, grads_own, *came = order.point(near_out, grads_own, *far_came, *near_came)
    far_came, near_came = came[:2], came[2:]
    hidden_grads = grads_own + grads_mid + grads_far
    hidden_grads = jnp.concatenate([hidden_grads[i] for i in range(3)], 1).astype(BF)
    hidden_grads = hidden_grads.reshape(n, own_rows, -1)
    last_sends = order.point(*normed_sum.last_sends(*far_came))
    last_came = normed_sum.last_hop(*last_sends)
    hidden_own, hidden_grads = order.point(hidden_own, hidden_grads)
    hidden_grads = lax.all_to_all(hidden_grads, ALL, 0, 0, tiled=True)
    down_near, down_far = down_stage(
        [hidden_own, hidden_mid, hidden_far], feed, n // 8, padded, slot, rows
    )
    parts = order.point(recv, *near_came, *last_came, down_far)
    down_far = parts[5]
    parts = (near_out, *parts[:5])

    grad_middle, grad_one, grad_low_out, low_down, gain_grad_two, early = norm_two_stage(
        adapter_ids, parts, middle, gain_two[None], grad_out, attended, low_out, normed_two, a_two, b_out
    )
    down_recv = exchange(down_far, C, n)
    grad_attended = back_stage(grad_one, w_out, grad_low_out, a_out, BF)
    down_sum = PlaneSum(n)
    for i in range(4):
        part = slice(i * rows, (i + 1) * rows)
        down_sum.put(i, down_near[part], down_recv[part])
    grad_query, grad_kv, kv_away = attend_back_stage(
        grad_attended, attended, query, key_value, other_kv, probs, cosine, sine
    )
    grad_query, grad_kv, kv_away, hidden_grads = order.point(
        grad_query, grad_kv, kv_away, hidden_grads
    )
    kv_came, *sends = order.point(
        exchange(kv_away, X, n), *down_sum.far_sends(), *down_sum.near_sends()
    )
    down_far = down_sum.hop(*sends[:2])
    grad_qkv, grad_low_att, late = project_back_stage(
        grad_query, grad_kv, kv_came, cosine, sine, b_query, b_kv, low_att, normed_one
    )

    late, grad_qkv = order.point(send_columns([late, early], n), grad_qkv)
    late = lax.all_to_all(late, ALL, 0, 0, tiled=True)
    down_near = down_sum.hop(*sends[2:])
    input_grad, gain_grad_one = norm_one_stage(
        grad_qkv, w_qkv, grad_low_att, a_att, tokens, gain_one[None], grad_middle
    )
    input_grad = input_grad.reshape(inputs.shape)
    gain_grads = jnp.concatenate(
        [gain_grad_one.reshape(n, gains), gain_grad_two.reshape(n, gains)], 1
    )
    gain_grads = jnp.broadcast_to(gain_grads[:, None], (n, own_rows, 2 * gains))
    input_grad, gain_grads, *down_far = order.point(input_grad, gain_grads, *down_far)
    down_last = down_sum.last_hop(*down_sum.last_sends(*down_far))
    late = jnp.concatenate([sum_columns(late, ids, own_rows), gain_grads], -1)
    late, hidden_grads, down_sum.mine[0] = order.point(late, hidden_grads, down_sum.mine[0])
    late = lax.all_to_all(late, ALL, 0, 0, tiled=True)
    branch_two = down_sum.total(down_near, down_last)
    output = (middle + branch_two + nn(low_down, b_down)).astype(BF)
    hidden_grads = hidden_grads.reshape(n // 8, 8, own_rows, 3, n // 8, slot)
    hidden_grads = jnp.sum(hidden_grads[..., :shard].astype(F32), 0)
    hidden_grads = hidden_grads.transpose(2, 1, 3, 0, 4).reshape(3, own_rows, -1)
    gain_grads = jnp.sum(late[:, 0, -2 * gains :], 0) + order.token
    late_rows = jnp.moveaxis(late[:, :, : -2 * gains], 0, 1).reshape(own_rows, -1)
    parts = [late_rows[:, i * width : (i + 1) * width] for i in range(4)]
    kv = late_rows[:, 4 * width : 4 * width + 2 * kv_width]
    start = 4 * width + 2 * kv_width
    parts += [late_rows[:, start + i * width : start + (i + 1) * width] for i in range(5)]
    return (
        output.reshape(inputs.shape),
        input_grad,
        gain_grads[:gains],
        gain_grads[gains:],
        jnp.stack(parts[:3]),
        parts[3],
        jnp.stack([kv[:, :kv_width], kv[:, kv_width:]]),
        parts[4],
        parts[5],
        jnp.stack(parts[6:8]),
        hidden_grads[:2],
        hidden_grads[2],
        parts[8],
    )


def solution(mesh):
    dp, seq = mesh.shape["dp"], mesh.shape["seq"]
    n = dp * seq
    dp_axes = ALL[:2]
    rows = P(ALL, None)
    stacked = P(None, ALL, None)
    vector = P(ALL)
    blocks = P(dp_axes, "seq", None, None)
    return jax.shard_map(
        functools.partial(per_device, n),
        mesh=Mesh(mesh.devices.reshape(dp // 4, 4, seq), ALL),
        in_specs=(
            (blocks, blocks, P(dp_axes), P(dp_axes, None), vector, vector)
            + (rows, rows, rows, rows, P(None, None, ALL), rows)
            + (stacked, rows, stacked, rows, rows, stacked, stacked, rows, rows)
        ),
        out_specs=(
            (blocks, blocks, vector, vector, stacked, rows, stacked, rows, rows)
            + (stacked, stacked, rows, rows)
        ),
        check_vma=False,
    )
```

```python
import functools

import jax
import jax.numpy as jnp
from jax import lax
from jax.experimental import pallas as pl
from jax.experimental.pallas import tpu as pltpu
from jax.sharding import Mesh
from jax.sharding import PartitionSpec as P

HEADS = 32
KV_HEADS = 4
HEAD_DIM = 64
ADAPTERS = 8
RANK = 16
TABLE = ADAPTERS * RANK

EPS = 1e-05
THETA = 10000.0

ALL = ("outer", "pair", "seq")
X, C, Y = 1, 2, 4
BF = jnp.bfloat16
F32 = jnp.float32
HBM = lambda value: pltpu.with_memory_space_constraint(value, pltpu.HBM)
LIGHT = pl.CostEstimate(flops=1 << 20, bytes_accessed=1 << 16, transcendentals=0)


def dot(a, b, dims):
    return lax.dot_general(a, b, (dims, ((), ())), preferred_element_type=F32)


def nn(a, b):
    return dot(a, b, ((1,), (0,)))


def nt(a, b):
    return dot(a, b, ((1,), (1,)))


def tn(a, b):
    return dot(a, b, ((0,), (0,)))


def exchange(value, mask, n):
    return lax.ppermute(value, ALL, [(i, i ^ mask) for i in range(n)])


def rotary_tables(positions):
    half = HEAD_DIM // 2
    speeds = THETA ** (-jnp.arange(half, dtype=F32) * (2.0 / HEAD_DIM))
    angles = positions.astype(F32)[:, None] * speeds
    cosine, sine = jnp.cos(angles), jnp.sin(angles)
    return jnp.tile(cosine, (1, 4)), jnp.tile(jnp.concatenate([-sine, sine], 1), (1, 2))


def outer_bits(n):
    bits, bit = [], 8
    while bit < n:
        bits.append(bit)
        bit *= 2
    return bits


class Outer:
    def __init__(self, value, n):
        self.n = n
        self.held = {0: value}
        self.offsets = sorted(range(8, n, 8), key=lambda offset: (bin(offset).count("1"), -offset))

    def step(self):
        if not self.offsets:
            return False
        level = bin(self.offsets[0]).count("1")
        while self.offsets and bin(self.offsets[0]).count("1") == level:
            offset = self.offsets.pop(0)
            low = offset & -offset
            self.held[offset] = exchange(self.held[offset ^ low], low, self.n)
        return bool(self.offsets)

    def step_all(self):
        while self.step():
            pass

    def pass_through(self, order, *others):
        keys = sorted(self.held)
        passed = order.point(*[self.held[k] for k in keys], *others)
        self.held = dict(zip(keys, passed))
        return passed[len(keys) :]

    def parts(self):
        return [self.held[offset] for offset in sorted(self.held)]


def place_copies(me, pieces, held, sems):
    z, y, c, x = me // 8, (me // 4) % 2, (me // 2) % 2, me % 2
    copies = []
    for i, piece in enumerate(pieces):
        dc, kind = i // 5, i % 5
        dy, dx = ((0, 0), (0, 1), (1, 0), (1, 1), (1, 1))[kind]
        first = piece.shape[0] if kind == 4 else 0
        for j in range(piece.shape[0]):
            dz = first + j
            block = (((z ^ dz) * 2 + (y ^ dy)) * 2 + (c ^ dc)) * 2 + (x ^ dx)
            rows = pl.ds(pl.multiple_of(block * piece.shape[1], piece.shape[1]), piece.shape[1])
            copies.append(
                pltpu.make_async_copy(piece.at[j], held.at[rows], sems.at[len(copies)])
            )
    return copies


def normed_of(values, gain):
    scale = lax.rsqrt(jnp.mean(values * values, -1, keepdims=True) + EPS)
    return (values * scale * gain).astype(BF)


class Outer:
    def __init__(self, value, n):
        self.n = n
        self.held = {0: value}
        self.offsets = sorted(range(8, n, 8), key=lambda offset: (bin(offset).count("1"), -offset))

    def step(self):
        if not self.offsets:
            return False
        level = bin(self.offsets[0]).count("1")
        while self.offsets and bin(self.offsets[0]).count("1") == level:
            offset = self.offsets.pop(0)
            low = offset & -offset
            self.held[offset] = exchange(self.held[offset ^ low], low, self.n)
        return bool(self.offsets)

    def step_all(self):
        while self.step():
            pass

    def pass_through(self, order, *others):
        keys = sorted(self.held)
        passed = order.point(*[self.held[k] for k in keys], *others)
        self.held = dict(zip(keys, passed))
        return passed[len(keys) :]

    def parts(self):
        return [self.held[offset] for offset in sorted(self.held)]


def sum_outer(parts, n):
    held = {8 * i: part for i, part in enumerate(parts)}
    for bit in outer_bits(n):
        for offset in sorted(held):
            if offset & bit:
                held[offset ^ bit] = held[offset ^ bit] + exchange(held.pop(offset), bit, n)
    return held[0]


def place_kernel(count, outer, width, me_ref, *refs):
    pieces, out, held, sems, last = refs[:count], *refs[count:]
    me = me_ref[0]
    z, y, c, x = me // 8, (me // 4) % 2, (me // 2) % 2, me % 2
    copies = []
    for i in range(count):
        part, dc, dy, dx = i // 8, (i // 4) % 2, (i // 2) % 2, i % 2
        for dz in range(outer):
            block = (((z ^ dz) * 2 + (y ^ dy)) * 2 + (c ^ dc)) * 2 + (x ^ dx)
            copies.append(
                pltpu.make_async_copy(
                    pieces[i].at[dz],
                    held.at[block, :, pl.ds(part * width, width)],
                    sems.at[len(copies)],
                )
            )
    for copy in copies:
        copy.start()
    for copy in copies:
        copy.wait()
    copy = pltpu.make_async_copy(held, out, last)
    copy.start()
    copy.wait()


class Rows:
    def __init__(self, parts, n):
        self.n = n
        self.whole = jnp.stack(parts)

    def start_plane(self):
        self.near = [exchange(self.whole, bit, self.n) for bit in (X, Y, C)]

    def end_plane(self):
        from_x, from_y, _ = self.near
        half = from_x.shape[0] // 2
        self.last = [
            exchange(from_x[:half], Y, self.n),
            exchange(from_y[half:], X, self.n),
        ]
        self.far = [exchange(v, C, self.n) for v in (from_x, from_y)]

    def pieces(self):
        last_far = [exchange(v, C, self.n) for v in self.last]
        from_x, from_y, other = self.near
        return [self.whole, from_x, from_y, *self.last, other, *self.far, *last_far]


class Plane:
    def __init__(self, value, n):
        self.n = n
        self.own = value
        self.near = [exchange(value, X, n), exchange(value, Y, n), exchange(value, C, n)]

    def end(self):
        from_x, from_y, _ = self.near
        half = from_x.shape[0] // 2
        self.last = [exchange(from_x[:half], Y, self.n), exchange(from_y[half:], X, self.n)]
        self.far = [exchange(v, C, self.n) for v in (from_x, from_y)]

    def finish(self):
        self.last_far = [exchange(v, C, self.n) for v in self.last]

    def group(self, *which):
        parts = []
        for g in which:
            if g == 3:
                parts += [*self.last, *self.last_far]
            else:
                parts += [self.near[g - 1], self.far[g - 1]] if g else [self.own, self.near[2]]
        return parts


class Order:
    def __init__(self):
        self.token = jnp.zeros((), F32)

    def point(self, *values):
        *values, self.token = lax.optimization_barrier((*values, self.token))
        return values[0] if len(values) == 1 else values


def half_of(block, part):
    half = block.shape[0] // 2
    return block[part * half : (part + 1) * half].astype(F32)


class PlaneSum:
    def __init__(self, n):
        self.n = n
        self.mine, self.recv = {}, {}

    def put(self, block, near, recv):
        self.mine[block], self.recv[block] = near, recv

    def held(self, block, part):
        return half_of(self.mine[block], part) + half_of(self.recv[block], part)

    def far_sends(self):
        return self.held(3, 0).astype(BF), self.held(3, 1).astype(BF)

    def near_sends(self):
        return self.held(1, 0).astype(BF), self.held(2, 1).astype(BF)

    def last_sends(self, first, second):
        return (
            (self.held(2, 0) + first.astype(F32)).astype(BF),
            (self.held(1, 1) + second.astype(F32)).astype(BF),
        )

    def hop(self, first, second):
        return exchange(first, X, self.n), exchange(second, Y, self.n)

    def last_hop(self, first, second):
        return exchange(first, Y, self.n), exchange(second, X, self.n)

    def total(self, near, last):
        return jnp.concatenate(
            [self.held(0, i) + near[i].astype(F32) + last[i].astype(F32) for i in range(2)], 0
        )


def full(value):
    shape = value.shape
    return pl.BlockSpec(shape, lambda i: (0,) * len(shape), pipeline_mode=pl.Buffered(1))


def copies_of(pieces, target, stride, sems):
    copies, row = [], 0
    for i, piece in enumerate(pieces):
        size = piece.shape[0]
        copies.append(pltpu.make_async_copy(piece, target.at[pl.ds(row, size)], sems.at[i]))
        row += stride or size
    return copies


def clear_spare(target, used, slot):
    if slot > used:
        for row in range(0, target.shape[0], slot):
            target[pl.ds(row + used, slot - used), :] = jnp.zeros(
                (slot - used, target.shape[1]), target.dtype
            )


def lift_of(adapter):
    row = lax.broadcasted_iota(jnp.int32, (TABLE, 3 * TABLE), 0)
    col = lax.broadcasted_iota(jnp.int32, (TABLE, 3 * TABLE), 1)
    goal = (row // RANK) * TABLE + adapter * RANK + row % RANK
    return ((col == goal) & (row < 3 * RANK)).astype(F32).astype(BF)


def feed_copies(feed, kind, padded, slot, target, first, columns, sems):
    start, size, to = columns
    return [
        pltpu.make_async_copy(
            feed.at[pl.ds((3 * i + kind) * padded, padded), pl.ds(start, size)],
            target.at[pl.ds(first + i * slot, padded), pl.ds(to, size)],
            sems.at[i],
        )
        for i in range(sems.shape[0])
    ]


def feed_kernel(sizes, ids_ref, feed_ref, *refs):
    parts, padded, slot, width, place = sizes
    normed_in, cot_in, refs = refs[:parts], refs[parts : 2 * parts], refs[2 * parts :]
    hidden_ref, grads_ref, near_ref, far_ref, refs = *refs[:4], refs[4:]
    w_both, w_down, normed_all, cot_all, both_all, grad_all, acts, *sems = refs
    group = pl.program_id(0)
    block, cols = hidden_ref.shape
    half = block // 2
    wide = width + TABLE
    loads = [
        copies_of(normed_in, normed_all.at[:, pl.ds(0, wide)], None, sems[0]),
        feed_copies(feed_ref, 0, padded, slot, w_both, 0, (0, wide, 0), sems[1]),
        feed_copies(feed_ref, 1, padded, slot, w_both, cols, (0, width, 0), sems[2])
        + feed_copies(feed_ref, 1, padded, slot, w_both, cols, (width, TABLE, wide), sems[3]),
        copies_of(cot_in, cot_all.at[:, pl.ds(0, width)], None, sems[4]),
        feed_copies(feed_ref, 2, padded, slot, w_down, 0, (0, wide, 0), sems[5]),
    ]

    def arrive(*which):
        @pl.when(group == 0)
        def _():
            for i in which:
                for copy in loads[i]:
                    copy.wait()

    @pl.when(group == 0)
    def _():
        for load in loads:
            for copy in load:
                copy.start()
        grads_ref[...] = jnp.zeros_like(grads_ref)
        zeros = jnp.zeros((cols, TABLE), BF)
        w_both[pl.ds(0, cols), wide:] = zeros
        w_both[pl.ds(cols, cols), width:wide] = zeros
        clear_spare(w_both, padded, slot)
        clear_spare(w_down, padded, slot)

    row = pl.multiple_of(group * block, block)
    own = pl.ds(row, block)
    arrive(0)
    for i in range(2):
        here = pl.ds(row + i * half, half)
        lows = nn(normed_all[here, width:wide], lift_of(ids_ref[place + 2 * group + i])).astype(BF)
        normed_all[here, width:] = lows[:, : 2 * TABLE]
        cot_all[here, width:] = lows[:, 2 * TABLE :]
    arrive(1, 2)
    both_all[...] = nt(normed_all[own, :], w_both[...])
    arrive(3, 4)
    grad_all[...] = nt(cot_all[own, :], w_down[...])
    step = 16

    def rows_of(i, carry):
        here = pl.ds(pl.multiple_of(i * step, step), step)
        gate, up, grad = both_all[here, :cols], both_all[here, cols:], grad_all[here, :]
        sigmoid = 0.5 * jnp.tanh(0.5 * gate) + 0.5
        silu = gate * sigmoid
        hidden_ref[here, :] = (silu * up).astype(BF)
        acts[here, :cols] = (grad * up * (sigmoid + silu * (1.0 - sigmoid))).astype(BF)
        acts[here, cols:] = (grad * silu).astype(BF)
        return carry

    lax.fori_loop(0, block // step, rows_of, 0)
    out = nn(acts[...], w_both[...]).astype(BF)
    low = nn(hidden_ref[...], w_down[:, width:]).astype(BF)
    for i, ref in enumerate((near_ref, far_ref)):
        ref[:, : wide + TABLE] = out[i * half : (i + 1) * half]
        ref[:, wide + TABLE :] = low[i * half : (i + 1) * half]
    grads_ref[0] += tn(normed_all[own, width:wide], acts[:, :cols])
    grads_ref[1] += tn(normed_all[own, wide:], acts[:, cols:])
    grads_ref[2] += tn(cot_all[own, width:], hidden_ref[...])


def feed_stage(ids, place, groups, feed, normed, cot, padded, slot):
    wide, width = normed[0].shape[1], cot[0].shape[1]
    tokens = sum(part.shape[0] for part in normed)
    block = tokens // groups
    pieces = feed.shape[0] // (3 * padded)
    cols = pieces * slot
    tile = pl.BlockSpec((block, cols), lambda i: (i, 0))
    anywhere = pl.BlockSpec(memory_space=pl.ANY)
    out = jax.ShapeDtypeStruct((tokens // 2, wide + 2 * TABLE), BF)
    out_tile = pl.BlockSpec((block // 2, wide + 2 * TABLE), lambda i: (i, 0))
    counts = (len(normed),) + (pieces,) * 3 + (len(cot), pieces)
    return pl.pallas_call(
        functools.partial(feed_kernel, (len(normed), padded, slot, width, place)),
        grid=(groups,),
        out_shape=(
            jax.ShapeDtypeStruct((tokens, cols), BF),
            jax.ShapeDtypeStruct((3, TABLE, cols), F32),
            out,
            out,
        ),
        in_specs=[pl.BlockSpec(memory_space=pltpu.SMEM)]
        + [anywhere] * (1 + len(normed) + len(cot)),
        out_specs=(
            tile,
            pl.BlockSpec((3, TABLE, cols), lambda i: (0, 0, 0)),
            out_tile,
            out_tile,
        ),
        scratch_shapes=[
            pltpu.VMEM((2 * cols, wide + TABLE), BF),
            pltpu.VMEM((cols, wide), BF),
            pltpu.VMEM((tokens, wide + TABLE), BF),
            pltpu.VMEM((tokens, wide), BF),
            pltpu.VMEM((block, 2 * cols), F32),
            pltpu.VMEM((block, cols), F32),
            pltpu.VMEM((block, 2 * cols), BF),
        ]
        + [pltpu.SemaphoreType.DMA((count,)) for count in counts],
        compiler_params=pltpu.CompilerParams(vmem_limit_bytes=44 << 20),
        cost_estimate=LIGHT,
        name="feed",
    )(ids, HBM(feed), *map(HBM, normed), *map(HBM, cot))


def down_kernel(padded, slot, *refs):
    *acts, feed_ref, near_ref, far_ref, w_down, sems = refs
    loads = feed_copies(feed_ref, 2, padded, slot, w_down, 0, (0, w_down.shape[1], 0), sems)
    for copy in loads:
        copy.start()
    clear_spare(w_down, padded, slot)
    for copy in loads:
        copy.wait()
    rows = near_ref.shape[0] // 4
    done = 0
    for act in acts:
        for i in range(act.shape[0] // (2 * rows)):
            out = nn(act[pl.ds(i * 2 * rows, 2 * rows), :], w_down[...]).astype(BF)
            near_ref[pl.ds(done, rows), :] = out[:rows]
            far_ref[pl.ds(done, rows), :] = out[rows:]
            done += rows


def down_stage(hiddens, feed, pieces, padded, slot, rows):
    width = feed.shape[1] - TABLE
    out = jax.ShapeDtypeStruct((4 * rows, width), BF)
    return pl.pallas_call(
        functools.partial(down_kernel, padded, slot),
        grid=(1,),
        out_shape=(out, out),
        in_specs=[full(v) for v in hiddens] + [pl.BlockSpec(memory_space=pl.ANY)],
        out_specs=(full(out), full(out)),
        scratch_shapes=[
            pltpu.VMEM((pieces * slot, width), BF),
            pltpu.SemaphoreType.DMA((pieces,)),
        ],
        compiler_params=pltpu.CompilerParams(vmem_limit_bytes=32 << 20),
        cost_estimate=LIGHT,
        name="down",
    )(*map(HBM, hiddens), HBM(feed))


LANES = 2 * HEAD_DIM


def swap_halves(values):
    lane = lax.broadcasted_iota(jnp.int32, values.shape, 1) % HEAD_DIM
    half = HEAD_DIM // 2
    left = pltpu.roll(values, LANES - half, 1)
    return jnp.where(lane < half, left, pltpu.roll(values, half, 1))


def rope(slab, cosine, sine):
    return slab * cosine + swap_halves(slab) * sine


def project_kernel(
    me_ref, x_ref, gain_ref, a_ref, b_ref, cos_ref, sin_ref, *refs
):
    *pieces, normed_ref, low_ref, kv_ref, w_ref, held, sems, last = refs
    copies = place_copies(me_ref[0], pieces, held, sems)
    for copy in copies:
        copy.start()
    normed = normed_of(x_ref[...].astype(F32), gain_ref[...])
    normed_ref[...] = normed
    low = nt(normed, a_ref[...]).astype(BF)
    low_ref[...] = low
    for copy in copies:
        copy.wait()
    copy = pltpu.make_async_copy(held, w_ref, last)
    copy.start()
    width = kv_ref.shape[1]
    kv = nn(normed, held[:, held.shape[1] - width :]) + nn(low, b_ref[...])
    for i in range(width // LANES):
        cols = slice(i * LANES, (i + 1) * LANES)
        slab = kv[:, cols]
        if i < width // LANES // 2:
            slab = rope(slab, cos_ref[...], sin_ref[...])
        kv_ref[:, cols] = slab.astype(BF)
    copy.wait()


def project_stage(me, x, gain, a_att, b_kv, cosine, sine, pieces, n):
    rows, width = x.shape
    outer, shard, columns = pieces[0].shape
    anywhere = pl.BlockSpec(memory_space=pl.ANY)
    outs = (
        jax.ShapeDtypeStruct((rows, width), BF),
        jax.ShapeDtypeStruct((rows, a_att.shape[0]), BF),
        jax.ShapeDtypeStruct((rows, b_kv.shape[1]), BF),
    )
    operands = (x, gain, a_att, b_kv, cosine, sine)
    normed, low, kv, weights = pl.pallas_call(
        project_kernel,
        grid=(1,),
        out_shape=(*outs, pltpu.HBM((n * shard, columns), BF)),
        in_specs=[pl.BlockSpec(memory_space=pltpu.SMEM)]
        + [full(v) for v in operands]
        + [anywhere] * len(pieces),
        out_specs=(*[full(v) for v in outs], anywhere),
        scratch_shapes=[
            pltpu.VMEM((n * shard, columns), BF),
            pltpu.SemaphoreType.DMA((n,)),
            pltpu.SemaphoreType.DMA(()),
        ],
        compiler_params=pltpu.CompilerParams(vmem_limit_bytes=28 << 20),
        cost_estimate=LIGHT,
        name="project",
    )(me.reshape(1), *map(HBM, operands), *map(HBM, pieces))
    return normed, low, kv, weights


def query_kernel(normed_ref, low_ref, b_ref, w_ref, cos_ref, sin_ref, out_ref):
    query = nn(normed_ref[...], w_ref[...]) + nn(low_ref[:, :RANK], b_ref[...])
    for i in range(out_ref.shape[1] // LANES):
        cols = slice(i * LANES, (i + 1) * LANES)
        slab = rope(query[:, cols], cos_ref[...], sin_ref[...]) * HEAD_DIM ** (-0.5)
        out_ref[:, cols] = slab.astype(BF)


def query_stage(normed, low, b_query, weights, cosine, sine):
    rows, width = normed.shape
    block = width // 4
    whole = lambda v: pl.BlockSpec(v.shape, lambda i: (0, 0))
    return pl.pallas_call(
        query_kernel,
        grid=(4,),
        out_shape=jax.ShapeDtypeStruct((rows, width), BF),
        in_specs=[
            whole(normed),
            whole(low),
            pl.BlockSpec((RANK, block), lambda i: (0, i)),
            pl.BlockSpec((width, block), lambda i: (0, i)),
            whole(cosine),
            whole(sine),
        ],
        out_specs=pl.BlockSpec((rows, block), lambda i: (0, i)),
        compiler_params=pltpu.CompilerParams(vmem_limit_bytes=24 << 20),
        cost_estimate=LIGHT,
        name="query",
    )(normed, low, b_query, HBM(weights), cosine, sine)


def output_kernel(me_ref, att_ref, a_ref, b_ref, x_ref, gain_ref, a_two_ref, e_ref, *refs):
    *pieces, middle_ref, normed_ref, low_ref, ext_ref, w_ref, held, sems, last = refs
    copies = place_copies(me_ref[0], pieces, held, sems)
    for copy in copies:
        copy.start()
    attended = att_ref[...]
    low = nt(attended, a_ref[...]).astype(BF)
    low_ref[...] = low
    for copy in copies:
        copy.wait()
    copy = pltpu.make_async_copy(held, w_ref, last)
    copy.start()
    rows, width = attended.shape
    middle = x_ref[...].astype(F32) + nn(attended, held[...]) + nn(low, b_ref[...])
    middle_ref[...] = middle
    normed = normed_of(middle, gain_ref[...])
    normed_ref[...] = normed
    lows = nt(normed, a_two_ref[...]).astype(BF)
    spare = jnp.zeros((rows, TABLE - 3 * RANK), BF)
    lows = jnp.concatenate([lows, e_ref[...], spare], 1)
    ext_ref[:, :width] = normed
    ext_ref[:, width:] = lows
    copy.wait()


def output_stage(me, attended, a_out, b_out, x, gain, a_two, grad_low, pieces, n):
    rows, width = attended.shape
    outer, shard, columns = pieces[0].shape
    anywhere = pl.BlockSpec(memory_space=pl.ANY)
    outs = (
        jax.ShapeDtypeStruct((rows, width), F32),
        jax.ShapeDtypeStruct((rows, width), BF),
        jax.ShapeDtypeStruct((rows, RANK), BF),
        jax.ShapeDtypeStruct((rows, width + TABLE), BF),
    )
    operands = (attended, a_out, b_out, x, gain, a_two, grad_low)
    *results, weights = pl.pallas_call(
        output_kernel,
        grid=(1,),
        out_shape=(*outs, pltpu.HBM((n * shard, columns), BF)),
        in_specs=[pl.BlockSpec(memory_space=pltpu.SMEM)]
        + [full(v) for v in operands]
        + [anywhere] * len(pieces),
        out_specs=(*[full(v) for v in outs], anywhere),
        scratch_shapes=[
            pltpu.VMEM((n * shard, columns), BF),
            pltpu.SemaphoreType.DMA((n,)),
            pltpu.SemaphoreType.DMA(()),
        ],
        compiler_params=pltpu.CompilerParams(vmem_limit_bytes=32 << 20),
        cost_estimate=LIGHT,
        name="output",
    )(me.reshape(1), *map(HBM, operands), *map(HBM, pieces))
    return (*results, weights)


def back_kernel(grad_ref, w_ref, low_ref, a_ref, out_ref):
    out = nt(grad_ref[...], w_ref[...]) + nn(low_ref[...], a_ref[...])
    out_ref[...] = out.astype(out_ref.dtype)


def back_stage(grad, weights, low, table, dtype):
    rows, inner = grad.shape
    width = weights.shape[0]
    block = width // 4
    whole = lambda v: pl.BlockSpec(v.shape, lambda i: (0, 0))
    return pl.pallas_call(
        back_kernel,
        grid=(4,),
        out_shape=jax.ShapeDtypeStruct((rows, width), dtype),
        in_specs=[
            whole(grad),
            pl.BlockSpec((block, inner), lambda i: (i, 0)),
            whole(low),
            pl.BlockSpec((table.shape[0], block), lambda i: (0, i)),
        ],
        out_specs=pl.BlockSpec((rows, block), lambda i: (0, i)),
        compiler_params=pltpu.CompilerParams(vmem_limit_bytes=24 << 20),
        cost_estimate=LIGHT,
        name="back",
    )(*map(HBM, (grad, weights, low, table)))


def norm_two_kernel(adapter_ref, *refs):
    mine, recv, near, last, refs = refs[0], refs[1], refs[2:4], refs[4:6], refs[6:]
    middle_ref, gain_ref, cot_ref, att_ref, low_ref, normed_ref, a_ref, b_ref, refs = *refs[:8], refs[8:]
    grad_ref, one_ref, low_out_ref, low_down_ref, gain_grad_ref, tables_ref = refs
    width = middle_ref.shape[1]
    half = middle_ref.shape[0] // 2
    came = [
        near[i][...].astype(F32) + last[i][...].astype(F32) for i in range(2)
    ]
    total = mine[...].astype(F32) + recv[...].astype(F32) + jnp.concatenate(came, 0)
    lift = lift_of(adapter_ref[0])
    lows = [
        nt(total[:, width + i * TABLE : width + (i + 1) * TABLE].astype(BF), lift[:RANK, :TABLE])
        for i in range(3)
    ]
    low_down = lows[2].astype(BF)
    low_down_ref[...] = low_down
    grad_low = jnp.concatenate(lows[:2], 1).astype(BF)
    grad = total[:, :width] + nn(grad_low, a_ref[...])
    middle = middle_ref[...]
    scale = lax.rsqrt(jnp.mean(middle * middle, -1, keepdims=True) + EPS)
    gain_grad_ref[...] = jnp.sum(grad * middle * scale, 0, keepdims=True)
    grad = grad * gain_ref[...]
    inner = jnp.mean(grad * middle, -1, keepdims=True)
    grad = cot_ref[...].astype(F32) + scale * grad - middle * (scale * scale * scale * inner)
    grad_ref[...] = grad
    one = grad.astype(BF)
    one_ref[...] = one
    low_out = nt(one, b_ref[...]).astype(BF)
    low_out_ref[...] = low_out
    tables_ref[:, :width] = tn(low_out, att_ref[...]).astype(BF)
    tables_ref[:, width : 2 * width] = tn(low_ref[...], one).astype(BF)
    both = tn(grad_low, normed_ref[...]).astype(BF)
    tables_ref[:, 2 * width : 3 * width] = both[:RANK]
    tables_ref[:, 3 * width : 4 * width] = both[RANK:]
    tables_ref[:, 4 * width :] = tn(low_down, cot_ref[...]).astype(BF)


def norm_two_stage(adapter, parts, middle, gain, cot, attended, low_out, normed, a_two, b_out):
    rows, width = middle.shape
    operands = (*parts, middle, gain, cot, attended, low_out, normed, a_two, b_out)
    outs = (
        jax.ShapeDtypeStruct((rows, width), F32),
        jax.ShapeDtypeStruct((rows, width), BF),
        jax.ShapeDtypeStruct((rows, RANK), BF),
        jax.ShapeDtypeStruct((rows, RANK), BF),
        jax.ShapeDtypeStruct((1, width), F32),
        jax.ShapeDtypeStruct((RANK, 5 * width), BF),
    )
    return pl.pallas_call(
        norm_two_kernel,
        grid=(1,),
        out_shape=outs,
        in_specs=[pl.BlockSpec(memory_space=pltpu.SMEM)] + [full(v) for v in operands],
        out_specs=tuple(full(v) for v in outs),
        compiler_params=pltpu.CompilerParams(vmem_limit_bytes=40 << 20),
        cost_estimate=LIGHT,
        name="norm_two",
    )(adapter, *map(HBM, operands))


def project_back_kernel(
    query_ref, kv_ref, came_ref, cos_ref, sin_ref, bq_ref, bkv_ref, low_ref, normed_ref, *outs
):
    grad_ref, grad_low_ref, tables_ref = outs
    width = query_ref.shape[1]
    kv_width = kv_ref.shape[1] // 2
    query = query_ref[...]
    grad_ref[:, :width] = query
    kv = kv_ref[...] + came_ref[...].astype(F32)
    for i in range(kv_ref.shape[1] // LANES):
        slab = kv[:, i * LANES : (i + 1) * LANES]
        if i < kv_width // LANES:
            slab = slab * cos_ref[...] - swap_halves(slab) * sin_ref[...]
        grad_ref[:, width + i * LANES : width + (i + 1) * LANES] = slab.astype(BF)
    kv = grad_ref[:, width:]
    grad_low = nt(kv, bkv_ref[...])
    first = lax.broadcasted_iota(jnp.int32, grad_low.shape, 1) < RANK
    table = jnp.concatenate([bq_ref[...], jnp.zeros((2 * RANK, width), BF)], 0)
    grad_low = jnp.where(first, nt(query, table), grad_low).astype(BF)
    grad_low_ref[...] = grad_low
    reduced = tn(grad_low, normed_ref[...]).astype(BF)
    for i in range(3):
        tables_ref[:, i * width : (i + 1) * width] = reduced[i * RANK : (i + 1) * RANK]
    low = low_ref[...]
    tables_ref[:, 3 * width : 4 * width] = tn(low, query)[:RANK].astype(BF)
    raised = tn(low, kv).astype(BF)
    tables_ref[:, 4 * width : 4 * width + kv_width] = raised[RANK : 2 * RANK, :kv_width]
    tables_ref[:, 4 * width + kv_width :] = raised[2 * RANK :, kv_width:]


def project_back_stage(grad_query, grad_kv, came, cosine, sine, b_query, b_kv, low, normed):
    rows, width = grad_query.shape
    kv = grad_kv.shape[1]
    operands = (grad_query, grad_kv, came, cosine, sine, b_query, b_kv, low, normed)
    outs = (
        jax.ShapeDtypeStruct((rows, width + kv), BF),
        jax.ShapeDtypeStruct(low.shape, BF),
        jax.ShapeDtypeStruct((RANK, 4 * width + kv), BF),
    )
    return pl.pallas_call(
        project_back_kernel,
        grid=(1,),
        out_shape=outs,
        in_specs=[full(v) for v in operands],
        out_specs=tuple(full(v) for v in outs),
        compiler_params=pltpu.CompilerParams(vmem_limit_bytes=32 << 20),
        cost_estimate=LIGHT,
        name="project_back",
    )(*map(HBM, operands))


def norm_one_kernel(grad_ref, w_ref, low_ref, a_ref, x_ref, gain_ref, mid_ref, out_ref, gain_grad_ref, held):
    step = pl.program_id(0)
    block = w_ref.shape[0]
    cols = pl.ds(pl.multiple_of(step * block, block), block)
    held[:, cols] = nt(grad_ref[...], w_ref[...]) + nn(low_ref[...], a_ref[...])

    @pl.when(step == pl.num_programs(0) - 1)
    def _():
        values = x_ref[...].astype(F32)
        scale = lax.rsqrt(jnp.mean(values * values, -1, keepdims=True) + EPS)
        gain_grad_ref[...] = jnp.sum(held[...] * values * scale, 0, keepdims=True)
        grad = held[...] * gain_ref[...]
        inner = jnp.mean(grad * values, -1, keepdims=True)
        out_ref[...] = mid_ref[...] + scale * grad - values * (scale * scale * scale * inner)


def norm_one_stage(grad, weights, low, table, x, gain, grad_middle):
    rows, inner = grad.shape
    width = weights.shape[0]
    block = width // 4
    whole = lambda v: pl.BlockSpec(v.shape, lambda i: (0, 0))
    return pl.pallas_call(
        norm_one_kernel,
        grid=(4,),
        out_shape=(
            jax.ShapeDtypeStruct((rows, width), F32),
            jax.ShapeDtypeStruct((1, width), F32),
        ),
        in_specs=[
            whole(grad),
            pl.BlockSpec((block, inner), lambda i: (i, 0)),
            whole(low),
            pl.BlockSpec((table.shape[0], block), lambda i: (0, i)),
            whole(x),
            whole(gain),
            whole(grad_middle),
        ],
        out_specs=(whole(grad_middle), whole(gain)),
        scratch_shapes=[pltpu.VMEM((rows, width), F32)],
        compiler_params=pltpu.CompilerParams(vmem_limit_bytes=32 << 20),
        cost_estimate=LIGHT,
        name="norm_one",
    )(*map(HBM, (grad, weights, low, table, x, gain, grad_middle)))


def head_pair(own_ref, other_ref, start, group):
    cols = pl.ds(pl.multiple_of(start + (group // 2) * LANES, LANES), LANES)
    slab = jnp.concatenate([own_ref[:, cols], other_ref[:, cols]], 0).astype(F32)
    lane = lax.broadcasted_iota(jnp.int32, slab.shape, 1)
    slab = jnp.where(group % 2 == 0, slab, pltpu.roll(slab, HEAD_DIM, 1))
    first = jnp.where(lane < HEAD_DIM, slab, 0.0)
    return first, pltpu.roll(first, HEAD_DIM, 1)


def attend_kernel(pos_ref, query_ref, own_ref, other_ref, out_ref, probs_ref):
    group = pl.program_id(0)
    rows = query_ref.shape[0]
    keys = [k.astype(BF) for k in head_pair(own_ref, other_ref, 0, group)]
    values = head_pair(own_ref, other_ref, KV_HEADS * HEAD_DIM, group)
    values = [v.T.astype(BF) for v in values]
    key_at = lax.broadcasted_iota(jnp.int32, (2 * rows, rows), 0)
    query_at = lax.broadcasted_iota(jnp.int32, (2 * rows, rows), 1)
    before = (pos_ref[1] < pos_ref[0]).astype(jnp.int32)
    visible = (key_at <= query_at) | ((key_at >= rows) & (before > 0))
    for j in range(query_ref.shape[1] // LANES):
        cols = pl.ds(j * LANES, LANES)
        query = query_ref[:, cols].astype(F32).T.astype(BF)
        mixed = 0.0
        for h in range(2):
            scores = jnp.where(visible, nn(keys[h], query), -1e30)
            weights = jnp.exp(scores - jnp.max(scores, 0, keepdims=True))
            probs = (weights * (1.0 / jnp.sum(weights, 0, keepdims=True))).astype(BF)
            probs_ref[0, 2 * j + h] = probs
            mixed += nn(values[h], probs)
        out_ref[:, cols] = mixed.T.astype(BF)


def attend_stage(blocks, query, own, other):
    rows, width = query.shape
    cols = width // KV_HEADS
    heads = HEADS // KV_HEADS
    tile = pl.BlockSpec((rows, cols), lambda i: (0, i))
    whole = pl.BlockSpec(own.shape, lambda i: (0, 0))
    return pl.pallas_call(
        attend_kernel,
        grid=(KV_HEADS,),
        out_shape=(
            jax.ShapeDtypeStruct((rows, width), BF),
            pltpu.HBM((KV_HEADS, heads, 2 * rows, rows), BF),
        ),
        in_specs=[pl.BlockSpec(memory_space=pltpu.SMEM), tile, whole, whole],
        out_specs=(tile, pl.BlockSpec((1, heads, 2 * rows, rows), lambda i: (i, 0, 0, 0))),
        compiler_params=pltpu.CompilerParams(vmem_limit_bytes=32 << 20),
        cost_estimate=LIGHT,
        name="attend",
    )(blocks, query, own, other)


def attend_back_kernel(
    grad_ref,
    out_ref,
    query_ref,
    own_ref,
    other_ref,
    probs_ref,
    cos_ref,
    sin_ref,
    gq_ref,
    gown_ref,
    gother_ref,
    gkv_ref,
):
    group = pl.program_id(0)
    keys = [k.T.astype(BF) for k in head_pair(own_ref, other_ref, 0, group)]
    values = head_pair(own_ref, other_ref, KV_HEADS * HEAD_DIM, group)
    values = [v.astype(BF) for v in values]
    cosine, sine = cos_ref[...], sin_ref[...]
    grad_keys, grad_values = [0.0, 0.0], [0.0, 0.0]
    for j in range(query_ref.shape[1] // LANES):
        cols = pl.ds(j * LANES, LANES)
        grad = grad_ref[:, cols]
        query = query_ref[:, cols]
        turned = grad.astype(F32).T
        product = turned * out_ref[:, cols].astype(F32).T
        turned = turned.astype(BF)
        grad_query = 0.0
        for h in range(2):
            inner = jnp.sum(product[h * HEAD_DIM : (h + 1) * HEAD_DIM], 0, keepdims=True)
            probs = probs_ref[0, 2 * j + h]
            grad_scores = (probs.astype(F32) * (nn(values[h], turned) - inner)).astype(BF)
            grad_values[h] += nn(probs, grad)
            grad_keys[h] += nn(grad_scores, query)
            grad_query += nn(keys[h], grad_scores)
        grad_query = grad_query.T * HEAD_DIM ** (-0.5)
        grad_query = grad_query * cosine - swap_halves(grad_query) * sine
        gq_ref[:, cols] = grad_query.astype(BF)

    @pl.when(group == 0)
    def _():
        gkv_ref[...] = jnp.zeros_like(gkv_ref)

    lane = lax.broadcasted_iota(jnp.int32, grad_keys[0].shape, 1)
    for start, (first, last) in ((0, grad_keys), (KV_HEADS * HEAD_DIM, grad_values)):
        total = jnp.where(lane < HEAD_DIM, first + pltpu.roll(last, HEAD_DIM, 1), 0.0)
        total = jnp.where(group % 2 == 0, total, pltpu.roll(total, HEAD_DIM, 1))
        cols = pl.ds(pl.multiple_of(start + (group // 2) * LANES, LANES), LANES)
        gkv_ref[:, cols] += total

    @pl.when(group == pl.num_programs(0) - 1)
    def _():
        rows = gown_ref.shape[0]
        gown_ref[...] = gkv_ref[pl.ds(0, rows), :]
        gother_ref[...] = gkv_ref[pl.ds(rows, rows), :].astype(BF)


def attend_back_stage(grad, out, query, own, other, probs, cosine, sine):
    rows, width = query.shape
    cols = width // KV_HEADS
    tile = pl.BlockSpec((rows, cols), lambda i: (0, i))
    whole = pl.BlockSpec(own.shape, lambda i: (0, 0))
    table = pl.BlockSpec((rows, LANES), lambda i: (0, 0))
    return pl.pallas_call(
        attend_back_kernel,
        grid=(KV_HEADS,),
        out_shape=(
            jax.ShapeDtypeStruct((rows, width), BF),
            jax.ShapeDtypeStruct(own.shape, F32),
            jax.ShapeDtypeStruct(own.shape, BF),
        ),
        scratch_shapes=[pltpu.VMEM((2 * rows, own.shape[1]), F32)],
        in_specs=[tile, tile, tile, whole, whole]
        + [pl.BlockSpec((1,) + probs.shape[1:], lambda i: (i, 0, 0, 0)), table, table],
        out_specs=(tile, whole, whole),
        compiler_params=pltpu.CompilerParams(vmem_limit_bytes=32 << 20),
        cost_estimate=LIGHT,
        name="attend_back",
    )(grad, out, query, own, other, probs, cosine, sine)


def send_columns(parts, n):
    whole = jnp.concatenate(parts, 1).astype(BF)
    whole = jnp.pad(whole, ((0, 0), (0, -whole.shape[1] % n)))
    return jnp.moveaxis(whole.reshape(RANK, n, -1), 1, 0)


def sum_columns(parts, ids, own_rows):
    n, _, chunk = parts.shape
    onehot = (ids[:, None] == jnp.arange(ADAPTERS, dtype=jnp.int32)[None, :]).astype(BF)
    summed = jnp.einsum("na,nrc->arc", onehot, parts, preferred_element_type=F32)
    return summed.reshape(n, own_rows, chunk)


def per_device(
    n,
    inputs,
    cotangent,
    adapter_ids,
    block_index,
    gain_first,
    gain_second,
    w_query,
    w_key,
    w_value,
    w_output,
    w_gate_up,
    w_down,
    reduce_attention,
    raise_query,
    raise_keyvalue,
    reduce_output,
    raise_output,
    reduce_gate_up,
    raise_gate_up,
    reduce_down,
    raise_down,
):
    width = inputs.shape[-1]
    rows = inputs.shape[-2]
    shard = w_down.shape[0]
    own_rows = raise_down.shape[0]
    gains = gain_first.shape[0]
    kv_width = KV_HEADS * HEAD_DIM
    side = lax.axis_index("seq")
    me = lax.axis_index(ALL).astype(jnp.int32)
    tokens = inputs.reshape(rows, width)
    grad_out = cotangent.reshape(rows, width)

    order = Order()
    qkv_width = width + 2 * kv_width
    att_rows = Outer(jnp.concatenate([w_query, w_key, w_value, w_output], 1), n)
    att_rows.step()
    cot_plane = Plane(grad_out, n)
    padded = -(-shard // 16) * 16
    slot = -(-(n // 8) * padded // 256) * 256 // (n // 8)
    feed = jnp.stack([w_gate_up[0].T, w_gate_up[1].T, w_down])

    table_width = 10 * width
    chunk = table_width // n
    table = jnp.concatenate(
        [reduce_attention[0], reduce_attention[1], reduce_attention[2], raise_query]
        + [reduce_output, raise_output, reduce_gate_up[0], reduce_gate_up[1], raise_down]
        + [raise_keyvalue[0], raise_keyvalue[1]],
        1,
    )
    table = jnp.pad(table, ((0, 0), (0, table_width - table.shape[1])))
    table = jnp.moveaxis(table.reshape(own_rows, n, chunk), 1, 0)
    hidden_table = jnp.stack([raise_gate_up[0], raise_gate_up[1], reduce_down])
    hidden_table = hidden_table.reshape(3, own_rows, n, shard).transpose(2, 1, 0, 3)
    hidden_table = hidden_table.reshape(n, own_rows, 3 * shard)
    small = jnp.concatenate([gain_first, gain_second, adapter_ids.astype(BF)])
    used = chunk + 3 * shard
    sent = -(-(used + small.shape[0]) // 128) * 128
    small = jnp.pad(small, (0, sent - used - small.shape[0]))
    small = jnp.broadcast_to(small, (n, own_rows, small.shape[0]))
    table = jnp.concatenate([table, hidden_table, small], -1)
    came = lax.all_to_all(table, ALL, 0, 0, tiled=True)
    cot_plane.near = att_rows.pass_through(order, *cot_plane.near)
    att_rows.step_all()
    gain_one = came[:, 0, used : used + gains].reshape(width).astype(F32)
    gain_two = came[:, 0, used + gains : used + 2 * gains].reshape(width).astype(F32)
    ids = came[:, 0, used + 2 * gains].astype(jnp.int32)
    columns = came[:, :, :chunk].reshape(ADAPTERS, RANK, chunk)
    hidden_cols = came[:, :, chunk:used].reshape(TABLE, 3, shard)
    own = lax.all_to_all(jnp.take(columns, ids, axis=0), ALL, 0, 0, tiled=True)
    feed = jnp.concatenate([feed, hidden_cols.transpose(1, 2, 0)], 2)
    feed = jnp.pad(feed, ((0, 0), (0, padded - shard), (0, 0))).reshape(3 * padded, -1)
    (feed,) = att_rows.pass_through(order, feed)
    feed = lax.all_gather(feed, "outer", axis=0, tiled=True)
    qkv_rows = Rows([part[:, :qkv_width] for part in att_rows.parts()], n)
    qkv_rows.start_plane()
    qkv_rows.near = order.point(*qkv_rows.near)
    qkv_rows.end_plane()
    own = jnp.moveaxis(own, 0, 1).reshape(RANK, table_width)
    (a_query, a_key, a_value, b_query, a_out, b_out, a_gate, a_up, b_down) = [
        own[:, i * width : (i + 1) * width] for i in range(9)
    ]
    b_key = own[:, 9 * width : 9 * width + kv_width]
    b_value = own[:, 9 * width + kv_width : 9 * width + 2 * kv_width]

    own_block = lax.dynamic_index_in_dim(block_index[0], side, 0, keepdims=False)
    other_block = lax.dynamic_index_in_dim(block_index[0], 1 - side, 0, keepdims=False)
    blocks = jnp.stack([own_block, other_block])
    cosine, sine = rotary_tables(own_block * rows + jnp.arange(rows, dtype=jnp.int32))
    a_att = jnp.concatenate([a_query, a_key, a_value], 0)
    a_two = jnp.concatenate([a_gate, a_up], 0)
    b_kv = jnp.concatenate(
        [
            jnp.zeros((RANK, 2 * kv_width), BF),
            jnp.pad(b_key, ((0, 0), (0, kv_width))),
            jnp.pad(b_value, ((0, 0), (kv_width, 0))),
        ],
        0,
    )
    grad_low_down = nt(grad_out, b_down).astype(BF)
    plane_ids = jnp.stack([ids[me], ids[me ^ C], ids[me ^ Y], ids[me ^ (Y | C)]])
    out_rows = Rows([part[:, qkv_width:] for part in att_rows.parts()], n)
    passed = order.point(
        *qkv_rows.last, a_att, a_two, b_kv, cosine, sine, grad_low_down, plane_ids, out_rows.whole
    )
    qkv_rows.last = passed[:2]
    a_att, a_two, b_kv, cosine, sine, grad_low_down, plane_ids, out_rows.whole = passed[2:]
    out_rows.start_plane()
    normed_one, low_att, key_value, w_qkv = project_stage(
        me, tokens, gain_one[None], a_att, b_kv, cosine, sine, qkv_rows.pieces(), n
    )
    low_query, low_key, low_value = [low_att[:, i * RANK : (i + 1) * RANK] for i in range(3)]
    key_value = order.point(key_value)
    other_kv = exchange(key_value, X, n)
    query = query_stage(normed_one, low_att, b_query, w_qkv, cosine, sine)
    key_value, other_kv, query = order.point(key_value, other_kv, query)
    attended, probs = attend_stage(blocks, query, key_value, other_kv)
    attended, *out_rows.near = order.point(attended, *out_rows.near)
    out_rows.end_plane()
    attended, *out_rows.last = order.point(attended, *out_rows.last)
    cot_plane.end()
    middle, normed_two, low_out, normed_ext, w_out = output_stage(
        me,
        attended,
        a_out,
        b_out,
        tokens,
        gain_two[None],
        a_two,
        grad_low_down,
        out_rows.pieces(),
        n,
    )

    normed_ext, *cot_plane.last = order.point(normed_ext, *cot_plane.last)
    cot_plane.finish()
    normed_plane = Plane(normed_ext, n)
    normed_plane.near = order.point(*normed_plane.near)
    normed_plane.end()
    passed = order.point(*normed_plane.far, *cot_plane.far, *cot_plane.last_far)
    normed_plane.far, cot_plane.far, cot_plane.last_far = passed[:2], passed[2:4], passed[4:]
    feed_of = lambda ids_here, place, groups: feed_stage(
        ids_here,
        place,
        len(groups),
        feed,
        normed_plane.group(*groups),
        cot_plane.group(*groups),
        padded,
        slot,
    )
    normed_sum = PlaneSum(n)
    hidden_mid, grads_mid, near_out, far_out = feed_of(plane_ids, 0, (1, 2))
    mid_recv = exchange(far_out, C, n)
    near_out, *normed_plane.last = order.point(near_out, *normed_plane.last)
    for j in range(2):
        part = slice(j * rows, (j + 1) * rows)
        normed_sum.put(j + 1, near_out[part], mid_recv[part])
    normed_plane.finish()
    hidden_far, grads_far, near_out, far_out = feed_of(plane_ids, 2, (3,))
    normed_sum.put(3, near_out, exchange(far_out, C, n))
    ids_own, *sends = order.point(plane_ids, *normed_sum.far_sends(), *normed_sum.near_sends())
    far_came, near_came = normed_sum.hop(*sends[:2]), normed_sum.hop(*sends[2:])
    hidden_own, grads_own, near_out, far_out = feed_of(ids_own, 0, (0,))
    recv = exchange(far_out, C, n)
    near_out, grads_own, *far_came = order.point(near_out, grads_own, *far_came)
    hidden_grads = grads_own + grads_mid + grads_far
    hidden_grads = jnp.concatenate([hidden_grads[i] for i in range(3)], 1).astype(BF)
    hidden_grads = hidden_grads.reshape(n, own_rows, -1)
    passed = order.point(*normed_sum.last_sends(*far_came), *near_came)
    last_sends, near_came = passed[:2], passed[2:]
    last_came = normed_sum.last_hop(*last_sends)
    hidden_own, hidden_grads = order.point(hidden_own, hidden_grads)
    hidden_grads = lax.all_to_all(hidden_grads, ALL, 0, 0, tiled=True)
    down_near, down_far = down_stage(
        [hidden_own, hidden_mid, hidden_far], feed, n // 8, padded, slot, rows
    )
    parts = order.point(recv, *near_came, *last_came, down_far)
    down_far = parts[5]
    parts = (near_out, *parts[:5])

    grad_middle, grad_one, grad_low_out, low_down, gain_grad_two, early = norm_two_stage(
        adapter_ids, parts, middle, gain_two[None], grad_out, attended, low_out, normed_two, a_two, b_out
    )
    down_recv = exchange(down_far, C, n)
    grad_attended = back_stage(grad_one, w_out, grad_low_out, a_out, BF)
    down_sum = PlaneSum(n)
    for i in range(4):
        part = slice(i * rows, (i + 1) * rows)
        down_sum.put(i, down_near[part], down_recv[part])
    grad_query, grad_kv, kv_away = attend_back_stage(
        grad_attended, attended, query, key_value, other_kv, probs, cosine, sine
    )
    grad_query, grad_kv, kv_away, hidden_grads = order.point(
        grad_query, grad_kv, kv_away, hidden_grads
    )
    kv_came, *sends = order.point(
        exchange(kv_away, X, n), *down_sum.far_sends(), *down_sum.near_sends()
    )
    down_far = down_sum.hop(*sends[:2])
    grad_qkv, grad_low_att, late = project_back_stage(
        grad_query, grad_kv, kv_came, cosine, sine, b_query, b_kv, low_att, normed_one
    )

    late, grad_qkv = order.point(send_columns([late, early], n), grad_qkv)
    late = lax.all_to_all(late, ALL, 0, 0, tiled=True)
    down_near = down_sum.hop(*sends[2:])
    input_grad, gain_grad_one = norm_one_stage(
        grad_qkv, w_qkv, grad_low_att, a_att, tokens, gain_one[None], grad_middle
    )
    input_grad = input_grad.reshape(inputs.shape)
    gain_grads = jnp.concatenate(
        [gain_grad_one.reshape(n, gains), gain_grad_two.reshape(n, gains)], 1
    )
    gain_grads = jnp.broadcast_to(gain_grads[:, None], (n, own_rows, 2 * gains))
    input_grad, gain_grads, *down_far = order.point(input_grad, gain_grads, *down_far)
    down_last = down_sum.last_hop(*down_sum.last_sends(*down_far))
    late = jnp.concatenate([sum_columns(late, ids, own_rows), gain_grads], -1)
    late, hidden_grads, down_sum.mine[0] = order.point(late, hidden_grads, down_sum.mine[0])
    late = lax.all_to_all(late, ALL, 0, 0, tiled=True)
    branch_two = down_sum.total(down_near, down_last)
    output = (middle + branch_two + nn(low_down, b_down)).astype(BF)
    hidden_grads = hidden_grads.reshape(n // 8, 8, own_rows, 3, n // 8, slot)
    hidden_grads = jnp.sum(hidden_grads[..., :shard].astype(F32), 0)
    hidden_grads = hidden_grads.transpose(2, 1, 3, 0, 4).reshape(3, own_rows, -1)
    gain_grads = jnp.sum(late[:, 0, -2 * gains :], 0) + order.token
    late_rows = jnp.moveaxis(late[:, :, : -2 * gains], 0, 1).reshape(own_rows, -1)
    parts = [late_rows[:, i * width : (i + 1) * width] for i in range(4)]
    kv = late_rows[:, 4 * width : 4 * width + 2 * kv_width]
    start = 4 * width + 2 * kv_width
    parts += [late_rows[:, start + i * width : start + (i + 1) * width] for i in range(5)]
    return (
        output.reshape(inputs.shape),
        input_grad,
        gain_grads[:gains],
        gain_grads[gains:],
        jnp.stack(parts[:3]),
        parts[3],
        jnp.stack([kv[:, :kv_width], kv[:, kv_width:]]),
        parts[4],
        parts[5],
        jnp.stack(parts[6:8]),
        hidden_grads[:2],
        hidden_grads[2],
        parts[8],
    )


def solution(mesh):
    dp, seq = mesh.shape["dp"], mesh.shape["seq"]
    n = dp * seq
    dp_axes = ALL[:2]
    rows = P(ALL, None)
    stacked = P(None, ALL, None)
    vector = P(ALL)
    blocks = P(dp_axes, "seq", None, None)
    return jax.shard_map(
        functools.partial(per_device, n),
        mesh=Mesh(mesh.devices.reshape(dp // 4, 4, seq), ALL),
        in_specs=(
            (blocks, blocks, P(dp_axes), P(dp_axes, None), vector, vector)
            + (rows, rows, rows, rows, P(None, None, ALL), rows)
            + (stacked, rows, stacked, rows, rows, stacked, stacked, rows, rows)
        ),
        out_specs=(
            (blocks, blocks, vector, vector, stacked, rows, stacked, rows, rows)
            + (stacked, stacked, rows, rows)
        ),
        check_vma=False,
    )
```
